32 devices in a mesh: stream: 8 (over z, y), span: 4 (over x, core).
Axes of the slice: x: 2, y: 2, z: 4, core: 2. Of those that a mesh axis runs over, the one named last changes fastest.
Arguments:
- right_sides: bfloat16 [8, 4, 4, 512, 128], P('stream', 'span'), may hold values from -2.5 to 2.5
- inverse: bfloat16 [8, 4, 4, 512, 512], P('stream', 'span'), as said below
- coupling: bfloat16 [8, 4, 4, 3, 64, 512], P('stream', 'span')
- sweep_order: int32 [8, 4, 4], P('stream', 'span'), may hold values from 0 to 3, each once within a row
Outputs:
- solution: bfloat16 [8, 4, 4, 512, 128], P('stream', 'span')
The draws below stay inside these ranges and needn't reach their ends.
Inputs may be any that keep to these rules, and one draw needn't show every extreme that they name: `sweep_order`: each group's 4 slots appear once each. Every diagonal block's inverse is well conditioned and of order one.
All inputs are finite; a program needn't handle non-finite values.
Results may differ from the reference program's by a relative error of at most 0.024.
Values may be sent and summed in bfloat16 or wider, within the bound.
No kernel may reach another device: no remote copies, remote signals or barrier semaphores. Data moves between devices by JAX's collectives and lax.ppermute only.
A program may use at most 64 MiB of HBM per device.

```python
import jax
import jax.numpy as jnp
from jax import lax

NP = 8
NODES = 512
FACE = 64
EL = 4
RHS = 128
SWEEPS = 6
SGROUPS = 8
PGROUPS = 4


def draw_inverse(key, part):
    shape = (SGROUPS, PGROUPS, EL, NODES, NODES)
    key_diag, key_off = jax.random.split(jax.random.fold_in(key, 11))
    off_part = jax.random.normal(key_off, shape, jnp.float32) * (0.5 / NODES ** 0.5)
    diag_part = jax.random.uniform(key_diag, shape[:-1], jnp.float32, 0.6, 1.4)
    row_ids = jnp.arange(NODES, dtype=jnp.int32)[:, None]
    col_ids = jnp.arange(NODES, dtype=jnp.int32)[None, :]
    carried = jnp.logical_and(col_ids < FACE, row_ids == col_ids + (NP - 1) * FACE).astype(jnp.float32)
    return (off_part + diag_part[..., None] * jnp.eye(NODES, dtype=jnp.float32) + carried).astype(jnp.bfloat16)


def draw_coupling(key, part):
    shape = (SGROUPS, PGROUPS, EL, 3, FACE, NODES)
    scales = jnp.array([0.096 / FACE ** 0.5, 0.15 / FACE ** 0.5, 0.15 / FACE ** 0.5], jnp.float32)[:, None, None]
    base_key = jax.random.fold_in(key, 23)
    key_noise, key_main = jax.random.split(base_key)
    values = jax.random.normal(key_noise, shape, jnp.float32)
    centre = (0.961 / (1.0 + 0.25 / NP)) ** 0.5
    main_part = jax.random.uniform(key_main, (SGROUPS, PGROUPS, EL, FACE), jnp.float32, centre - 0.03, centre + 0.03)
    face_ids = jnp.arange(FACE, dtype=jnp.int32)[:, None]
    node_ids = jnp.arange(NODES, dtype=jnp.int32)[None, :]
    matching = (face_ids == node_ids).astype(jnp.float32)
    first_only = (jnp.arange(3, dtype=jnp.int32) == 0).astype(jnp.float32)[:, None, None]
    placed = main_part[:, :, :, None, :, None] * (first_only * matching)[None, None, None]
    return (values * scales + placed).astype(jnp.bfloat16)


def block_scale(own_key, dims, cuts, smallest, high):
    def one(dim, blocks):
        steps = jax.random.uniform(jax.random.fold_in(jax.random.fold_in(own_key, 6), dim), (blocks,), jnp.float32, smallest / len(cuts), high / len(cuts))
        return jnp.repeat(jnp.exp(steps), dims[dim] // blocks).reshape((-1,) + (1,) * (len(dims) - dim - 1))

    gain = one(*cuts[0])
    for cut in cuts[1:]:
        gain = gain * one(*cut)
    return gain


def scatter_about(own_key, dims, spread, bound, cuts=(), held_as=jnp.bfloat16):
    factor_of = block_scale(own_key, dims, cuts, -0.22, 0.18) if cuts else 1.0
    values = jax.random.normal(own_key, dims, jnp.float32) * spread * factor_of
    return jnp.minimum(jnp.maximum(values, -bound), bound).astype(held_as)


def setup_inputs(seed: int = 0) -> dict:
    keys = jax.random.split(jax.random.key(seed), 5)
    right_sides = scatter_about(keys[0], (SGROUPS, PGROUPS, EL, NODES, RHS), 0.4, 2.5, ((0, 8), (1, 4)))
    inverse = draw_inverse(jax.random.fold_in(keys[4], 71), 0)
    coupling = draw_coupling(jax.random.fold_in(keys[4], 71), 0)
    sweep_order = jax.vmap(lambda own: jax.random.permutation(own, EL))(jax.random.split(keys[3], SGROUPS * PGROUPS)).reshape((SGROUPS, PGROUPS, EL)).astype(jnp.int32)
    return {"right_sides": right_sides, "inverse": inverse, "coupling": coupling, "sweep_order": sweep_order}


def face_rows(values, layer):
    leading = values.shape[:-2]
    columns = values.shape[-1]
    shaped = values.reshape(leading + (NP, NP, NP, columns))
    return shaped[..., :, layer, :, :].reshape(leading + (NP * NP, columns))


def select_slots(values, chosen):
    return jax.vmap(lambda blocks, picks: blocks[picks])(values, chosen)


def reference(right_sides, inverse, coupling, sweep_order):
    highest = lax.Precision.HIGHEST

    def lifting_group(items):
        inverse_group, coupling_group, order_group = items
        inverse_pos = select_slots(inverse_group, order_group).astype(jnp.float32)
        inflow_pos = select_slots(coupling_group, order_group)[:, :, 0].astype(jnp.float32)
        return jnp.einsum("penm,pefm->penf", inverse_pos, inflow_pos, precision=highest)

    liftings = lax.map(lifting_group, (inverse, coupling, sweep_order))
    solution = jnp.zeros(right_sides.shape, jnp.bfloat16)
    for sweep_index in range(SWEEPS):
        upper_layer = face_rows(solution, NP - 1)
        lower_layer = face_rows(solution, 0)
        blank = jnp.zeros_like(upper_layer[:, :1])
        from_below = jnp.concatenate([blank, upper_layer[:, :-1]], axis=1)
        from_above = jnp.concatenate([lower_layer[:, 1:], blank], axis=1)

        def group_step(inflow, items):
            inverse_group, coupling_group, rhs_group, order_group, below, above, lifting = items
            inverse_pos = select_slots(inverse_group, order_group).astype(jnp.float32)
            coupling_pos = select_slots(coupling_group, order_group).astype(jnp.float32)
            rhs_pos = select_slots(rhs_group, order_group).astype(jnp.float32)
            source = rhs_pos + jnp.einsum("pefn,pefr->penr", coupling_pos[:, :, 1], below.astype(jnp.float32), precision=highest)
            source = source + jnp.einsum("pefn,pefr->penr", coupling_pos[:, :, 2], above.astype(jnp.float32), precision=highest)
            source = source.astype(jnp.bfloat16)
            gained = jnp.einsum("penm,pemr->penr", inverse_pos, source.astype(jnp.float32), precision=highest)
            pieces = []
            for position in range(EL):
                added = jnp.einsum("pnf,pfr->pnr", lifting[:, position], inflow, precision=highest)
                pieces.append((gained[:, position] + added).astype(jnp.bfloat16))
                inflow = jnp.einsum("pgf,pfr->pgr", lifting[:, position, NODES - FACE:], inflow, precision=highest) + gained[:, position, NODES - FACE:]
            return inflow, jnp.stack(pieces, axis=1)

        start = jnp.zeros((PGROUPS, FACE, RHS), jnp.float32)
        final_trace, solution = lax.scan(group_step, start, (inverse, coupling, right_sides, sweep_order, from_below, from_above, liftings))
    placed = jax.vmap(jax.vmap(lambda blocks, picks: jnp.zeros_like(blocks).at[picks].set(blocks)))(solution, sweep_order)
    return placed
```

```python
import functools

import jax
import jax.numpy as jnp
from jax import lax
from jax.experimental import pallas as pl
from jax.experimental.pallas import tpu as pltpu
from jax.sharding import PartitionSpec as P

NP = 8
SWEEPS = 6
VMEM = pl.BlockSpec(memory_space=pltpu.VMEM)
SMEM = pl.BlockSpec(memory_space=pltpu.SMEM)
F32 = jnp.float32
BF16 = jnp.bfloat16


def bits_of(count):
    return [1 << i for i in range(count.bit_length() - 1)]


def reversed_bits(value, count):
    bits = bits_of(count)
    total = 0
    for low, high in zip(bits, bits[::-1]):
        total = total + jnp.where((value & low) != 0, high, 0)
    return total


def reversed_static(value, count):
    bits = bits_of(count)
    return sum(high for low, high in zip(bits, bits[::-1]) if value & low)


def swap(value, axis, mask):
    count = lax.axis_size(axis)
    return lax.ppermute(value, axis, [(i, i ^ mask) for i in range(count)])


def dot(left, right):
    return jnp.dot(left, right, preferred_element_type=F32)


def dot_nt(left, right):
    return lax.dot_general(left, right, (((1,), (1,)), ((), ())), preferred_element_type=F32)


def lane_is_low(shape, face):
    return lax.broadcasted_iota(jnp.int32, shape, len(shape) - 1) < face


def facemap_kernel(place, order, inverse, coupling, given, maps, gains, *, groups):
    count, nodes, width = given.shape
    face = coupling.shape[1] // 3
    part = nodes // NP
    layer = part // NP
    share = width // groups
    outs = []
    for p in range(count):
        slot = order[p]
        lower = []
        upper = []
        for a in range(NP):
            head = inverse[slot, a * part : a * part + 2 * layer, :].astype(F32)
            tail = inverse[slot, (a + 1) * part - 2 * layer : (a + 1) * part, :].astype(F32)
            lower.append(head[:layer])
            upper.append(tail[layer:])
        faces = jnp.concatenate(lower + upper, axis=0).astype(BF16)
        outflow = inverse[slot, nodes - face :, :]
        blank = jnp.zeros_like(outflow)
        pair = [outflow, blank] if p % 2 == 0 else [blank, outflow]
        rows = jnp.concatenate([faces] + pair, axis=0)
        full = dot_nt(coupling[slot], rows)
        full = jnp.concatenate([full[2 * face :], full[face : 2 * face], full[:face]], axis=0)
        maps[p * 3 * face : (p + 1) * 3 * face, :] = full[:, : 2 * face].astype(BF16)
        outs.append(full[:, 2 * face :])
        if p % 2 == 1:
            at = (count + p // 2) * 3 * face
            maps[at : at + 3 * face, :] = (outs[p - 1] + outs[p]).astype(BF16)
        gain = dot(rows, given[slot]).T.astype(BF16)
        for j in range(groups):
            gains[place[0] ^ j, p] = gain[j * share : (j + 1) * share]


def unpack_maps(map_refs, weights, count, face):
    shape = (3 * face, 2 * face)
    low = lane_is_low(shape, face)
    blank = jnp.zeros((face, 4 * face), BF16)
    for pos, ref in enumerate(map_refs):
        for p in range(count):
            sides = ref[p * 3 * face : (p + 1) * 3 * face, :]
            at = (count + p // 2) * 3 * face
            outs = ref[at : at + 3 * face, :]
            outs = jnp.where(low if p % 2 == 0 else jnp.logical_not(low), outs, jnp.zeros_like(outs))
            full = jnp.concatenate([sides, outs], axis=1)
            weights[pos, p, : 2 * face, :] = full[: 2 * face]
            inflow_at = (2 + (p + 1) % 2) * face
            other_at = (2 + p % 2) * face
            weights[pos, p, inflow_at : inflow_at + face, :] = full[2 * face :]
            weights[pos, p, other_at : other_at + face, :] = blank


def sweep_step(me, pos, now, before, groups, count, face, share, weights, gains, states, inflow, keep=None):
    own = me ^ reversed_bits(pos, groups)
    below = jnp.where(own > 0, reversed_bits((own - 1) & (groups - 1) ^ me, groups), groups)
    above = jnp.where(own < groups - 1, reversed_bits((own + 1) & (groups - 1) ^ me, groups), groups)
    rel = reversed_bits(pos, groups)
    entry = inflow
    out = None
    for p in range(count):
        upper = states[before, above, p]
        lower = states[before, below, p]
        lag = jnp.where(lane_is_low(upper.shape, face), upper, lower)
        if keep is not None:
            keep(p, lag, entry)
        result = dot(jnp.concatenate([lag, entry], axis=1), weights[pos, p])
        head = result[:share] + gains[rel, p].astype(F32)
        result = head if result.shape[0] == share else jnp.concatenate([head, result[share:]], axis=0)
        states[now, pos, p] = result[:, : 2 * face].astype(BF16)
        out = result[:, 2 * face :]
        entry = out.astype(BF16)
    return out


def respond_kernel(place, *refs, groups, count, face):
    map_refs = refs[:groups]
    gains, response, offset, weights, states, unit = refs[groups:]
    me = place[0]
    share = gains.shape[2]
    rows = states.shape[3]
    half = groups // 2
    unpack_maps(map_refs, weights, count, face)
    states[...] = jnp.zeros_like(states)
    unit[...] = jnp.zeros_like(unit)
    row = lax.broadcasted_iota(jnp.int32, (rows, 2 * face), 0) - share
    lane = lax.broadcasted_iota(jnp.int32, (rows, 2 * face), 1) - face
    for pos in range(half):
        hit = jnp.logical_and(lane >= 0, row == lane + pos * face)
        unit[0, pos] = jnp.where(hit, 1.0, 0.0).astype(BF16)

    def sweep(k, carry):
        now = k % 2
        before = 1 - now

        def tiles(t):
            ends = []
            for pos in (2 * t, 2 * t + 1, 2 * t + half, 2 * t + half + 1):
                inflow = unit[jnp.minimum(k, 1), pos]
                ends.append(
                    sweep_step(me, pos, now, before, groups, count, face, share, weights, gains, states, inflow)
                )
            even = pltpu.roll(ends[0], face, 1) + ends[1]
            odd = pltpu.roll(ends[2], face, 1) + ends[3]
            return even, odd

        def put(t, even, odd):
            at = t * 2 * face
            offset[k, :, pl.ds(at, 2 * face)] = even[:share].astype(BF16)
            offset[k, :, pl.ds(half * face + at, 2 * face)] = odd[:share].astype(BF16)
            response[k, :, pl.ds(at, 2 * face)] = (even[share:] + odd[share:]).astype(BF16)

        if groups == 4:
            put(0, *tiles(0))
        else:

            def block(t, inner):
                even, odd = tiles(t)
                put(pl.multiple_of(t, 1), even, odd)
                return inner

            lax.fori_loop(0, groups // 4, block, 0)
        return carry

    lax.fori_loop(0, SWEEPS, sweep, 0)


def pick(flag, first, second):
    return jnp.where(flag != 0, first, second)


def compose_kernel(flag, own_even, own_odd, got_even, got_odd, own_offset, got_offset, response, offset):
    down = flag[0]
    width = own_even.shape[1]
    upper = []
    for k in range(SWEEPS):
        upper.append(
            (pick(down, own_even[k], got_even[k]), pick(down, own_odd[k], got_odd[k]))
        )
    first = [pick(down, got_even[k], own_even[k]) for k in range(SWEEPS)]
    for m in range(SWEEPS):
        total = None
        for j in range(m + 1):
            term = dot(first[j], upper[m - j][j % 2])
            total = term if total is None else total + term
        response[m] = total.astype(BF16)
    inner = [pick(down, got_offset[k], own_offset[k]) for k in range(SWEEPS)]
    for k in range(SWEEPS):
        total = pick(down, own_offset[k], got_offset[k]).astype(F32)
        total = total + through(inner, upper, k, width)
        offset[k] = total.astype(BF16)


def through(inner, maps, k, width):
    parts = [None, None]
    for m in range(k + 1):
        value = inner[k - m]
        for group in (0, 1):
            term = dot(value[:, group * width : (group + 1) * width], maps[m][group])
            target = (group + m) % 2
            parts[target] = term if parts[target] is None else parts[target] + term
    return jnp.concatenate(parts, axis=1)


def resolve_kernel(place, flags, *refs, groups, count, face, levels):
    map_refs = refs[:groups]
    gains = refs[groups]
    top = refs[groups + 1]
    lower = refs[groups + 2 : groups + 2 + 3 * levels]
    wanted, weights, states, inflows = refs[groups + 2 + 3 * levels :]
    me = place[0]
    share = gains.shape[2]
    half = groups // 2
    width = half * face
    unpack_maps(map_refs, weights, count, face)
    states[...] = jnp.zeros_like(states)
    values = [pick(flags[levels], top[k], jnp.zeros_like(top[k])) for k in range(SWEEPS)]
    for level in range(levels - 1, -1, -1):
        even, odd, offset = lower[3 * level : 3 * level + 3]
        maps = [(even[k], odd[k]) for k in range(SWEEPS)]
        moved = [
            (offset[k].astype(F32) + through(values, maps, k, width)).astype(BF16) for k in range(SWEEPS)
        ]
        values = [pick(flags[level], moved[k], values[k]) for k in range(SWEEPS)]
    for k in range(SWEEPS):
        for tile in range(half):
            both = values[k][:, tile * 2 * face : (tile + 1) * 2 * face]
            inflows[k, 2 * tile] = pltpu.roll(both.astype(F32), face, 1).astype(BF16)
            inflows[k, 2 * tile + 1] = both

    def sweep(k, carry):
        now = k % 2
        before = 1 - now

        def group(pos):
            rel = reversed_bits(pos, groups)
            kept = []

            def keep(p, lag, entry):
                wanted[rel, p] = lag
                kept.append(entry)
                if p % 2 == 1:
                    low = lane_is_low(entry.shape, face)
                    wanted[rel, count + p // 2] = jnp.where(low, kept[p], kept[p - 1])

            sweep_step(
                me, pos, now, before, groups, count, face, share, weights, gains, states, inflows[k, pos], keep
            )

        if groups == 4:
            for pos in range(groups):
                group(pos)
        else:

            def block(pos, inner):
                group(pos)
                return inner

            lax.fori_loop(0, groups, block, 0)
        return carry

    lax.fori_loop(0, SWEEPS, sweep, 0)


def final_kernel(place, order, inverse, coupling, given, wanted, placed, gathered, *, groups):
    count, nodes, width = given.shape
    face = coupling.shape[1] // 3
    share = width // groups
    for rel in range(groups):
        at = pl.multiple_of((place[0] ^ rel) * share, share)
        for m in range(wanted.shape[1]):
            gathered[m, pl.ds(at, share), :] = wanted[rel, m].astype(F32)
    for p in range(count):
        slot = order[p]
        rows = coupling[slot]
        blank = jnp.zeros((face, nodes), BF16)
        inflow_rows = rows[:face]
        pair = [blank, inflow_rows] if p % 2 == 0 else [inflow_rows, blank]
        sides = jnp.concatenate([rows[2 * face :], rows[face : 2 * face]] + pair, axis=0)
        traces = jnp.concatenate([gathered[p], gathered[count + p // 2]], axis=1).astype(BF16)
        source = given[slot].astype(F32) + dot(traces, sides).T
        placed[slot] = dot(inverse[slot], source.astype(BF16)).astype(BF16)


def gather_list(value, axis):
    values = [value]
    for mask in bits_of(lax.axis_size(axis))[::-1]:
        values = values + [swap(v, axis, mask) for v in values]
    return values


def exchange(value, axis):
    groups = value.shape[0]
    bits = bits_of(groups)
    rest = value.shape[1:]
    value = value.reshape((2,) * len(bits) + rest)
    for dim, mask in enumerate(bits[::-1]):
        kept = lax.index_in_dim(value, 0, dim, keepdims=True)
        sent = lax.index_in_dim(value, 1, dim, keepdims=True)
        value = jnp.concatenate([kept, swap(sent, axis, mask)], axis=dim)
    return value.reshape((groups,) + rest)


def shards(right_sides, inverse, coupling, sweep_order):
    given = right_sides[0, 0]
    inverse = inverse[0, 0]
    order = sweep_order[0, 0]
    count, nodes, width = given.shape
    face = coupling.shape[4]
    coupling = coupling[0, 0].reshape(count, 3 * face, nodes)
    groups = lax.axis_size("span")
    share = width // groups
    half = groups // 2
    me = lax.axis_index("span")
    place = me.astype(jnp.int32).reshape(1)
    line = lax.axis_index("stream").astype(jnp.int32)
    masks = bits_of(lax.axis_size("stream"))
    flags = jnp.stack([(line // mask) % 2 for mask in masks])
    map_rows = (count + count // 2) * 3 * face
    maps, gains = pl.pallas_call(
        functools.partial(facemap_kernel, groups=groups),
        out_shape=(
            jax.ShapeDtypeStruct((map_rows, 2 * face), BF16),
            jax.ShapeDtypeStruct((groups, count, share, 4 * face), BF16),
        ),
        in_specs=[SMEM, SMEM, VMEM, VMEM, VMEM],
        out_specs=(VMEM, VMEM),
        name="facemaps",
    )(place, order, inverse, coupling, given)
    all_maps = gather_list(maps, "span")
    gains = exchange(gains, "span")
    rows = share + half * face
    response, offset = pl.pallas_call(
        functools.partial(respond_kernel, groups=groups, count=count, face=face),
        out_shape=(
            jax.ShapeDtypeStruct((SWEEPS, half * face, half * face), BF16),
            jax.ShapeDtypeStruct((SWEEPS, share, groups * face), BF16),
        ),
        in_specs=[SMEM] + [VMEM] * (groups + 1),
        out_specs=(VMEM, VMEM),
        scratch_shapes=[
            pltpu.VMEM((groups, count, 4 * face, 4 * face), BF16),
            pltpu.VMEM((2, groups + 1, count, rows, 2 * face), BF16),
            pltpu.VMEM((2, groups, rows, 2 * face), BF16),
        ],
        name="respond",
    )(place, *all_maps, gains)
    levels = []
    for level, mask in enumerate(masks[:-1]):
        other = swap(response, "span", 1)
        got = swap(response, "stream", mask)
        got_offset = swap(offset, "stream", mask)
        got_other = swap(got, "span", 1)
        levels += [got, got_other, got_offset]
        response, offset = pl.pallas_call(
            compose_kernel,
            out_shape=(
                jax.ShapeDtypeStruct(response.shape, BF16),
                jax.ShapeDtypeStruct(offset.shape, BF16),
            ),
            in_specs=[SMEM] + [VMEM] * 6,
            out_specs=(VMEM, VMEM),
            name="compose",
        )(flags[level : level + 1], response, other, got, got_other, offset, got_offset)
    top = swap(offset, "stream", masks[-1])
    wanted = pl.pallas_call(
        functools.partial(
            resolve_kernel, groups=groups, count=count, face=face, levels=len(masks) - 1
        ),
        out_shape=jax.ShapeDtypeStruct((groups, count + count // 2, share, 2 * face), BF16),
        in_specs=[SMEM, SMEM] + [VMEM] * (groups + 2 + len(levels)),
        out_specs=VMEM,
        scratch_shapes=[
            pltpu.VMEM((groups, count, 4 * face, 4 * face), BF16),
            pltpu.VMEM((2, groups + 1, count, share, 2 * face), BF16),
            pltpu.VMEM((SWEEPS, groups, share, 2 * face), BF16),
        ],
        name="resolve",
    )(place, flags, *all_maps, gains, top, *levels)
    wanted = exchange(wanted, "span")
    placed = pl.pallas_call(
        functools.partial(final_kernel, groups=groups),
        out_shape=jax.ShapeDtypeStruct((count, nodes, width), BF16),
        in_specs=[SMEM, SMEM] + [VMEM] * 4,
        out_specs=VMEM,
        scratch_shapes=[pltpu.VMEM((count + count // 2, width, 2 * face), F32)],
        name="finish",
    )(place, order, inverse, coupling, given, wanted)
    return placed[None, None]


def solution(mesh):
    in_specs = (
        P("stream", "span", None, None, None),
        P("stream", "span", None, None, None),
        P("stream", "span", None, None, None, None),
        P("stream", "span", None),
    )
    out_specs = P("stream", "span", None, None, None)
    return jax.shard_map(shards, mesh=mesh, in_specs=in_specs, out_specs=out_specs, check_vma=False)
```

```python
import functools

import jax
import jax.numpy as jnp
from jax import lax
from jax.experimental import pallas as pl
from jax.experimental.pallas import tpu as pltpu
from jax.sharding import PartitionSpec as P

NP = 8
SWEEPS = 6
VMEM = pl.BlockSpec(memory_space=pltpu.VMEM)
SMEM = pl.BlockSpec(memory_space=pltpu.SMEM)
F32 = jnp.float32
BF16 = jnp.bfloat16


def bits_of(count):
    return [1 << i for i in range(count.bit_length() - 1)]


def reversed_bits(value, count):
    bits = bits_of(count)
    total = 0
    for low, high in zip(bits, bits[::-1]):
        total = total + jnp.where((value & low) != 0, high, 0)
    return total


def reversed_static(value, count):
    bits = bits_of(count)
    return sum(high for low, high in zip(bits, bits[::-1]) if value & low)


def swap(value, axis, mask):
    count = lax.axis_size(axis)
    return lax.ppermute(value, axis, [(i, i ^ mask) for i in range(count)])


def dot(left, right):
    return jnp.dot(left, right, preferred_element_type=F32)


def dot_nt(left, right):
    return lax.dot_general(left, right, (((1,), (1,)), ((), ())), preferred_element_type=F32)


def by_half(low, high):
    lane = lax.broadcasted_iota(jnp.int32, low.shape, low.ndim - 1)
    return jnp.where(lane < low.shape[-1] // 2, low, high)


def turned(value):
    return pltpu.roll(value.astype(F32), value.shape[-1] // 2, 1).astype(value.dtype)


def facemap_kernel(place, order, inverse, coupling, given, maps, *gains):
    groups = len(gains)
    count, nodes, width = given.shape
    face = coupling.shape[1] // 3
    part = nodes // NP
    layer = part // NP
    share = width // groups
    outs = []
    every = []
    for p in range(count):
        slot = order[p]
        lower = []
        upper = []
        for a in range(NP):
            head = inverse[slot, a * part : a * part + 2 * layer, :].astype(F32)
            tail = inverse[slot, (a + 1) * part - 2 * layer : (a + 1) * part, :].astype(F32)
            lower.append(head[:layer])
            upper.append(tail[layer:])
        faces = jnp.concatenate(lower + upper, axis=0).astype(BF16)
        outflow = inverse[slot, nodes - face :, :]
        rows = jnp.concatenate([faces, outflow, outflow], axis=0)
        full = dot_nt(coupling[slot], rows)
        full = jnp.concatenate([full[2 * face :], full[face : 2 * face], full[:face]], axis=0).astype(BF16)
        maps[p * 3 * face : (p + 1) * 3 * face, :] = full[:, : 2 * face]
        outs.append(full[:, 2 * face :])
        if p % 2 == 1:
            at = (count + p // 2) * 3 * face
            maps[at : at + 3 * face, :] = by_half(outs[p - 1], outs[p])
        every.append(dot(rows, given[slot]).T)
    tiles = [gain[:, : 2 * face] for gain in every]
    for p in range(0, count, 2):
        tiles.append(by_half(every[p][:, 2 * face :], every[p + 1][:, 2 * face :]))
    for m, tile in enumerate(tiles):
        tile = tile.astype(BF16)
        for j in range(groups):
            piece = tile[j * share : (j + 1) * share]
            for rel in range(groups):

                @pl.when((place[0] ^ j) == rel)
                def _():
                    gains[rel][m] = piece


def unpack(map_refs, gain_refs, weights, gains, count, face):
    for pos, ref in enumerate(map_refs):
        for p in range(count):
            sides = ref[p * 3 * face : (p + 1) * 3 * face, :]
            at = (count + p // 2) * 3 * face
            outs = ref[at : at + 3 * face, :]
            other = turned(outs)
            outs = by_half(outs, other) if p % 2 == 0 else by_half(other, outs)
            full = jnp.concatenate([sides, outs], axis=1)
            weights[pos, p, : 3 * face, :] = full
            weights[pos, p, 3 * face :, :] = full[2 * face :]
    for pos in range(len(map_refs)):
        ref = gain_refs[reversed_static(pos, len(map_refs))]
        for p in range(count):
            outs = ref[count + p // 2]
            other = turned(outs)
            outs = by_half(outs, other) if p % 2 == 0 else by_half(other, outs)
            gains[pos, p] = jnp.concatenate([ref[p], outs], axis=1).astype(F32)


def neighbours(me, pos, groups):
    own = me ^ reversed_bits(pos, groups)
    below = jnp.where(own > 0, reversed_bits(((own - 1) & (groups - 1)) ^ me, groups), groups)
    above = jnp.where(own < groups - 1, reversed_bits(((own + 1) & (groups - 1)) ^ me, groups), groups)
    return below, above


def read_lags(me, states, lags, groups, count):
    def read(pos):
        below, above = neighbours(me, pos, groups)
        for p in range(count):
            lags[pos, p] = by_half(states[above, p], states[below, p])

    over(groups, read)


def over(count, body, limit=4):
    if count <= limit:
        for i in range(count):
            body(i)
    else:

        def step(i, carry):
            body(i)
            return carry

        lax.fori_loop(0, count, step, 0)


def split_trace(out):
    high = out.astype(BF16)
    return by_half(high, (out - high.astype(F32)).astype(BF16)), high


def run_chains(chosen, entries, lags, weights, gains, states, count, face):
    share = gains.shape[2]
    outs = [[] for _ in chosen]
    for p in range(count):
        for i, pos in enumerate(chosen):
            result = dot(jnp.concatenate([lags[pos, p], entries[i]], axis=1), weights[pos, p])
            first = result[:share] + gains[pos, p]
            if result.shape[0] == share:
                result = first
            else:
                result = jnp.concatenate([first, result[share:]], axis=0)
            states[pos, p] = result[:, : 2 * face].astype(BF16)
            outs[i].append(result[:, 2 * face :])
        if p < count - 1:
            entries = [split_trace(o[p])[0] for o in outs]
    return outs


def respond_kernel(place, *refs, groups, count, face):
    map_refs = refs[:groups]
    gain_refs = refs[groups : 2 * groups]
    pack, weights, gains, states, lags, unit = refs[2 * groups :]
    me = place[0]
    share = gains.shape[2]
    rows = lags.shape[2]
    half = groups // 2
    unpack(map_refs, gain_refs, weights, gains, count, face)
    states[...] = jnp.zeros_like(states)
    unit[...] = jnp.zeros_like(unit)
    row = lax.broadcasted_iota(jnp.int32, (rows, 2 * face), 0) - share
    lane = lax.broadcasted_iota(jnp.int32, (rows, 2 * face), 1)
    for pos in range(half):
        hit = jnp.logical_and(lane < face, row == lane + pos * face)
        unit[0, pos] = jnp.where(hit, 1.0, 0.0).astype(BF16)

    def sweep(k, carry):
        read_lags(me, states, lags, groups, count)

        def block(t):
            chosen = (2 * t, 2 * t + 1, 2 * t + half, 2 * t + half + 1)
            entries = [unit[jnp.minimum(k, 1), pos] for pos in chosen]
            ends = [outs[-1] for outs in run_chains(chosen, entries, lags, weights, gains, states, count, face)]
            even = by_half(ends[0], ends[1])
            odd = by_half(ends[2], ends[3])
            at = pl.ds(pl.multiple_of(t * 2 * face, 2 * face), 2 * face)
            answered = half * face
            pack[k, :answered, at] = (even[share:] + odd[share:]).astype(BF16)
            pack[k, answered : answered + share, at] = even[:share].astype(BF16)
            pack[k, answered + share :, at] = odd[:share].astype(BF16)

        over(groups // 4, block, 1)
        return carry

    lax.fori_loop(0, SWEEPS, sweep, 0)


def pick(flag, first, second):
    return jnp.where(flag != 0, first, second)


def offsets_of(ref, k):
    width = ref.shape[2]
    share = (ref.shape[1] - width) // 2
    return ref[k, width : width + share], ref[k, width + share :]


def compose_kernel(line, own, own_other, got, got_other, pack, *, mask):
    down = (line[0] // mask) % 2
    width = own.shape[2]
    share = (own.shape[1] - width) // 2
    after = []
    before = []
    inner = []
    for k in range(SWEEPS):
        mine = own[k, :width], own_other[k, :width]
        theirs = got[k, :width], got_other[k, :width]
        after.append([pick(down, a, b) for a, b in zip(mine, theirs)])
        before.append(pick(down, theirs[0], mine[0]))
        inner.append([pick(down, b, a) for a, b in zip(offsets_of(own, k), offsets_of(got, k))])
    for m in range(SWEEPS):
        for target in (m % 2, 1 - m % 2):
            stack = jnp.concatenate([after[d][(target + d) % 2] for d in range(m + 1)], axis=0)
            left = jnp.concatenate([inner[m - d][(target + d) % 2] for d in range(m + 1)], axis=1)
            if target == m % 2:
                top = jnp.concatenate([before[m - d] for d in range(m + 1)], axis=1)
                left = jnp.concatenate([top, left], axis=0)
            total = dot(left, stack)
            if target == m % 2:
                pack[m, :width] = total[:width].astype(BF16)
                total = total[width:]
            added = pick(down, offsets_of(own, m)[target], offsets_of(got, m)[target]).astype(F32)
            at = width + target * share
            pack[m, at : at + share] = (total + added).astype(BF16)


def resolve_kernel(place, line, *refs, groups, count, face, masks):
    weights, gains, top = refs[:3]
    levels = len(masks) - 1
    lower = refs[3 : 3 + 2 * levels]
    wanted = refs[3 + 2 * levels : 3 + 2 * levels + groups]
    states, lags, inflows = refs[3 + 2 * levels + groups :]
    me = place[0]
    half = groups // 2
    states[...] = jnp.zeros_like(states)
    flags = [(line[0] // mask) % 2 for mask in masks]
    values = []
    for k in range(SWEEPS):
        both = offsets_of(top, k)
        values.append([pick(flags[levels], b, jnp.zeros_like(b)) for b in both])
    for level in range(levels - 1, -1, -1):
        even, odd = lower[2 * level : 2 * level + 2]
        width = even.shape[2]
        maps = [(even[k, :width], odd[k, :width]) for k in range(SWEEPS)]
        moved = []
        for k in range(SWEEPS):
            pair = []
            for target in (0, 1):
                stack = jnp.concatenate([maps[d][(target + d) % 2] for d in range(k + 1)], axis=0)
                left = jnp.concatenate([values[k - d][(target + d) % 2] for d in range(k + 1)], axis=1)
                total = dot(left, stack) + offsets_of(even, k)[target].astype(F32)
                pair.append(pick(flags[level], total.astype(BF16), values[k][target]))
            moved.append(pair)
        values = moved
    blank = jnp.zeros((values[0][0].shape[0], 2 * face), BF16)
    for k in range(SWEEPS):
        for pos in range(groups):
            tile = (pos % half) // 2
            both = values[k][pos // half][:, tile * 2 * face : (tile + 1) * 2 * face]
            inflows[k, pos] = by_half(both if pos % 2 == 0 else turned(both), blank)

    def sweep(k, carry):
        read_lags(me, states, lags, groups, count)

        def block(t):
            chosen = tuple(4 * t + i for i in range(4))
            run_chains(
                chosen, [inflows[k, pos] for pos in chosen], lags, weights, gains, states, count, face
            )

        over(groups // 4, block, 1)
        return carry

    lax.fori_loop(0, SWEEPS - 1, sweep, 0)
    read_lags(me, states, lags, groups, count)
    for t in range(groups // 4):
        chosen = tuple(4 * t + i for i in range(4))
        entries = [inflows[SWEEPS - 1, pos] for pos in chosen]
        outs = run_chains(chosen, entries, lags, weights, gains, states, count, face)
        for i, pos in enumerate(chosen):
            target = wanted[reversed_static(pos, groups)]
            traces = [entries[i]] + [o.astype(BF16) for o in outs[i][:-1]]
            for p in range(count):
                target[p] = lags[pos, p]
            target[count] = by_half(traces[0], traces[-1])
            for m in range(1, count // 2):
                target[count + m] = by_half(traces[2 * m - 1], traces[2 * m])


def final_kernel(place, order, inverse, coupling, given, *refs):
    wanted = refs[:-2]
    placed, gathered = refs[-2:]
    count, nodes, width = given.shape
    face = coupling.shape[1] // 3
    share = width // len(wanted)
    for rel, ref in enumerate(wanted):
        at = pl.multiple_of((place[0] ^ rel) * share, share)
        for m in range(ref.shape[0]):
            gathered[m, pl.ds(at, share), :] = ref[m].astype(F32)
    blank = jnp.zeros((face, nodes), BF16)
    for p in range(count):
        slot = order[p]
        rows = coupling[slot]
        second = p == count - 1 or (p > 0 and p % 2 == 0)
        tile = 0 if p == count - 1 else (p + 1) // 2
        pair = [blank, rows[:face]] if second else [rows[:face], blank]
        sides = jnp.concatenate([rows[2 * face :], rows[face : 2 * face]] + pair, axis=0)
        traces = jnp.concatenate([gathered[p], gathered[count + tile]], axis=1).astype(BF16)
        source = given[slot].astype(F32) + dot(traces, sides).T
        placed[slot] = dot(inverse[slot], source.astype(BF16)).astype(BF16)


def gather_list(value, axis):
    values = [value]
    for mask in bits_of(lax.axis_size(axis))[::-1]:
        values = values + [swap(v, axis, mask) for v in values]
    return values


def exchange(values, axis):
    return [v if rel == 0 else swap(v, axis, rel) for rel, v in enumerate(values)]


def call(kernel, name, outs, scratch, scalars, arrays):
    def size(shape, kind):
        total = jnp.dtype(kind).itemsize
        for extent in shape:
            total *= extent
        return total

    held = sum(size(o.shape, o.dtype) for o in outs) + sum(size(a.shape, a.dtype) for a in arrays)
    held += sum(size(shape, kind) for shape, kind in scratch)
    return pl.pallas_call(
        kernel,
        out_shape=outs,
        in_specs=[SMEM] * len(scalars) + [VMEM] * len(arrays),
        out_specs=[VMEM] * len(outs),
        scratch_shapes=[pltpu.VMEM(shape, kind) for shape, kind in scratch],
        compiler_params=pltpu.CompilerParams(vmem_limit_bytes=min(held + (6 << 20), 60 << 20)),
        name=name,
    )(*scalars, *arrays)


def shards(right_sides, inverse, coupling, sweep_order):
    given = right_sides[0, 0]
    inverse = inverse[0, 0]
    order = sweep_order[0, 0]
    count, nodes, width = given.shape
    face = coupling.shape[4]
    coupling = coupling[0, 0].reshape(count, 3 * face, nodes)
    groups = lax.axis_size("span")
    share = width // groups
    half = groups // 2
    place = lax.axis_index("span").astype(jnp.int32).reshape(1)
    line = lax.axis_index("stream").astype(jnp.int32).reshape(1)
    masks = bits_of(lax.axis_size("stream"))
    tiles = count + count // 2
    shape = jax.ShapeDtypeStruct
    maps, *gains = call(
        facemap_kernel,
        "facemaps",
        [shape((tiles * 3 * face, 2 * face), BF16)] + [shape((tiles, share, 2 * face), BF16)] * groups,
        [],
        [place, order],
        [inverse, coupling, given],
    )
    all_maps = gather_list(maps, "span")
    gains = exchange(gains, "span")
    rows = share + half * face
    sizes = dict(groups=groups, count=count, face=face)
    pack, weights, gains = call(
        functools.partial(respond_kernel, **sizes),
        "respond",
        [
            shape((SWEEPS, half * face + 2 * share, half * face), BF16),
            shape((groups, count, 4 * face, 4 * face), BF16),
            shape((groups, count, share, 4 * face), F32),
        ],
        [
            ((groups + 1, count, rows, 2 * face), BF16),
            ((groups, count, rows, 2 * face), BF16),
            ((2, groups, rows, 2 * face), BF16),
        ],
        [place],
        [*all_maps, *gains],
    )
    levels = []
    for mask in masks[:-1]:
        other = swap(pack, "span", 1)
        got = swap(pack, "stream", mask)
        got_other = swap(got, "span", 1)
        levels += [got, got_other]
        (pack,) = call(
            functools.partial(compose_kernel, mask=mask),
            "compose",
            [shape(pack.shape, BF16)],
            [],
            [line],
            [pack, other, got, got_other],
        )
    top = swap(pack, "stream", masks[-1])
    wanted = call(
        functools.partial(resolve_kernel, masks=masks, **sizes),
        "resolve",
        [shape((tiles, share, 2 * face), BF16)] * groups,
        [
            ((groups + 1, count, share, 2 * face), BF16),
            ((groups, count, share, 2 * face), BF16),
            ((SWEEPS, groups, share, 2 * face), BF16),
        ],
        [place, line],
        [weights, gains, top, *levels],
    )
    wanted = exchange(wanted, "span")
    (placed,) = call(
        final_kernel,
        "finish",
        [shape((count, nodes, width), BF16)],
        [((tiles, width, 2 * face), F32)],
        [place, order],
        [inverse, coupling, given, *wanted],
    )
    return placed[None, None]


def solution(mesh):
    in_specs = (
        P("stream", "span", None, None, None),
        P("stream", "span", None, None, None),
        P("stream", "span", None, None, None, None),
        P("stream", "span", None),
    )
    out_specs = P("stream", "span", None, None, None)
    return jax.shard_map(shards, mesh=mesh, in_specs=in_specs, out_specs=out_specs, check_vma=False)
```

```python
import functools

import jax
import jax.numpy as jnp
from jax import lax
from jax.experimental import pallas as pl
from jax.experimental.pallas import tpu as pltpu
from jax.sharding import PartitionSpec as P

NP = 8
SWEEPS = 6
VMEM = pl.BlockSpec(memory_space=pltpu.VMEM)
SMEM = pl.BlockSpec(memory_space=pltpu.SMEM)
HBM = pl.BlockSpec(memory_space=pltpu.HBM)
F32 = jnp.float32
BF16 = jnp.bfloat16


def bits_of(count):
    return [1 << i for i in range(count.bit_length() - 1)]


def reversed_bits(value, count):
    bits = bits_of(count)
    total = 0
    for low, high in zip(bits, bits[::-1]):
        total = total + jnp.where((value & low) != 0, high, 0)
    return total


def reversed_static(value, count):
    bits = bits_of(count)
    return sum(high for low, high in zip(bits, bits[::-1]) if value & low)


def swap(value, axis, mask):
    count = lax.axis_size(axis)
    return lax.ppermute(value, axis, [(i, i ^ mask) for i in range(count)])


def dot(left, right):
    return jnp.dot(left, right, preferred_element_type=F32)


def dot_nt(left, right):
    return lax.dot_general(left, right, (((1,), (1,)), ((), ())), preferred_element_type=F32)


def by_half(low, high):
    lane = lax.broadcasted_iota(jnp.int32, low.shape, low.ndim - 1)
    return jnp.where(lane < low.shape[-1] // 2, low, high)


def turned(value):
    return pltpu.roll(value.astype(F32), value.shape[-1] // 2, 1).astype(value.dtype)


def facemap_kernel(place, order_far, inverse_far, coupling_far, given_far, kept, *refs):
    sends = refs[:-7]
    order, inverse, coupling, given, gathered, order_done, done = refs[-7:]
    groups = 1 << len(sends)
    count, nodes, width = given.shape
    face = coupling.shape[1] // 3
    part = nodes // NP
    first = pltpu.make_async_copy(order_far, order, order_done)
    first.start()
    pairs = ((inverse_far, inverse), (coupling_far, coupling), (given_far, given))

    def fetch(kind, slot):
        far, near = pairs[kind]
        return pltpu.make_async_copy(far.at[slot], near.at[slot], done.at[kind, slot])

    for slot in range(count):
        for kind in range(3):
            fetch(kind, slot).start()
    first.wait()
    layer = part // NP
    share = width // groups
    outs = []
    every = []
    for p in range(count):
        slot = order[p]
        for kind in range(3):
            fetch(kind, slot).wait()
        lower = []
        upper = []
        for a in range(NP):
            head = inverse[slot, a * part : a * part + 2 * layer, :].astype(F32)
            tail = inverse[slot, (a + 1) * part - 2 * layer : (a + 1) * part, :].astype(F32)
            lower.append(head[:layer])
            upper.append(tail[layer:])
        faces = jnp.concatenate(lower + upper, axis=0).astype(BF16)
        outflow = inverse[slot, nodes - face :, :]
        rows = jnp.concatenate([faces, outflow, outflow], axis=0)
        full = dot_nt(coupling[slot], rows)
        full = jnp.concatenate([full[2 * face :], full[face : 2 * face], full[:face]], axis=0).astype(BF16)
        for maps in sends:
            maps[p * 3 * face : (p + 1) * 3 * face, :] = full[:, : 2 * face]
        outs.append(full[:, 2 * face :])
        if p % 2 == 1:
            at = (count + p // 2) * 3 * face
            both = by_half(outs[p - 1], outs[p])
            for maps in sends:
                maps[at : at + 3 * face, :] = both
        every.append(dot(rows, given[slot]).T)
    tiles = [gain[:, : 2 * face] for gain in every]
    for p in range(0, count, 2):
        tiles.append(by_half(every[p][:, 2 * face :], every[p + 1][:, 2 * face :]))
    for m, tile in enumerate(tiles):
        gathered[m] = tile
    for rel in range(groups):
        at = pl.multiple_of((place[0] ^ rel) * share, share)
        for m in range(len(tiles)):
            piece = gathered[m, pl.ds(at, share), :].astype(BF16)
            if rel == 0:
                kept[m * share : (m + 1) * share, :] = piece
            else:
                target = sends[rel.bit_length() - 1]
                low = gain_row(rel, count, face, share) + m * share
                target[low : low + share, :] = piece


def gain_row(rel, count, face, share):
    first = 1 << (rel.bit_length() - 1)
    return (count + count // 2) * (3 * face + (rel - first) * share)


def unpack(map_refs, kept, weights, gains, count, face):
    for pos, ref in enumerate(map_refs):
        for p in range(count):
            sides = ref[p * 3 * face : (p + 1) * 3 * face, :]
            at = (count + p // 2) * 3 * face
            outs = ref[at : at + 3 * face, :]
            other = turned(outs)
            outs = by_half(outs, other) if p % 2 == 0 else by_half(other, outs)
            full = jnp.concatenate([sides, outs], axis=1)
            weights[pos, p, : 3 * face, :] = full
            weights[pos, p, 3 * face :, :] = full[2 * face :]
    for pos in range(len(map_refs)):
        rel = reversed_static(pos, len(map_refs))
        ref = map_refs[pos] if rel else kept
        share = gains.shape[2]
        first = gain_row(rel, count, face, share) if rel else 0
        for p in range(count):
            outs = ref[first + (count + p // 2) * share : first + (count + p // 2 + 1) * share]
            other = turned(outs)
            outs = by_half(outs, other) if p % 2 == 0 else by_half(other, outs)
            sides = ref[first + p * share : first + (p + 1) * share]
            gains[pos, p] = jnp.concatenate([sides, outs], axis=1).astype(F32)


def neighbours(me, pos, groups):
    own = me ^ reversed_bits(pos, groups)
    below = jnp.where(own > 0, reversed_bits(((own - 1) & (groups - 1)) ^ me, groups), groups)
    above = jnp.where(own < groups - 1, reversed_bits(((own + 1) & (groups - 1)) ^ me, groups), groups)
    return below, above


def read_lags(me, states, lags, groups, count):
    def read(pos):
        below, above = neighbours(me, pos, groups)
        for p in range(count):
            lags[pos, p] = by_half(states[above, p], states[below, p])

    over(groups, read)


def over(count, body, limit=4):
    if count <= limit:
        for i in range(count):
            body(i)
    else:

        def step(i, carry):
            body(i)
            return carry

        lax.fori_loop(0, count, step, 0)


def split_trace(out):
    high = out.astype(BF16)
    return by_half(high, (out - high.astype(F32)).astype(BF16)), high


def run_chains(chosen, entries, lags, weights, gains, states, count, face):
    share = gains.shape[2]
    outs = [[] for _ in chosen]
    for p in range(count):
        for i, pos in enumerate(chosen):
            result = dot(jnp.concatenate([lags[pos, p], entries[i]], axis=1), weights[pos, p])
            first = result[:share] + gains[pos, p]
            if result.shape[0] == share:
                result = first
            else:
                result = jnp.concatenate([first, result[share:]], axis=0)
            states[pos, p] = result[:, : 2 * face].astype(BF16)
            outs[i].append(result[:, 2 * face :])
        if p < count - 1:
            entries = [split_trace(o[p])[0] for o in outs]
    return outs


def respond_kernel(place, *refs, groups, count, face):
    map_refs = refs[:groups]
    kept, pack, weights, gains, states, lags, unit = refs[groups:]
    me = place[0]
    share = gains.shape[2]
    rows = lags.shape[2]
    half = groups // 2
    unpack(map_refs, kept, weights, gains, count, face)
    states[...] = jnp.zeros_like(states)
    unit[...] = jnp.zeros_like(unit)
    row = lax.broadcasted_iota(jnp.int32, (rows, 2 * face), 0) - share
    lane = lax.broadcasted_iota(jnp.int32, (rows, 2 * face), 1)
    for pos in range(half):
        hit = jnp.logical_and(lane < face, row == lane + pos * face)
        unit[0, pos] = jnp.where(hit, 1.0, 0.0).astype(BF16)

    def sweep(k, carry):
        read_lags(me, states, lags, groups, count)

        def block(t):
            chosen = (2 * t, 2 * t + 1, 2 * t + half, 2 * t + half + 1)
            entries = [unit[jnp.minimum(k, 1), pos] for pos in chosen]
            ends = [outs[-1] for outs in run_chains(chosen, entries, lags, weights, gains, states, count, face)]
            even = by_half(ends[0], ends[1])
            odd = by_half(ends[2], ends[3])
            at = pl.ds(pl.multiple_of(t * 2 * face, 2 * face), 2 * face)
            answered = half * face
            pack[k, :answered, at] = (even[share:] + odd[share:]).astype(BF16)
            pack[k, answered : answered + share, at] = even[:share].astype(BF16)
            pack[k, answered + share :, at] = odd[:share].astype(BF16)

        over(groups // 4, block, 1)
        return carry

    lax.fori_loop(0, SWEEPS, sweep, 0)


def pick(flag, first, second):
    return jnp.where(flag != 0, first, second)


def offsets_of(ref, k):
    width = ref.shape[2]
    share = (ref.shape[1] - width) // 2
    return ref[k, width : width + share], ref[k, width + share :]


def compose_kernel(line, own, own_other, got, got_other, pack, *, mask, last):
    down = (line[0] // mask) % 2
    width = own.shape[2]
    share = (own.shape[1] - width) // 2
    after = []
    before = []
    inner = []
    for k in range(SWEEPS):
        mine = own[k, :width], own_other[k, :width]
        theirs = got[k, :width], got_other[k, :width]
        after.append([pick(down, a, b) for a, b in zip(mine, theirs)])
        before.append(pick(down, theirs[0], mine[0]))
        inner.append([pick(down, b, a) for a, b in zip(offsets_of(own, k), offsets_of(got, k))])
    for m in range(SWEEPS):
        for target in (m % 2, 1 - m % 2):
            stack = jnp.concatenate([after[d][(target + d) % 2] for d in range(m + 1)], axis=0)
            left = jnp.concatenate([inner[m - d][(target + d) % 2] for d in range(m + 1)], axis=1)
            if target == m % 2 and not last:
                top = jnp.concatenate([before[m - d] for d in range(m + 1)], axis=1)
                left = jnp.concatenate([top, left], axis=0)
            total = dot(left, stack)
            if target == m % 2 and not last:
                pack[m, :width] = total[:width].astype(BF16)
                total = total[width:]
            added = pick(down, offsets_of(own, m)[target], offsets_of(got, m)[target]).astype(F32)
            at = target * share if last else width + target * share
            pack[m, at : at + share] = (total + added).astype(BF16)


def resolve_kernel(place, line, *refs, groups, count, face, masks):
    weights, gains, top = refs[:3]
    levels = len(masks) - 1
    lower = refs[3 : 3 + 2 * levels]
    wanted = refs[3 + 2 * levels : 3 + 2 * levels + groups]
    states, lags, inflows = refs[3 + 2 * levels + groups :]
    me = place[0]
    half = groups // 2
    states[...] = jnp.zeros_like(states)
    flags = [(line[0] // mask) % 2 for mask in masks]
    values = []
    for k in range(SWEEPS):
        share = top.shape[1] // 2
        both = top[k, :share], top[k, share:]
        values.append([pick(flags[levels], b, jnp.zeros_like(b)) for b in both])
    for level in range(levels - 1, -1, -1):
        even, odd = lower[2 * level : 2 * level + 2]
        width = even.shape[2]
        maps = [(even[k, :width], odd[k, :width]) for k in range(SWEEPS)]
        moved = []
        for k in range(SWEEPS):
            pair = []
            for target in (0, 1):
                stack = jnp.concatenate([maps[d][(target + d) % 2] for d in range(k + 1)], axis=0)
                left = jnp.concatenate([values[k - d][(target + d) % 2] for d in range(k + 1)], axis=1)
                total = dot(left, stack) + offsets_of(even, k)[target].astype(F32)
                pair.append(pick(flags[level], total.astype(BF16), values[k][target]))
            moved.append(pair)
        values = moved
    blank = jnp.zeros((values[0][0].shape[0], 2 * face), BF16)
    for k in range(SWEEPS):
        for pos in range(groups):
            tile = (pos % half) // 2
            both = values[k][pos // half][:, tile * 2 * face : (tile + 1) * 2 * face]
            inflows[k, pos] = by_half(both if pos % 2 == 0 else turned(both), blank)

    def sweep(k, carry):
        read_lags(me, states, lags, groups, count)

        def block(t):
            chosen = tuple(4 * t + i for i in range(4))
            run_chains(
                chosen, [inflows[k, pos] for pos in chosen], lags, weights, gains, states, count, face
            )

        over(groups // 4, block, 1)
        return carry

    lax.fori_loop(0, SWEEPS - 1, sweep, 0)
    read_lags(me, states, lags, groups, count)
    for t in range(groups // 4):
        chosen = tuple(4 * t + i for i in range(4))
        entries = [inflows[SWEEPS - 1, pos] for pos in chosen]
        outs = run_chains(chosen, entries, lags, weights, gains, states, count, face)
        for i, pos in enumerate(chosen):
            target = wanted[reversed_static(pos, groups)]
            traces = [entries[i]] + [o.astype(BF16) for o in outs[i][:-1]]
            for p in range(count):
                target[p] = lags[pos, p]
            target[count] = by_half(traces[0], traces[-1])
            for m in range(1, count // 2):
                target[count + m] = by_half(traces[2 * m - 1], traces[2 * m])


def final_kernel(place, order, inverse, coupling, given, *refs):
    wanted = refs[:-2]
    placed, gathered = refs[-2:]
    count, nodes, width = given.shape
    face = coupling.shape[1] // 3
    share = width // len(wanted)
    for rel, ref in enumerate(wanted):
        at = pl.multiple_of((place[0] ^ rel) * share, share)
        for m in range(ref.shape[0]):
            gathered[m, pl.ds(at, share), :] = ref[m].astype(F32)
    blank = jnp.zeros((face, nodes), BF16)
    for p in range(count):
        slot = order[p]
        rows = coupling[slot]
        second = p == count - 1 or (p > 0 and p % 2 == 0)
        tile = 0 if p == count - 1 else (p + 1) // 2
        pair = [blank, rows[:face]] if second else [rows[:face], blank]
        sides = jnp.concatenate([rows[2 * face :], rows[face : 2 * face]] + pair, axis=0)
        traces = jnp.concatenate([gathered[p], gathered[count + tile]], axis=1).astype(BF16)
        source = given[slot].astype(F32) + dot(traces, sides).T
        placed[slot] = dot(inverse[slot], source.astype(BF16)).astype(BF16)


def gather_list(sends, axis):
    masks = bits_of(lax.axis_size(axis))
    values = [sends[0]]
    for mask, send in zip(masks[::-1], sends[::-1]):
        values = values + [swap(send if i == 0 else v, axis, mask) for i, v in enumerate(values)]
    return values


def exchange(values, axis):
    return [v if rel == 0 else swap(v, axis, rel) for rel, v in enumerate(values)]


def call(kernel, name, outs, scratch, scalars, arrays, far=0, others=(), grant=0):
    def size(shape, kind):
        total = jnp.dtype(kind).itemsize
        for extent in shape:
            total *= extent
        return total

    held = sum(size(o.shape, o.dtype) for o in outs) + sum(size(a.shape, a.dtype) for a in arrays)
    held += sum(size(shape, kind) for shape, kind in scratch)
    return pl.pallas_call(
        kernel,
        out_shape=outs,
        in_specs=[SMEM] * len(scalars) + [VMEM] * (len(arrays) - far) + [HBM] * far,
        out_specs=[VMEM] * len(outs),
        scratch_shapes=[*others[:1], *[pltpu.VMEM(shape, kind) for shape, kind in scratch], *others[1:]],
        compiler_params=pltpu.CompilerParams(vmem_limit_bytes=grant or min(held + (6 << 20), 60 << 20)),
        name=name,
    )(*scalars, *arrays)


def shards(right_sides, inverse, coupling, sweep_order):
    given = right_sides[0, 0]
    inverse = inverse[0, 0]
    order = sweep_order[0, 0]
    count, nodes, width = given.shape
    face = coupling.shape[4]
    coupling = coupling[0, 0].reshape(count, 3 * face, nodes)
    groups = lax.axis_size("span")
    share = width // groups
    half = groups // 2
    place = lax.axis_index("span").astype(jnp.int32).reshape(1)
    line = lax.axis_index("stream").astype(jnp.int32).reshape(1)
    masks = bits_of(lax.axis_size("stream"))
    tiles = count + count // 2
    shape = jax.ShapeDtypeStruct
    spans = bits_of(groups)
    kept, *sends = call(
        facemap_kernel,
        "facemaps",
        [shape((tiles * share, 2 * face), BF16)]
        + [shape((tiles * (3 * face + mask * share), 2 * face), BF16) for mask in spans],
        [
            (inverse.shape, BF16),
            (coupling.shape, BF16),
            (given.shape, BF16),
            ((tiles, width, 2 * face), F32),
        ],
        [place],
        [pltpu.with_memory_space_constraint(a, pltpu.HBM) for a in (order, inverse, coupling, given)],
        4,
        (pltpu.SMEM(order.shape, order.dtype), pltpu.SemaphoreType.DMA, pltpu.SemaphoreType.DMA((3, count))),
    )
    arrays = gather_list(sends, "span")
    rows = share + half * face
    sizes = dict(groups=groups, count=count, face=face)
    pack, weights, gains = call(
        functools.partial(respond_kernel, **sizes),
        "respond",
        [
            shape((SWEEPS, half * face + 2 * share, half * face), BF16),
            shape((groups, count, 4 * face, 4 * face), BF16),
            shape((groups, count, share, 4 * face), F32),
        ],
        [
            ((groups + 1, count, rows, 2 * face), BF16),
            ((groups, count, rows, 2 * face), BF16),
            ((2, groups, rows, 2 * face), BF16),
        ],
        [place],
        [*arrays, kept],
    )
    levels = []
    for mask in masks[:-1]:
        last = mask == masks[-2]
        wide = 2 * share if last else pack.shape[1]
        other = swap(pack, "span", 1)
        got = swap(pack, "stream", mask)
        got_other = swap(got, "span", 1)
        levels += [got, got_other]
        (pack,) = call(
            functools.partial(compose_kernel, mask=mask, last=last),
            "compose",
            [shape((SWEEPS, wide, pack.shape[2]), BF16)],
            [],
            [line],
            [pack, other, got, got_other],
        )
    top = swap(pack, "stream", masks[-1])
    wanted = call(
        functools.partial(resolve_kernel, masks=masks, **sizes),
        "resolve",
        [shape((tiles, share, 2 * face), BF16)] * groups,
        [
            ((groups + 1, count, share, 2 * face), BF16),
            ((groups, count, share, 2 * face), BF16),
            ((SWEEPS, groups, share, 2 * face), BF16),
        ],
        [place, line],
        [weights, gains, top, *levels],
    )
    wanted = exchange(wanted, "span")
    (placed,) = call(
        final_kernel,
        "finish",
        [shape((count, nodes, width), BF16)],
        [((tiles, width, 2 * face), F32)],
        [place, order],
        [inverse, coupling, given, *wanted],
    )
    return placed[None, None]


def solution(mesh):
    in_specs = (
        P("stream", "span", None, None, None),
        P("stream", "span", None, None, None),
        P("stream", "span", None, None, None, None),
        P("stream", "span", None),
    )
    out_specs = P("stream", "span", None, None, None)
    return jax.shard_map(shards, mesh=mesh, in_specs=in_specs, out_specs=out_specs, check_vma=False)
```

```python
import functools

import jax
import jax.numpy as jnp
from jax import lax
from jax.experimental import pallas as pl
from jax.experimental.pallas import tpu as pltpu
from jax.sharding import PartitionSpec as P

NP = 8
SWEEPS = 6
VMEM = pl.BlockSpec(memory_space=pltpu.VMEM)
SMEM = pl.BlockSpec(memory_space=pltpu.SMEM)
HBM = pl.BlockSpec(memory_space=pltpu.HBM)
F32 = jnp.float32
BF16 = jnp.bfloat16


def bits_of(count):
    return [1 << i for i in range(count.bit_length() - 1)]


def reversed_bits(value, count):
    bits = bits_of(count)
    total = 0
    for low, high in zip(bits, bits[::-1]):
        total = total + jnp.where((value & low) != 0, high, 0)
    return total


def reversed_static(value, count):
    bits = bits_of(count)
    return sum(high for low, high in zip(bits, bits[::-1]) if value & low)


def swap(value, axis, mask):
    count = lax.axis_size(axis)
    return lax.ppermute(value, axis, [(i, i ^ mask) for i in range(count)])


def crossing(masks):
    pairs = []
    for i in range(2 * masks[-1]):
        inner = bool(i & masks[-1]) != bool(i & masks[-2])
        pairs.append((i, i ^ (masks[-1] | masks[-2] if inner else 1)))
    return pairs


def dot(left, right):
    return jnp.dot(left, right, preferred_element_type=F32)


def dot_nt(left, right):
    return lax.dot_general(left, right, (((1,), (1,)), ((), ())), preferred_element_type=F32)


def by_half(low, high):
    lane = lax.broadcasted_iota(jnp.int32, low.shape, low.ndim - 1)
    return jnp.where(lane < low.shape[-1] // 2, low, high)


def turned(value):
    return pltpu.roll(value.astype(F32), value.shape[-1] // 2, 1).astype(value.dtype)


def facemap_kernel(place, order_far, inverse_far, coupling_far, given_far, kept, *refs):
    sends = refs[:-7]
    order, inverse, coupling, given, gathered, order_done, done = refs[-7:]
    groups = 1 << len(sends)
    count, nodes, width = given.shape
    face = coupling.shape[1] // 3
    part = nodes // NP
    first = pltpu.make_async_copy(order_far, order, order_done)
    first.start()
    pairs = ((inverse_far, inverse), (coupling_far, coupling), (given_far, given))

    def fetch(kind, slot):
        far, near = pairs[kind]
        return pltpu.make_async_copy(far.at[slot], near.at[slot], done.at[kind, slot])

    for slot in range(count):
        for kind in range(3):
            fetch(kind, slot).start()
    first.wait()
    layer = part // NP
    share = width // groups
    outs = []
    every = []
    for p in range(count):
        slot = order[p]
        for kind in range(3):
            fetch(kind, slot).wait()
        lower = []
        upper = []
        for a in range(NP):
            head = inverse[slot, a * part : a * part + 2 * layer, :].astype(F32)
            tail = inverse[slot, (a + 1) * part - 2 * layer : (a + 1) * part, :].astype(F32)
            lower.append(head[:layer])
            upper.append(tail[layer:])
        faces = jnp.concatenate(lower + upper, axis=0).astype(BF16)
        outflow = inverse[slot, nodes - face :, :]
        rows = jnp.concatenate([faces, outflow, outflow], axis=0)
        full = dot_nt(coupling[slot], rows)
        full = jnp.concatenate([full[2 * face :], full[face : 2 * face], full[:face]], axis=0).astype(BF16)
        for maps in sends:
            maps[p * 3 * face : (p + 1) * 3 * face, :] = full[:, : 2 * face]
        outs.append(full[:, 2 * face :])
        if p % 2 == 1:
            at = (count + p // 2) * 3 * face
            both = by_half(outs[p - 1], outs[p])
            for maps in sends:
                maps[at : at + 3 * face, :] = both
        every.append(dot(rows, given[slot]).T)
    tiles = [gain[:, : 2 * face] for gain in every]
    for p in range(0, count, 2):
        tiles.append(by_half(every[p][:, 2 * face :], every[p + 1][:, 2 * face :]))
    for m, tile in enumerate(tiles):
        gathered[m] = tile
    for rel in range(groups):
        at = pl.multiple_of((place[0] ^ rel) * share, share)
        for m in range(len(tiles)):
            piece = gathered[m, pl.ds(at, share), :].astype(BF16)
            if rel == 0:
                kept[m * share : (m + 1) * share, :] = piece
            else:
                target = sends[rel.bit_length() - 1]
                low = gain_row(rel, count, face, share) + m * share
                target[low : low + share, :] = piece


def gain_row(rel, count, face, share):
    first = 1 << (rel.bit_length() - 1)
    return (count + count // 2) * (3 * face + (rel - first) * share)


def unpack(map_refs, kept, weights, gains, count, face):
    for pos, ref in enumerate(map_refs):
        for p in range(count):
            sides = ref[p * 3 * face : (p + 1) * 3 * face, :]
            at = (count + p // 2) * 3 * face
            outs = ref[at : at + 3 * face, :]
            other = turned(outs)
            outs = by_half(outs, other) if p % 2 == 0 else by_half(other, outs)
            full = jnp.concatenate([sides, outs], axis=1)
            weights[pos, p, : 3 * face, :] = full
            weights[pos, p, 3 * face :, :] = full[2 * face :]
    for pos in range(len(map_refs)):
        rel = reversed_static(pos, len(map_refs))
        ref = map_refs[pos] if rel else kept
        share = gains.shape[2]
        first = gain_row(rel, count, face, share) if rel else 0
        for p in range(count):
            outs = ref[first + (count + p // 2) * share : first + (count + p // 2 + 1) * share]
            other = turned(outs)
            outs = by_half(outs, other) if p % 2 == 0 else by_half(other, outs)
            sides = ref[first + p * share : first + (p + 1) * share]
            gains[pos, p] = jnp.concatenate([sides, outs], axis=1).astype(F32)


def neighbours(me, pos, groups):
    own = me ^ reversed_bits(pos, groups)
    below = jnp.where(own > 0, reversed_bits(((own - 1) & (groups - 1)) ^ me, groups), groups)
    above = jnp.where(own < groups - 1, reversed_bits(((own + 1) & (groups - 1)) ^ me, groups), groups)
    return below, above


def read_lags(me, states, lags, groups, count):
    def read(pos):
        below, above = neighbours(me, pos, groups)
        for p in range(count):
            lags[pos, p] = by_half(states[above, p], states[below, p])

    over(groups, read)


def over(count, body, limit=4):
    if count <= limit:
        for i in range(count):
            body(i)
    else:

        def step(i, carry):
            body(i)
            return carry

        lax.fori_loop(0, count, step, 0)


def split_trace(out):
    high = out.astype(BF16)
    return by_half(high, (out - high.astype(F32)).astype(BF16)), high


def run_chains(chosen, entries, lags, weights, gains, states, count, face):
    share = gains.shape[2]
    outs = [[] for _ in chosen]
    for p in range(count):
        for i, pos in enumerate(chosen):
            rows = entries[i].shape[0]
            result = dot(jnp.concatenate([lags[pos, p, :rows], entries[i]], axis=1), weights[pos, p])
            first = result[:share] + gains[pos, p]
            if result.shape[0] == share:
                result = first
            else:
                result = jnp.concatenate([first, result[share:]], axis=0)
            states[pos, p, :rows] = result[:, : 2 * face].astype(BF16)
            outs[i].append(result[:, 2 * face :])
        if p < count - 1:
            entries = [split_trace(o[p])[0] for o in outs]
    return outs


def respond_kernel(place, *refs, groups, count, face):
    map_refs = refs[:groups]
    kept, pack, weights, gains, states, lags, unit = refs[groups:]
    me = place[0]
    share = gains.shape[2]
    rows = lags.shape[2]
    half = groups // 2
    unpack(map_refs, kept, weights, gains, count, face)
    states[...] = jnp.zeros_like(states)
    unit[...] = jnp.zeros_like(unit)
    row = lax.broadcasted_iota(jnp.int32, (rows, 2 * face), 0) - share
    lane = lax.broadcasted_iota(jnp.int32, (rows, 2 * face), 1)
    for pos in range(half):
        hit = jnp.logical_and(lane < face, row == lane + pos * face)
        unit[0, pos] = jnp.where(hit, 1.0, 0.0).astype(BF16)

    def sweep(k, parity):
        read_lags(me, states, lags, groups, count)

        def block(t):
            live = [2 * t + half * parity, 2 * t + 1 + half * parity]
            bare = [2 * t + half * (1 - parity), 2 * t + 1 + half * (1 - parity)]
            entries = [unit[jnp.minimum(k, 1), pos] for pos in live]
            entries += [jnp.zeros((share, 2 * face), BF16)] * 2
            chosen = live + bare
            ends = [outs[-1] for outs in run_chains(chosen, entries, lags, weights, gains, states, count, face)]
            at = pl.ds(pl.multiple_of(t * 2 * face, 2 * face), 2 * face)
            answered = half * face
            full = by_half(ends[0], ends[1])
            pack[k, :answered, at] = full[share:].astype(BF16)
            for target, tile in ((parity, full[:share]), (1 - parity, by_half(ends[2], ends[3]))):
                low = answered + target * share
                pack[k, low : low + share, at] = tile.astype(BF16)

        over(groups // 4, block, 1)

    def both(i, carry):
        sweep(2 * i, 0)
        sweep(2 * i + 1, 1)
        return carry

    lax.fori_loop(0, SWEEPS // 2, both, 0)


def pick(flag, first, second):
    return jnp.where(flag != 0, first, second)


def offsets_of(ref, k):
    width = ref.shape[2]
    share = (ref.shape[1] - width) // 2
    return ref[k, width : width + share], ref[k, width + share :]


def compose_kernel(line, own, own_other, got, got_other, *outs, mask):
    down = (line[0] // mask) % 2
    width = own.shape[2]
    share = (own.shape[1] - width) // 2
    after = []
    before = []
    inner = []
    for k in range(SWEEPS):
        mine = own[k, :width], own_other[k, :width]
        theirs = got[k, :width], got_other[k, :width]
        after.append([pick(down, a, b) for a, b in zip(mine, theirs)])
        before.append(pick(down, theirs[0], mine[0]))
        inner.append([pick(down, b, a) for a, b in zip(offsets_of(own, k), offsets_of(got, k))])
    for m in range(SWEEPS):
        for target in (m % 2, 1 - m % 2):
            stack = jnp.concatenate([after[d][(target + d) % 2] for d in range(m + 1)], axis=0)
            left = jnp.concatenate([inner[m - d][(target + d) % 2] for d in range(m + 1)], axis=1)
            if target == m % 2:
                top = jnp.concatenate([before[m - d] for d in range(m + 1)], axis=1)
                left = jnp.concatenate([top, left], axis=0)
            total = dot(left, stack)
            if target == m % 2:
                outs[0][m, :width] = total[:width].astype(BF16)
                total = total[width:]
            added = pick(down, offsets_of(own, m)[target], offsets_of(got, m)[target]).astype(F32)
            at = target * share if len(outs) == 2 else width + target * share
            outs[-1][m, at : at + share] = (total + added).astype(BF16)


def halves_of(ref, k):
    share = ref.shape[1] // 2
    return ref[k, :share], ref[k, share:]


def moved_by(values, maps, k):
    pair = []
    for target in (0, 1):
        stack = jnp.concatenate([maps[d][(target + d) % 2] for d in range(k + 1)], axis=0)
        left = jnp.concatenate([values[k - d][(target + d) % 2] for d in range(k + 1)], axis=1)
        pair.append(dot(left, stack))
    return pair


def join_kernel(even, odd, entry, own, joined):
    maps = [(even[k], odd[k]) for k in range(SWEEPS)]
    values = [halves_of(entry, k) for k in range(SWEEPS)]
    share = own.shape[1] // 2
    for k in range(SWEEPS):
        added = halves_of(own, k)
        for target, total in enumerate(moved_by(values, maps, k)):
            total = total + added[target].astype(F32)
            joined[k, target * share : (target + 1) * share] = total.astype(BF16)


def resolve_kernel(place, line, *refs, groups, count, face, masks):
    weights, gains, ahead, second, third, ahead_even, ahead_odd = refs[:7]
    levels = len(masks) - 2
    lower = refs[7 : 7 + 2 * levels]
    wanted = refs[7 + 2 * levels : 7 + 2 * levels + groups]
    states, lags, inflows = refs[7 + 2 * levels + groups :]
    me = place[0]
    half = groups // 2
    states[...] = jnp.zeros_like(states)
    flags = [(line[0] // mask) % 2 for mask in masks]
    maps = [(ahead_even[k], ahead_odd[k]) for k in range(SWEEPS)]
    given = [halves_of(third, k) for k in range(SWEEPS)]
    values = []
    for k in range(SWEEPS):
        pair = []
        for target, total in enumerate(moved_by(given, maps, k)):
            own = halves_of(ahead, k)[target]
            last = (total + own.astype(F32)).astype(BF16)
            upper = pick(flags[-2], last, halves_of(second, k)[target])
            pair.append(pick(flags[-1], upper, pick(flags[-2], own, jnp.zeros_like(own))))
        values.append(pair)
    for level in range(levels - 1, -1, -1):
        even, odd = lower[2 * level : 2 * level + 2]
        width = even.shape[2]
        maps = [(even[k, :width], odd[k, :width]) for k in range(SWEEPS)]
        moved = []
        for k in range(SWEEPS):
            pair = []
            for target, total in enumerate(moved_by(values, maps, k)):
                total = total + offsets_of(even, k)[target].astype(F32)
                pair.append(pick(flags[level], total.astype(BF16), values[k][target]))
            moved.append(pair)
        values = moved
    blank = jnp.zeros((values[0][0].shape[0], 2 * face), BF16)
    for k in range(SWEEPS):
        for pos in range(groups):
            tile = (pos % half) // 2
            both = values[k][pos // half][:, tile * 2 * face : (tile + 1) * 2 * face]
            inflows[k, pos] = by_half(both if pos % 2 == 0 else turned(both), blank)

    def sweep(k, carry):
        read_lags(me, states, lags, groups, count)

        def block(t):
            chosen = tuple(4 * t + i for i in range(4))
            run_chains(
                chosen, [inflows[k, pos] for pos in chosen], lags, weights, gains, states, count, face
            )

        over(groups // 4, block, 1)
        return carry

    lax.fori_loop(0, SWEEPS - 1, sweep, 0)
    read_lags(me, states, lags, groups, count)
    for t in range(groups // 4):
        chosen = tuple(4 * t + i for i in range(4))
        entries = [inflows[SWEEPS - 1, pos] for pos in chosen]
        outs = run_chains(chosen, entries, lags, weights, gains, states, count, face)
        for i, pos in enumerate(chosen):
            target = wanted[reversed_static(pos, groups)]
            traces = [entries[i]] + [o.astype(BF16) for o in outs[i][:-1]]
            for p in range(count):
                target[p] = lags[pos, p]
            target[count] = by_half(traces[0], traces[-1])
            for m in range(1, count // 2):
                target[count + m] = by_half(traces[2 * m - 1], traces[2 * m])


def final_kernel(place, order, inverse, coupling, given, *refs):
    wanted = refs[:-2]
    placed, gathered = refs[-2:]
    count, nodes, width = given.shape
    face = coupling.shape[1] // 3
    share = width // len(wanted)
    for rel, ref in enumerate(wanted):
        at = pl.multiple_of((place[0] ^ rel) * share, share)
        for m in range(ref.shape[0]):
            gathered[m, pl.ds(at, share), :] = ref[m].astype(F32)
    blank = jnp.zeros((face, nodes), BF16)
    for p in range(count):
        slot = order[p]
        rows = coupling[slot]
        second = p == count - 1 or (p > 0 and p % 2 == 0)
        tile = 0 if p == count - 1 else (p + 1) // 2
        pair = [blank, rows[:face]] if second else [rows[:face], blank]
        sides = jnp.concatenate([rows[2 * face :], rows[face : 2 * face]] + pair, axis=0)
        traces = jnp.concatenate([gathered[p], gathered[count + tile]], axis=1).astype(BF16)
        source = given[slot].astype(F32) + dot(traces, sides).T
        placed[slot] = dot(inverse[slot], source.astype(BF16)).astype(BF16)


def gather_list(sends, axis):
    masks = bits_of(lax.axis_size(axis))
    values = [sends[0]]
    for mask, send in zip(masks[::-1], sends[::-1]):
        values = values + [swap(send if i == 0 else v, axis, mask) for i, v in enumerate(values)]
    return values


def exchange(values, axis):
    return [v if rel == 0 else swap(v, axis, rel) for rel, v in enumerate(values)]


def call(kernel, outs, scratch, scalars, arrays, far=0, others=(), grant=0):
    def size(shape, kind):
        total = jnp.dtype(kind).itemsize
        for extent in shape:
            total *= extent
        return total

    held = sum(size(o.shape, o.dtype) for o in outs) + sum(size(a.shape, a.dtype) for a in arrays)
    held += sum(size(shape, kind) for shape, kind in scratch)
    return pl.pallas_call(
        kernel,
        out_shape=outs,
        in_specs=[SMEM] * len(scalars) + [VMEM] * (len(arrays) - far) + [HBM] * far,
        out_specs=[VMEM] * len(outs),
        scratch_shapes=[*others[:1], *[pltpu.VMEM(shape, kind) for shape, kind in scratch], *others[1:]],
        compiler_params=pltpu.CompilerParams(vmem_limit_bytes=grant or min(held + (6 << 20), 60 << 20)),
    )(*scalars, *arrays)


def shards(right_sides, inverse, coupling, sweep_order):
    given = right_sides[0, 0]
    inverse = inverse[0, 0]
    order = sweep_order[0, 0]
    count, nodes, width = given.shape
    face = coupling.shape[4]
    coupling = coupling[0, 0].reshape(count, 3 * face, nodes)
    groups = lax.axis_size("span")
    share = width // groups
    half = groups // 2
    place = lax.axis_index("span").astype(jnp.int32).reshape(1)
    line = lax.axis_index("stream").astype(jnp.int32).reshape(1)
    masks = bits_of(lax.axis_size("stream"))
    tiles = count + count // 2
    shape = jax.ShapeDtypeStruct
    spans = bits_of(groups)
    kept, *sends = call(
        facemap_kernel,
        [shape((tiles * share, 2 * face), BF16)]
        + [shape((tiles * (3 * face + mask * share), 2 * face), BF16) for mask in spans],
        [
            (inverse.shape, BF16),
            (coupling.shape, BF16),
            (given.shape, BF16),
            ((tiles, width, 2 * face), F32),
        ],
        [place],
        [pltpu.with_memory_space_constraint(a, pltpu.HBM) for a in (order, inverse, coupling, given)],
        4,
        (pltpu.SMEM(order.shape, order.dtype), pltpu.SemaphoreType.DMA, pltpu.SemaphoreType.DMA((3, count))),
    )
    arrays = gather_list(sends, "span")
    rows = share + half * face
    sizes = dict(groups=groups, count=count, face=face)
    pack, weights, gains = call(
        functools.partial(respond_kernel, **sizes),
        [
            shape((SWEEPS, half * face + 2 * share, half * face), BF16),
            shape((groups, count, 4 * face, 4 * face), BF16),
            shape((groups, count, share, 4 * face), F32),
        ],
        [
            ((groups + 1, count, rows, 2 * face), BF16),
            ((groups, count, rows, 2 * face), BF16),
            ((2, groups, rows, 2 * face), BF16),
        ],
        [place],
        [*arrays, kept],
    )
    levels = []
    for mask in masks[:-2]:
        other = swap(pack, "span", 1)
        got = swap(pack, "stream", mask)
        got_other = swap(got, "span", 1)
        levels += [got, got_other]
        if mask == masks[-3]:
            wide = [pack.shape[2], 2 * share]
        else:
            wide = [pack.shape[1]]
        pack, *rest = call(
            functools.partial(compose_kernel, mask=mask),
            [shape((SWEEPS, extent, pack.shape[2]), BF16) for extent in wide],
            [],
            [line],
            [pack, other, got, got_other],
        )
    (offset,) = rest
    ahead = swap(offset, "stream", masks[-2])
    other = swap(pack, "span", 1)
    ahead_even = swap(pack, "stream", masks[-2])
    (joined,) = call(join_kernel, [shape(offset.shape, BF16)], [], [], [pack, other, ahead, offset])
    second = lax.ppermute(joined, "stream", crossing(masks))
    third = swap(joined, "stream", masks[-1])
    ahead_odd = swap(ahead_even, "span", 1)
    wanted = call(
        functools.partial(resolve_kernel, masks=masks, **sizes),
        [shape((tiles, share, 2 * face), BF16)] * groups,
        [
            ((groups + 1, count, share, 2 * face), BF16),
            ((groups, count, share, 2 * face), BF16),
            ((SWEEPS, groups, share, 2 * face), BF16),
        ],
        [place, line],
        [weights, gains, ahead, second, third, ahead_even, ahead_odd, *levels],
    )
    wanted = exchange(wanted, "span")
    (placed,) = call(
        final_kernel,
        [shape((count, nodes, width), BF16)],
        [((tiles, width, 2 * face), F32)],
        [place, order],
        [inverse, coupling, given, *wanted],
    )
    return placed[None, None]


def solution(mesh):
    in_specs = (
        P("stream", "span", None, None, None),
        P("stream", "span", None, None, None),
        P("stream", "span", None, None, None, None),
        P("stream", "span", None),
    )
    out_specs = P("stream", "span", None, None, None)
    return jax.shard_map(shards, mesh=mesh, in_specs=in_specs, out_specs=out_specs, check_vma=False)
```

```python
import functools

import jax
import jax.numpy as jnp
from jax import lax
from jax.experimental import pallas as pl
from jax.experimental.pallas import tpu as pltpu
from jax.sharding import PartitionSpec as P

NP = 8
SWEEPS = 6
VMEM = pl.BlockSpec(memory_space=pltpu.VMEM)
SMEM = pl.BlockSpec(memory_space=pltpu.SMEM)
HBM = pl.BlockSpec(memory_space=pltpu.HBM)
F32 = jnp.float32
BF16 = jnp.bfloat16


def bits_of(count):
    return [1 << i for i in range(count.bit_length() - 1)]


def reversed_bits(value, count):
    bits = bits_of(count)
    total = 0
    for low, high in zip(bits, bits[::-1]):
        total = total + jnp.where((value & low) != 0, high, 0)
    return total


def reversed_static(value, count):
    bits = bits_of(count)
    return sum(high for low, high in zip(bits, bits[::-1]) if value & low)


def swap(value, axis, mask):
    count = lax.axis_size(axis)
    return lax.ppermute(value, axis, [(i, i ^ mask) for i in range(count)])


def crossing(masks):
    pairs = []
    for i in range(2 * masks[-1]):
        inner = bool(i & masks[-1]) != bool(i & masks[-2])
        pairs.append((i, i ^ (masks[-1] | masks[-2] if inner else 1)))
    return pairs


def dot(left, right):
    return jnp.dot(left, right, preferred_element_type=F32)


def dot_nt(left, right):
    return lax.dot_general(left, right, (((1,), (1,)), ((), ())), preferred_element_type=F32)


def by_half(low, high):
    lane = lax.broadcasted_iota(jnp.int32, low.shape, low.ndim - 1)
    return jnp.where(lane < low.shape[-1] // 2, low, high)


def turned(value):
    return pltpu.roll(value.astype(F32), value.shape[-1] // 2, 1).astype(value.dtype)


def facemap_kernel(place, order_far, inverse_far, coupling_far, given_far, maps, *refs):
    gains = refs[:-7]
    order, inverse, coupling, given, gathered, order_done, done = refs[-7:]
    groups = len(gains)
    count, nodes, width = given.shape
    face = coupling.shape[1] // 3
    part = nodes // NP
    first = pltpu.make_async_copy(order_far, order, order_done)
    first.start()
    pairs = ((inverse_far, inverse), (coupling_far, coupling), (given_far, given))

    def fetch(kind, slot):
        far, near = pairs[kind]
        return pltpu.make_async_copy(far.at[slot], near.at[slot], done.at[kind, slot])

    for slot in range(count):
        for kind in range(3):
            fetch(kind, slot).start()
    first.wait()
    layer = part // NP
    share = width // groups
    outs = []
    every = []
    for p in range(count):
        slot = order[p]
        for kind in range(3):
            fetch(kind, slot).wait()
        lower = []
        upper = []
        for a in range(NP):
            head = inverse[slot, a * part : a * part + 2 * layer, :].astype(F32)
            tail = inverse[slot, (a + 1) * part - 2 * layer : (a + 1) * part, :].astype(F32)
            lower.append(head[:layer])
            upper.append(tail[layer:])
        faces = jnp.concatenate(lower + upper, axis=0).astype(BF16)
        outflow = inverse[slot, nodes - face :, :]
        rows = jnp.concatenate([faces, outflow, outflow], axis=0)
        full = dot_nt(coupling[slot], rows)
        full = jnp.concatenate([full[2 * face :], full[face : 2 * face], full[:face]], axis=0).astype(BF16)
        maps[p * 3 * face : (p + 1) * 3 * face, :] = full[:, : 2 * face]
        outs.append(full[:, 2 * face :])
        if p % 2 == 1:
            at = (count + p // 2) * 3 * face
            maps[at : at + 3 * face, :] = by_half(outs[p - 1], outs[p])
        every.append(dot(rows, given[slot]).T)
    tiles = [gain[:, : 2 * face] for gain in every]
    for p in range(0, count, 2):
        tiles.append(by_half(every[p][:, 2 * face :], every[p + 1][:, 2 * face :]))
    for m, tile in enumerate(tiles):
        gathered[m] = tile
    for rel in range(groups):
        at = pl.multiple_of((place[0] ^ rel) * share, share)
        for m in range(len(tiles)):
            gains[rel][m] = gathered[m, pl.ds(at, share), :].astype(BF16)


def unpack_maps(map_refs, weights, count, face):
    for pos, ref in enumerate(map_refs):
        for p in range(count):
            sides = ref[p * 3 * face : (p + 1) * 3 * face, :]
            at = (count + p // 2) * 3 * face
            outs = ref[at : at + 3 * face, :]
            other = turned(outs)
            outs = by_half(outs, other) if p % 2 == 0 else by_half(other, outs)
            full = jnp.concatenate([sides, outs], axis=1)
            weights[pos, p, : 3 * face, :] = full
            weights[pos, p, 3 * face :, :] = full[2 * face :]


def unpack_gains(gain_refs, gains, count):
    for rel, ref in enumerate(gain_refs):
        for p in range(count):
            outs = ref[count + p // 2]
            other = turned(outs)
            outs = by_half(outs, other) if p % 2 == 0 else by_half(other, outs)
            gains[reversed_static(rel, len(gain_refs)), p] = jnp.concatenate([ref[p], outs], axis=1).astype(F32)


def neighbours(me, pos, groups):
    own = me ^ reversed_bits(pos, groups)
    below = jnp.where(own > 0, reversed_bits(((own - 1) & (groups - 1)) ^ me, groups), groups)
    above = jnp.where(own < groups - 1, reversed_bits(((own + 1) & (groups - 1)) ^ me, groups), groups)
    return below, above


def read_lags(me, states, lags, groups, count, first=0, live=None):
    def read(i):
        pos = first + i
        below, above = neighbours(me, pos, groups)
        for p in range(count):
            lags[pos, p] = by_half(states[above, p], states[below, p])

    over(live or groups, read)


def over(count, body, limit=4):
    if count <= limit:
        for i in range(count):
            body(i)
    else:

        def step(i, carry):
            body(i)
            return carry

        lax.fori_loop(0, count, step, 0)


def split_trace(out):
    high = out.astype(BF16)
    return by_half(high, (out - high.astype(F32)).astype(BF16)), high


def run_chains(chosen, entries, lags, weights, gains, states, count, face):
    outs = [[] for _ in chosen]
    for p in range(count):
        for i, pos in enumerate(chosen):
            result = dot(jnp.concatenate([lags[pos, p], entries[i]], axis=1), weights[pos, p])
            if gains is not None:
                result = result + gains[pos, p]
            states[pos, p] = result[:, : 2 * face].astype(BF16)
            outs[i].append(result[:, 2 * face :])
        if p < count - 1:
            entries = [split_trace(o[p])[0] for o in outs]
    return outs


def respond_kernel(place, *refs, groups, count, face):
    map_refs = refs[:groups]
    response, weights, states, lags, unit = refs[groups:]
    me = place[0]
    half = groups // 2
    unpack_maps(map_refs, weights, count, face)
    states[...] = jnp.zeros_like(states)
    unit[...] = jnp.zeros_like(unit)
    row = lax.broadcasted_iota(jnp.int32, unit.shape[2:], 0)
    lane = lax.broadcasted_iota(jnp.int32, unit.shape[2:], 1)
    for pos in range(half):
        hit = jnp.logical_and(lane < face, row == lane + pos * face)
        unit[0, pos] = jnp.where(hit, 1.0, 0.0).astype(BF16)

    def sweep(k, parity):
        read_lags(me, states, lags, groups, count, half * parity, half)

        def block(t):
            chosen = [2 * t + half * parity, 2 * t + 1 + half * parity]
            entries = [unit[jnp.minimum(k, 1), pos] for pos in chosen]
            ends = [outs[-1] for outs in run_chains(chosen, entries, lags, weights, None, states, count, face)]
            at = pl.ds(pl.multiple_of(t * 2 * face, 2 * face), 2 * face)
            response[k, :, at] = by_half(ends[0], ends[1]).astype(BF16)

        over(groups // 4, block, 1)

    def both(i, carry):
        sweep(2 * i, 0)
        sweep(2 * i + 1, 1)
        return carry

    lax.fori_loop(0, SWEEPS // 2, both, 0)


def offset_kernel(place, weights, *refs, groups, count, face):
    gain_refs = refs[:groups]
    offset, gains, states, lags = refs[groups:]
    me = place[0]
    half = groups // 2
    unpack_gains(gain_refs, gains, count)
    states[...] = jnp.zeros_like(states)
    share = gains.shape[2]
    blank = jnp.zeros((share, 2 * face), BF16)

    def sweep(k, carry):
        read_lags(me, states, lags, groups, count)

        def block(t):
            chosen = [2 * t, 2 * t + 1, 2 * t + half, 2 * t + 1 + half]
            outs = run_chains(chosen, [blank] * 4, lags, weights, gains, states, count, face)
            ends = [out[-1] for out in outs]
            at = pl.ds(pl.multiple_of(t * 2 * face, 2 * face), 2 * face)
            offset[k, :share, at] = by_half(ends[0], ends[1]).astype(BF16)
            offset[k, share:, at] = by_half(ends[2], ends[3]).astype(BF16)

        over(groups // 4, block, 1)
        return carry

    lax.fori_loop(0, SWEEPS, sweep, 0)


def pick(flag, first, second):
    return jnp.where(flag != 0, first, second)


def pair_offset_kernel(line, own, other, got, got_other, own_offset, got_offset, offset, *, mask):
    down = (line[0] // mask) % 2
    share = own_offset.shape[1] // 2
    maps = [
        (pick(down, own[k], got[k]), pick(down, other[k], got_other[k])) for k in range(SWEEPS)
    ]
    values = []
    for k in range(SWEEPS):
        both = zip(halves_of(got_offset, k), halves_of(own_offset, k))
        values.append([pick(down, a, b) for a, b in both])
    for k in range(SWEEPS):
        both = zip(halves_of(own_offset, k), halves_of(got_offset, k))
        added = [pick(down, a, b).astype(F32) for a, b in both]
        for target, total in enumerate(moved_by(values, maps, k)):
            offset[k, target * share : (target + 1) * share] = (total + added[target]).astype(BF16)


def pair_map_kernel(line, own, other, got, got_other, response, *, mask):
    down = (line[0] // mask) % 2
    after = [
        (pick(down, own[k], got[k]), pick(down, other[k], got_other[k])) for k in range(SWEEPS)
    ]
    before = [pick(down, got[k], own[k]) for k in range(SWEEPS)]
    for m in range(SWEEPS):
        stack = jnp.concatenate([after[d][(m + d) % 2] for d in range(m + 1)], axis=0)
        left = jnp.concatenate([before[m - d] for d in range(m + 1)], axis=1)
        response[m] = dot(left, stack).astype(BF16)


def halves_of(ref, k):
    share = ref.shape[1] // 2
    return ref[k, :share], ref[k, share:]


def moved_by(values, maps, k):
    pair = []
    for target in (0, 1):
        stack = jnp.concatenate([maps[d][(target + d) % 2] for d in range(k + 1)], axis=0)
        left = jnp.concatenate([values[k - d][(target + d) % 2] for d in range(k + 1)], axis=1)
        pair.append(dot(left, stack))
    return pair


def join_kernel(even, odd, entry, own, joined):
    maps = [(even[k], odd[k]) for k in range(SWEEPS)]
    values = [halves_of(entry, k) for k in range(SWEEPS)]
    share = own.shape[1] // 2
    for k in range(SWEEPS):
        added = halves_of(own, k)
        for target, total in enumerate(moved_by(values, maps, k)):
            total = total + added[target].astype(F32)
            joined[k, target * share : (target + 1) * share] = total.astype(BF16)


def resolve_kernel(place, line, *refs, groups, count, face, masks):
    weights, gains, ahead, second, third, ahead_even, ahead_odd = refs[:7]
    levels = len(masks) - 2
    lower = refs[7 : 7 + 3 * levels]
    wanted = refs[7 + 3 * levels : 7 + 3 * levels + groups]
    states, lags, inflows = refs[7 + 3 * levels + groups :]
    me = place[0]
    half = groups // 2
    states[...] = jnp.zeros_like(states)
    flags = [(line[0] // mask) % 2 for mask in masks]
    maps = [(ahead_even[k], ahead_odd[k]) for k in range(SWEEPS)]
    given = [halves_of(third, k) for k in range(SWEEPS)]
    values = []
    for k in range(SWEEPS):
        pair = []
        for target, total in enumerate(moved_by(given, maps, k)):
            own = halves_of(ahead, k)[target]
            last = (total + own.astype(F32)).astype(BF16)
            upper = pick(flags[-2], last, halves_of(second, k)[target])
            pair.append(pick(flags[-1], upper, pick(flags[-2], own, jnp.zeros_like(own))))
        values.append(pair)
    for level in range(levels - 1, -1, -1):
        even, odd, offset = lower[3 * level : 3 * level + 3]
        maps = [(even[k], odd[k]) for k in range(SWEEPS)]
        moved = []
        for k in range(SWEEPS):
            pair = []
            for target, total in enumerate(moved_by(values, maps, k)):
                total = total + halves_of(offset, k)[target].astype(F32)
                pair.append(pick(flags[level], total.astype(BF16), values[k][target]))
            moved.append(pair)
        values = moved
    blank = jnp.zeros((values[0][0].shape[0], 2 * face), BF16)
    for k in range(SWEEPS):
        for pos in range(groups):
            tile = (pos % half) // 2
            both = values[k][pos // half][:, tile * 2 * face : (tile + 1) * 2 * face]
            inflows[k, pos] = by_half(both if pos % 2 == 0 else turned(both), blank)

    def sweep(k, carry):
        read_lags(me, states, lags, groups, count)

        def block(t):
            chosen = tuple(4 * t + i for i in range(4))
            run_chains(
                chosen, [inflows[k, pos] for pos in chosen], lags, weights, gains, states, count, face
            )

        over(groups // 4, block, 1)
        return carry

    lax.fori_loop(0, SWEEPS - 1, sweep, 0)
    read_lags(me, states, lags, groups, count)
    for t in range(groups // 4):
        chosen = tuple(4 * t + i for i in range(4))
        entries = [inflows[SWEEPS - 1, pos] for pos in chosen]
        outs = run_chains(chosen, entries, lags, weights, gains, states, count, face)
        for i, pos in enumerate(chosen):
            target = wanted[reversed_static(pos, groups)]
            traces = [entries[i]] + [o.astype(BF16) for o in outs[i][:-1]]
            for p in range(count):
                target[p] = lags[pos, p]
            target[count] = by_half(traces[0], traces[-1])
            for m in range(1, count // 2):
                target[count + m] = by_half(traces[2 * m - 1], traces[2 * m])


def final_kernel(place, order, inverse, coupling, given, *refs):
    wanted = refs[:-2]
    placed, gathered = refs[-2:]
    count, nodes, width = given.shape
    face = coupling.shape[1] // 3
    share = width // len(wanted)
    for rel, ref in enumerate(wanted):
        at = pl.multiple_of((place[0] ^ rel) * share, share)
        for m in range(ref.shape[0]):
            gathered[m, pl.ds(at, share), :] = ref[m].astype(F32)
    blank = jnp.zeros((face, nodes), BF16)
    for p in range(count):
        slot = order[p]
        rows = coupling[slot]
        second = p == count - 1 or (p > 0 and p % 2 == 0)
        tile = 0 if p == count - 1 else (p + 1) // 2
        pair = [blank, rows[:face]] if second else [rows[:face], blank]
        sides = jnp.concatenate([rows[2 * face :], rows[face : 2 * face]] + pair, axis=0)
        traces = jnp.concatenate([gathered[p], gathered[count + tile]], axis=1).astype(BF16)
        source = given[slot].astype(F32) + dot(traces, sides).T
        placed[slot] = dot(inverse[slot], source.astype(BF16)).astype(BF16)


def gather_list(value, axis):
    values = [value]
    for mask in bits_of(lax.axis_size(axis))[::-1]:
        values = values + [swap(v, axis, mask) for v in values]
    return values


def exchange(values, axis):
    return [v if rel == 0 else swap(v, axis, rel) for rel, v in enumerate(values)]


def call(kernel, outs, scratch, scalars, arrays, far=0, others=(), grant=0):
    def size(shape, kind):
        total = jnp.dtype(kind).itemsize
        for extent in shape:
            total *= extent
        return total

    held = sum(size(o.shape, o.dtype) for o in outs) + sum(size(a.shape, a.dtype) for a in arrays)
    held += sum(size(shape, kind) for shape, kind in scratch)
    return pl.pallas_call(
        kernel,
        out_shape=outs,
        in_specs=[SMEM] * len(scalars) + [VMEM] * (len(arrays) - far) + [HBM] * far,
        out_specs=[VMEM] * len(outs),
        scratch_shapes=[*others[:1], *[pltpu.VMEM(shape, kind) for shape, kind in scratch], *others[1:]],
        compiler_params=pltpu.CompilerParams(vmem_limit_bytes=grant or min(held + (6 << 20), 60 << 20)),
    )(*scalars, *arrays)


def shards(right_sides, inverse, coupling, sweep_order):
    given = right_sides[0, 0]
    inverse = inverse[0, 0]
    order = sweep_order[0, 0]
    count, nodes, width = given.shape
    face = coupling.shape[4]
    coupling = coupling[0, 0].reshape(count, 3 * face, nodes)
    groups = lax.axis_size("span")
    share = width // groups
    half = groups // 2
    place = lax.axis_index("span").astype(jnp.int32).reshape(1)
    line = lax.axis_index("stream").astype(jnp.int32).reshape(1)
    masks = bits_of(lax.axis_size("stream"))
    tiles = count + count // 2
    shape = jax.ShapeDtypeStruct
    maps, *gains = call(
        facemap_kernel,
        [shape((tiles * 3 * face, 2 * face), BF16)] + [shape((tiles, share, 2 * face), BF16)] * groups,
        [
            (inverse.shape, BF16),
            (coupling.shape, BF16),
            (given.shape, BF16),
            ((tiles, width, 2 * face), F32),
        ],
        [place],
        [pltpu.with_memory_space_constraint(a, pltpu.HBM) for a in (order, inverse, coupling, given)],
        4,
        (
            pltpu.SMEM(order.shape, order.dtype),
            pltpu.SemaphoreType.DMA,
            pltpu.SemaphoreType.DMA((3, count)),
        ),
    )
    all_maps = gather_list(maps, "span")
    gains = exchange(gains, "span")
    sizes = dict(groups=groups, count=count, face=face)
    wide = half * face
    response, weights = call(
        functools.partial(respond_kernel, **sizes),
        [
            shape((SWEEPS, wide, wide), BF16),
            shape((groups, count, 4 * face, 4 * face), BF16),
        ],
        [
            ((groups + 1, count, wide, 2 * face), BF16),
            ((groups, count, wide, 2 * face), BF16),
            ((2, groups, wide, 2 * face), BF16),
        ],
        [place],
        all_maps,
    )
    offset, gains = call(
        functools.partial(offset_kernel, **sizes),
        [
            shape((SWEEPS, 2 * share, wide), BF16),
            shape((groups, count, share, 4 * face), F32),
        ],
        [
            ((groups + 1, count, share, 2 * face), BF16),
            ((groups, count, share, 2 * face), BF16),
        ],
        [place],
        [weights, *gains],
    )
    levels = []
    for mask in masks[:-2]:
        got = swap(response, "stream", mask)
        other = swap(response, "span", 1)
        got_other = swap(got, "span", 1)
        got_offset = swap(offset, "stream", mask)
        levels += [got, got_other, got_offset]
        arrays = [response, other, got, got_other]
        (offset,) = call(
            functools.partial(pair_offset_kernel, mask=mask),
            [shape(offset.shape, BF16)],
            [],
            [line],
            arrays + [offset, got_offset],
        )
        (response,) = call(
            functools.partial(pair_map_kernel, mask=mask), [shape(response.shape, BF16)], [], [line], arrays
        )
    ahead = swap(offset, "stream", masks[-2])
    other = swap(response, "span", 1)
    ahead_even = swap(response, "stream", masks[-2])
    (joined,) = call(join_kernel, [shape(offset.shape, BF16)], [], [], [response, other, ahead, offset])
    second = lax.ppermute(joined, "stream", crossing(masks))
    third = swap(joined, "stream", masks[-1])
    ahead_odd = swap(ahead_even, "span", 1)
    wanted = call(
        functools.partial(resolve_kernel, masks=masks, **sizes),
        [shape((tiles, share, 2 * face), BF16)] * groups,
        [
            ((groups + 1, count, share, 2 * face), BF16),
            ((groups, count, share, 2 * face), BF16),
            ((SWEEPS, groups, share, 2 * face), BF16),
        ],
        [place, line],
        [weights, gains, ahead, second, third, ahead_even, ahead_odd, *levels],
    )
    wanted = exchange(wanted, "span")
    (placed,) = call(
        final_kernel,
        [shape((count, nodes, width), BF16)],
        [((tiles, width, 2 * face), F32)],
        [place, order],
        [inverse, coupling, given, *wanted],
    )
    return placed[None, None]


def solution(mesh):
    in_specs = (
        P("stream", "span", None, None, None),
        P("stream", "span", None, None, None),
        P("stream", "span", None, None, None, None),
        P("stream", "span", None),
    )
    out_specs = P("stream", "span", None, None, None)
    return jax.shard_map(shards, mesh=mesh, in_specs=in_specs, out_specs=out_specs, check_vma=False)
```

```python
import functools

import jax
import jax.numpy as jnp
from jax import lax
from jax.experimental import pallas as pl
from jax.experimental.pallas import tpu as pltpu
from jax.sharding import PartitionSpec as P

NP = 8
SWEEPS = 6
VMEM = pl.BlockSpec(memory_space=pltpu.VMEM)
SMEM = pl.BlockSpec(memory_space=pltpu.SMEM)
HBM = pl.BlockSpec(memory_space=pltpu.HBM)
F32 = jnp.float32
BF16 = jnp.bfloat16


def bits_of(count):
    return [1 << i for i in range(count.bit_length() - 1)]


def reversed_bits(value, count):
    bits = bits_of(count)
    total = 0
    for low, high in zip(bits, bits[::-1]):
        total = total + jnp.where((value & low) != 0, high, 0)
    return total


def reversed_static(value, count):
    bits = bits_of(count)
    return sum(high for low, high in zip(bits, bits[::-1]) if value & low)


def swap(value, axis, mask):
    count = lax.axis_size(axis)
    return lax.ppermute(value, axis, [(i, i ^ mask) for i in range(count)])


def crossing(masks):
    pairs = []
    for i in range(2 * masks[-1]):
        inner = bool(i & masks[-1]) != bool(i & masks[-2])
        pairs.append((i, i ^ (masks[-1] | masks[-2] if inner else 1)))
    return pairs


def dot(left, right):
    return jnp.dot(left, right, preferred_element_type=F32)


def dot_nt(left, right):
    return lax.dot_general(left, right, (((1,), (1,)), ((), ())), preferred_element_type=F32)


def by_half(low, high):
    lane = lax.broadcasted_iota(jnp.int32, low.shape, low.ndim - 1)
    return jnp.where(lane < low.shape[-1] // 2, low, high)


def turned(value):
    return pltpu.roll(value.astype(F32), value.shape[-1] // 2, 1).astype(value.dtype)


def face_rows_of(inverse, slot, face):
    nodes = inverse.shape[1]
    part = nodes // NP
    layer = part // NP
    lower = []
    upper = []
    for a in range(NP):
        head = inverse[slot, a * part : a * part + 2 * layer, :].astype(F32)
        tail = inverse[slot, (a + 1) * part - 2 * layer : (a + 1) * part, :].astype(F32)
        lower.append(head[:layer])
        upper.append(tail[layer:])
    faces = jnp.concatenate(lower + upper, axis=0).astype(BF16)
    outflow = inverse[slot, nodes - face :, :]
    return jnp.concatenate([faces, outflow, outflow], axis=0)


def pair_maps(maps, coupling, slots, rows, face):
    outs = []
    for i, slot in enumerate(slots):
        full = dot_nt(coupling[slot], rows[i])
        full = jnp.concatenate([full[2 * face :], full[face : 2 * face], full[:face]], axis=0).astype(BF16)
        maps[i * 3 * face : (i + 1) * 3 * face, :] = full[:, : 2 * face]
        outs.append(full[:, 2 * face :])
    maps[2 * 3 * face :, :] = by_half(outs[0], outs[1])


def first_kernel(order_far, inverse_far, coupling_far, given_far, maps, inverse, coupling, given, *refs):
    order, order_done, done = refs
    count = inverse.shape[0]
    face = coupling.shape[1] // 3
    first = pltpu.make_async_copy(order_far, order, order_done)
    first.start()
    pairs = ((inverse_far, inverse), (coupling_far, coupling), (given_far, given))

    def fetch(kind, slot):
        far, near = pairs[kind]
        return pltpu.make_async_copy(far.at[slot], near.at[slot], done.at[kind, slot])

    for kind in range(3):
        for slot in range(count):
            fetch(kind, slot).start()
    first.wait()
    for kind in range(2):
        for slot in range(count):
            fetch(kind, slot).wait()
    slots = [order[p] for p in range(2)]
    pair_maps(maps, coupling, slots, [face_rows_of(inverse, slot, face) for slot in slots], face)
    for slot in range(count):
        fetch(2, slot).wait()


def rest_kernel(place, order, inverse, coupling, given, *refs):
    count, _, width = given.shape
    maps = refs[: count // 2 - 1]
    gains = refs[count // 2 - 1 : -1]
    gathered = refs[-1]
    face = coupling.shape[1] // 3
    groups = len(gains)
    share = width // groups
    slots = [order[p] for p in range(count)]
    rows = [face_rows_of(inverse, slot, face) for slot in slots]
    for j, target in enumerate(maps):
        pair_maps(target, coupling, slots[2 * j + 2 : 2 * j + 4], rows[2 * j + 2 : 2 * j + 4], face)
    every = [dot(rows[p], given[slots[p]]).T for p in range(count)]
    tiles = [gain[:, : 2 * face] for gain in every]
    for p in range(0, count, 2):
        tiles.append(by_half(every[p][:, 2 * face :], every[p + 1][:, 2 * face :]))
    for m, tile in enumerate(tiles):
        gathered[m] = tile
    for rel in range(groups):
        at = pl.multiple_of((place[0] ^ rel) * share, share)
        for m in range(len(tiles)):
            gains[rel][m] = gathered[m, pl.ds(at, share), :].astype(BF16)


def unpack_maps(map_refs, weights, face):
    for j, refs in enumerate(map_refs):
        for pos, ref in enumerate(refs):
            outs = ref[2 * 3 * face :, :]
            other = turned(outs)
            for i in range(2):
                sides = ref[i * 3 * face : (i + 1) * 3 * face, :]
                full = jnp.concatenate([sides, by_half(outs, other) if i == 0 else by_half(other, outs)], axis=1)
                weights[pos, 2 * j + i, : 3 * face, :] = full
                weights[pos, 2 * j + i, 3 * face :, :] = full[2 * face :]


def unpack_gains(gain_refs, gains, count):
    for rel, ref in enumerate(gain_refs):
        for p in range(count):
            outs = ref[count + p // 2]
            other = turned(outs)
            outs = by_half(outs, other) if p % 2 == 0 else by_half(other, outs)
            gains[reversed_static(rel, len(gain_refs)), p] = jnp.concatenate([ref[p], outs], axis=1)


def neighbours(me, pos, groups):
    own = me ^ reversed_bits(pos, groups)
    below = jnp.where(own > 0, reversed_bits(((own - 1) & (groups - 1)) ^ me, groups), groups)
    above = jnp.where(own < groups - 1, reversed_bits(((own + 1) & (groups - 1)) ^ me, groups), groups)
    return below, above


def read_lags(me, states, lags, groups, count, first=0, live=None):
    def read(i):
        pos = first + i
        below, above = neighbours(me, pos, groups)
        for p in range(count):
            lags[pos, p] = by_half(states[above, p], states[below, p])

    over(live or groups, read)


def over(count, body, limit=4):
    if count <= limit:
        for i in range(count):
            body(i)
    else:

        def step(i, carry):
            body(i)
            return carry

        lax.fori_loop(0, count, step, 0)


def split_trace(out):
    high = out.astype(BF16)
    return by_half(high, (out - high.astype(F32)).astype(BF16)), high


def run_chains(chosen, entries, lags, weights, gains, states, count, face):
    outs = [[] for _ in chosen]
    for p in range(count):
        for i, pos in enumerate(chosen):
            result = dot(jnp.concatenate([lags[pos, p], entries[i]], axis=1), weights[pos, p])
            if gains is not None:
                result = result + gains[pos, p].astype(F32)
            states[pos, p] = result[:, : 2 * face].astype(BF16)
            outs[i].append(result[:, 2 * face :])
        if p < count - 1:
            entries = [split_trace(o[p])[0] for o in outs]
    return outs


def respond_kernel(place, *refs, groups, count, face):
    pairs = count // 2
    map_refs = [refs[j * groups : (j + 1) * groups] for j in range(pairs)]
    response, weights, states, lags, unit = refs[pairs * groups :]
    me = place[0]
    half = groups // 2
    unpack_maps(map_refs, weights, face)
    states[...] = jnp.zeros_like(states)
    unit[...] = jnp.zeros_like(unit)
    row = lax.broadcasted_iota(jnp.int32, unit.shape[2:], 0)
    lane = lax.broadcasted_iota(jnp.int32, unit.shape[2:], 1)
    for pos in range(half):
        hit = jnp.logical_and(lane < face, row == lane + pos * face)
        unit[0, pos] = jnp.where(hit, 1.0, 0.0).astype(BF16)

    def sweep(k, parity):
        read_lags(me, states, lags, groups, count, half * parity, half)

        def block(t):
            chosen = [2 * t + half * parity, 2 * t + 1 + half * parity]
            entries = [unit[jnp.minimum(k, 1), pos] for pos in chosen]
            ends = [outs[-1] for outs in run_chains(chosen, entries, lags, weights, None, states, count, face)]
            at = pl.ds(pl.multiple_of(t * 2 * face, 2 * face), 2 * face)
            response[k, :, at] = by_half(ends[0], ends[1]).astype(BF16)

        over(groups // 4, block, 1)

    def both(i, carry):
        sweep(2 * i, 0)
        sweep(2 * i + 1, 1)
        return carry

    lax.fori_loop(0, SWEEPS // 2, both, 0)


def offset_kernel(place, weights, *refs, groups, count, face):
    gain_refs = refs[:groups]
    offset, gains, states, lags = refs[groups:]
    me = place[0]
    half = groups // 2
    unpack_gains(gain_refs, gains, count)
    states[...] = jnp.zeros_like(states)
    share = gains.shape[2]
    blank = jnp.zeros((share, 2 * face), BF16)

    def sweep(k, carry):
        read_lags(me, states, lags, groups, count)

        def block(t):
            chosen = [2 * t, 2 * t + 1, 2 * t + half, 2 * t + 1 + half]
            outs = run_chains(chosen, [blank] * 4, lags, weights, gains, states, count, face)
            ends = [out[-1] for out in outs]
            at = pl.ds(pl.multiple_of(t * 2 * face, 2 * face), 2 * face)
            offset[k, :share, at] = by_half(ends[0], ends[1]).astype(BF16)
            offset[k, share:, at] = by_half(ends[2], ends[3]).astype(BF16)

        over(groups // 4, block, 1)
        return carry

    lax.fori_loop(0, SWEEPS, sweep, 0)


def pick(flag, first, second):
    return jnp.where(flag != 0, first, second)


def pair_offset_kernel(line, own, other, got, got_other, own_offset, got_offset, offset, *, mask):
    down = (line[0] // mask) % 2
    share = own_offset.shape[1] // 2
    maps = [
        (pick(down, own[k], got[k]), pick(down, other[k], got_other[k])) for k in range(SWEEPS)
    ]
    values = []
    for k in range(SWEEPS):
        both = zip(halves_of(got_offset, k), halves_of(own_offset, k))
        values.append([pick(down, a, b) for a, b in both])
    for k in range(SWEEPS):
        both = zip(halves_of(own_offset, k), halves_of(got_offset, k))
        added = [pick(down, a, b).astype(F32) for a, b in both]
        for target, total in enumerate(moved_by(values, maps, k)):
            offset[k, target * share : (target + 1) * share] = (total + added[target]).astype(BF16)


def pair_map_kernel(line, own, other, got, got_other, response, *, mask):
    down = (line[0] // mask) % 2
    after = [
        (pick(down, own[k], got[k]), pick(down, other[k], got_other[k])) for k in range(SWEEPS)
    ]
    before = [pick(down, got[k], own[k]) for k in range(SWEEPS)]
    for m in range(SWEEPS):
        stack = jnp.concatenate([after[d][(m + d) % 2] for d in range(m + 1)], axis=0)
        left = jnp.concatenate([before[m - d] for d in range(m + 1)], axis=1)
        response[m] = dot(left, stack).astype(BF16)


def halves_of(ref, k):
    share = ref.shape[1] // 2
    return ref[k, :share], ref[k, share:]


def moved_by(values, maps, k):
    pair = []
    for target in (0, 1):
        stack = jnp.concatenate([maps[d][(target + d) % 2] for d in range(k + 1)], axis=0)
        left = jnp.concatenate([values[k - d][(target + d) % 2] for d in range(k + 1)], axis=1)
        pair.append(dot(left, stack))
    return pair


def join_kernel(even, odd, entry, own, joined):
    maps = [(even[k], odd[k]) for k in range(SWEEPS)]
    values = [halves_of(entry, k) for k in range(SWEEPS)]
    share = own.shape[1] // 2
    for k in range(SWEEPS):
        added = halves_of(own, k)
        for target, total in enumerate(moved_by(values, maps, k)):
            total = total + added[target].astype(F32)
            joined[k, target * share : (target + 1) * share] = total.astype(BF16)


def resolve_kernel(place, line, *refs, groups, count, face, masks):
    weights, gains, ahead, second, third, ahead_even, ahead_odd = refs[:7]
    levels = len(masks) - 2
    lower = refs[7 : 7 + 3 * levels]
    wanted = refs[7 + 3 * levels : 7 + 3 * levels + groups]
    states, lags, inflows = refs[7 + 3 * levels + groups :]
    me = place[0]
    half = groups // 2
    states[...] = jnp.zeros_like(states)
    flags = [(line[0] // mask) % 2 for mask in masks]
    maps = [(ahead_even[k], ahead_odd[k]) for k in range(SWEEPS)]
    given = [halves_of(third, k) for k in range(SWEEPS)]
    values = []
    for k in range(SWEEPS):
        pair = []
        for target, total in enumerate(moved_by(given, maps, k)):
            own = halves_of(ahead, k)[target]
            last = (total + own.astype(F32)).astype(BF16)
            upper = pick(flags[-2], last, halves_of(second, k)[target])
            pair.append(pick(flags[-1], upper, pick(flags[-2], own, jnp.zeros_like(own))))
        values.append(pair)
    for level in range(levels - 1, -1, -1):
        even, odd, offset = lower[3 * level : 3 * level + 3]
        maps = [(even[k], odd[k]) for k in range(SWEEPS)]
        moved = []
        for k in range(SWEEPS):
            pair = []
            for target, total in enumerate(moved_by(values, maps, k)):
                total = total + halves_of(offset, k)[target].astype(F32)
                pair.append(pick(flags[level], total.astype(BF16), values[k][target]))
            moved.append(pair)
        values = moved
    blank = jnp.zeros((values[0][0].shape[0], 2 * face), BF16)
    for k in range(SWEEPS):
        for pos in range(groups):
            tile = (pos % half) // 2
            both = values[k][pos // half][:, tile * 2 * face : (tile + 1) * 2 * face]
            inflows[k, pos] = by_half(both if pos % 2 == 0 else turned(both), blank)

    def sweep(k, carry):
        read_lags(me, states, lags, groups, count)

        def block(t):
            chosen = tuple(4 * t + i for i in range(4))
            run_chains(
                chosen, [inflows[k, pos] for pos in chosen], lags, weights, gains, states, count, face
            )

        over(groups // 4, block, 1)
        return carry

    lax.fori_loop(0, SWEEPS - 1, sweep, 0)
    read_lags(me, states, lags, groups, count)
    for t in range(groups // 4):
        chosen = tuple(4 * t + i for i in range(4))
        entries = [inflows[SWEEPS - 1, pos] for pos in chosen]
        outs = run_chains(chosen, entries, lags, weights, gains, states, count, face)
        for i, pos in enumerate(chosen):
            target = wanted[reversed_static(pos, groups)]
            traces = [entries[i]] + [o.astype(BF16) for o in outs[i][:-1]]
            for p in range(count):
                target[p] = lags[pos, p]
            target[count] = by_half(traces[0], traces[-1])
            for m in range(1, count // 2):
                target[count + m] = by_half(traces[2 * m - 1], traces[2 * m])


def final_kernel(place, order, inverse, coupling, given, *refs):
    wanted = refs[:-2]
    placed, gathered = refs[-2:]
    count, nodes, width = given.shape
    face = coupling.shape[1] // 3
    share = width // len(wanted)
    for rel, ref in enumerate(wanted):
        at = pl.multiple_of((place[0] ^ rel) * share, share)
        for m in range(ref.shape[0]):
            gathered[m, pl.ds(at, share), :] = ref[m].astype(F32)
    blank = jnp.zeros((face, nodes), BF16)
    for p in range(count):
        slot = order[p]
        rows = coupling[slot]
        second = p == count - 1 or (p > 0 and p % 2 == 0)
        tile = 0 if p == count - 1 else (p + 1) // 2
        pair = [blank, rows[:face]] if second else [rows[:face], blank]
        sides = jnp.concatenate([rows[2 * face :], rows[face : 2 * face]] + pair, axis=0)
        traces = jnp.concatenate([gathered[p], gathered[count + tile]], axis=1).astype(BF16)
        source = given[slot].astype(F32) + dot(traces, sides).T
        placed[slot] = dot(inverse[slot], source.astype(BF16)).astype(BF16)


def gather_list(value, axis):
    values = [value]
    for mask in bits_of(lax.axis_size(axis))[::-1]:
        values = values + [swap(v, axis, mask) for v in values]
    return values


def exchange(values, axis):
    return [v if rel == 0 else swap(v, axis, rel) for rel, v in enumerate(values)]


def call(kernel, outs, scratch, scalars, arrays, far=0, others=(), grant=0):
    def size(shape, kind):
        total = jnp.dtype(kind).itemsize
        for extent in shape:
            total *= extent
        return total

    held = sum(size(o.shape, o.dtype) for o in outs) + sum(size(a.shape, a.dtype) for a in arrays)
    held += sum(size(shape, kind) for shape, kind in scratch)
    return pl.pallas_call(
        kernel,
        out_shape=outs,
        in_specs=[SMEM] * len(scalars) + [VMEM] * (len(arrays) - far) + [HBM] * far,
        out_specs=[VMEM] * len(outs),
        scratch_shapes=[*others[:1], *[pltpu.VMEM(shape, kind) for shape, kind in scratch], *others[1:]],
        compiler_params=pltpu.CompilerParams(vmem_limit_bytes=grant or min(held + (3 << 20), 60 << 20)),
    )(*scalars, *arrays)


def shards(right_sides, inverse, coupling, sweep_order):
    given = right_sides[0, 0]
    inverse = inverse[0, 0]
    order = sweep_order[0, 0]
    count, nodes, width = given.shape
    face = coupling.shape[4]
    coupling = coupling[0, 0].reshape(count, 3 * face, nodes)
    groups = lax.axis_size("span")
    share = width // groups
    half = groups // 2
    place = lax.axis_index("span").astype(jnp.int32).reshape(1)
    line = lax.axis_index("stream").astype(jnp.int32).reshape(1)
    masks = bits_of(lax.axis_size("stream"))
    tiles = count + count // 2
    shape = jax.ShapeDtypeStruct
    far = [pltpu.with_memory_space_constraint(a, pltpu.HBM) for a in (order, inverse, coupling, given)]
    maps, *near = call(
        first_kernel,
        [
            shape((3 * 3 * face, 2 * face), BF16),
            shape(inverse.shape, BF16),
            shape(coupling.shape, BF16),
            shape(given.shape, BF16),
        ],
        [],
        [],
        far,
        4,
        (
            pltpu.SMEM(order.shape, order.dtype),
            pltpu.SemaphoreType.DMA,
            pltpu.SemaphoreType.DMA((3, count)),
        ),
    )
    all_maps = gather_list(maps, "span")
    outs = call(
        rest_kernel,
        [shape(maps.shape, BF16)] * (count // 2 - 1) + [shape((tiles, share, 2 * face), BF16)] * groups,
        [((tiles, width, 2 * face), F32)],
        [place, far[0]],
        near,
    )
    gains = outs[count // 2 - 1 :]
    for maps in outs[: count // 2 - 1]:
        all_maps += gather_list(maps, "span")
    gains = exchange(gains, "span")
    sizes = dict(groups=groups, count=count, face=face)
    wide = half * face
    response, weights = call(
        functools.partial(respond_kernel, **sizes),
        [
            shape((SWEEPS, wide, wide), BF16),
            shape((groups, count, 4 * face, 4 * face), BF16),
        ],
        [
            ((groups + 1, count, wide, 2 * face), BF16),
            ((groups, count, wide, 2 * face), BF16),
            ((2, groups, wide, 2 * face), BF16),
        ],
        [place],
        all_maps,
    )
    offset, gains = call(
        functools.partial(offset_kernel, **sizes),
        [
            shape((SWEEPS, 2 * share, wide), BF16),
            shape((groups, count, share, 4 * face), BF16),
        ],
        [
            ((groups + 1, count, share, 2 * face), BF16),
            ((groups, count, share, 2 * face), BF16),
        ],
        [place],
        [weights, *gains],
    )
    levels = []
    for mask in masks[:-2]:
        got = swap(response, "stream", mask)
        other = swap(response, "span", 1)
        got_other = swap(got, "span", 1)
        got_offset = swap(offset, "stream", mask)
        levels += [got, got_other, got_offset]
        arrays = [response, other, got, got_other]
        (offset,) = call(
            functools.partial(pair_offset_kernel, mask=mask),
            [shape(offset.shape, BF16)],
            [],
            [line],
            arrays + [offset, got_offset],
        )
        (response,) = call(
            functools.partial(pair_map_kernel, mask=mask), [shape(response.shape, BF16)], [], [line], arrays
        )
    ahead = swap(offset, "stream", masks[-2])
    other = swap(response, "span", 1)
    ahead_even = swap(response, "stream", masks[-2])
    (joined,) = call(join_kernel, [shape(offset.shape, BF16)], [], [], [response, other, ahead, offset])
    second = lax.ppermute(joined, "stream", crossing(masks))
    third = swap(joined, "stream", masks[-1])
    ahead_odd = swap(ahead_even, "span", 1)
    wanted = call(
        functools.partial(resolve_kernel, masks=masks, **sizes),
        [shape((tiles, share, 2 * face), BF16)] * groups,
        [
            ((groups + 1, count, share, 2 * face), BF16),
            ((groups, count, share, 2 * face), BF16),
            ((SWEEPS, groups, share, 2 * face), BF16),
        ],
        [place, line],
        [weights, gains, ahead, second, third, ahead_even, ahead_odd, *levels],
    )
    wanted = exchange(wanted, "span")
    (placed,) = call(
        final_kernel,
        [shape((count, nodes, width), BF16)],
        [((tiles, width, 2 * face), F32)],
        [place, order],
        [inverse, coupling, given, *wanted],
    )
    return placed[None, None]


def solution(mesh):
    in_specs = (
        P("stream", "span", None, None, None),
        P("stream", "span", None, None, None),
        P("stream", "span", None, None, None, None),
        P("stream", "span", None),
    )
    out_specs = P("stream", "span", None, None, None)
    return jax.shard_map(shards, mesh=mesh, in_specs=in_specs, out_specs=out_specs, check_vma=False)
```

```python
import functools

import jax
import jax.numpy as jnp
from jax import lax
from jax.experimental import pallas as pl
from jax.experimental.pallas import tpu as pltpu
from jax.sharding import PartitionSpec as P

NP = 8
SWEEPS = 6
VMEM = pl.BlockSpec(memory_space=pltpu.VMEM)
SMEM = pl.BlockSpec(memory_space=pltpu.SMEM)
HBM = pl.BlockSpec(memory_space=pltpu.HBM)
F32 = jnp.float32
BF16 = jnp.bfloat16


def bits_of(count):
    return [1 << i for i in range(count.bit_length() - 1)]


def reversed_bits(value, count):
    bits = bits_of(count)
    total = 0
    for low, high in zip(bits, bits[::-1]):
        total = total + jnp.where((value & low) != 0, high, 0)
    return total


def reversed_static(value, count):
    bits = bits_of(count)
    return sum(high for low, high in zip(bits, bits[::-1]) if value & low)


def swap(value, axis, mask):
    count = lax.axis_size(axis)
    return lax.ppermute(value, axis, [(i, i ^ mask) for i in range(count)])


def crossing(masks):
    pairs = []
    for i in range(2 * masks[-1]):
        inner = bool(i & masks[-1]) != bool(i & masks[-2])
        pairs.append((i, i ^ (masks[-1] | masks[-2] if inner else 1)))
    return pairs


def dot(left, right):
    return jnp.dot(left, right, preferred_element_type=F32)


def dot_nt(left, right):
    return lax.dot_general(left, right, (((1,), (1,)), ((), ())), preferred_element_type=F32)


def by_half(low, high):
    lane = lax.broadcasted_iota(jnp.int32, low.shape, low.ndim - 1)
    return jnp.where(lane < low.shape[-1] // 2, low, high)


def turned(value):
    return pltpu.roll(value.astype(F32), value.shape[-1] // 2, 1).astype(value.dtype)


def face_rows_of(inverse, slot, face):
    nodes = inverse.shape[1]
    part = nodes // NP
    layer = part // NP
    lower = []
    upper = []
    for a in range(NP):
        head = inverse[slot, a * part : a * part + 2 * layer, :].astype(F32)
        tail = inverse[slot, (a + 1) * part - 2 * layer : (a + 1) * part, :].astype(F32)
        lower.append(head[:layer])
        upper.append(tail[layer:])
    faces = jnp.concatenate(lower + upper, axis=0).astype(BF16)
    outflow = inverse[slot, nodes - face :, :]
    return jnp.concatenate([faces, outflow, outflow], axis=0)


def pair_maps(maps, coupling, slots, rows, face):
    outs = []
    for i, slot in enumerate(slots):
        full = dot_nt(coupling[slot], rows[i])
        full = jnp.concatenate([full[2 * face :], full[face : 2 * face], full[:face]], axis=0).astype(BF16)
        maps[i * 3 * face : (i + 1) * 3 * face, :] = full[:, : 2 * face]
        outs.append(full[:, 2 * face :])
    maps[2 * 3 * face :, :] = by_half(outs[0], outs[1])


def first_kernel(order_far, inverse_far, coupling_far, given_far, *refs):
    maps, rows, inverse_near, coupling_near, given_near = refs[:5]
    inverse, coupling, order, order_done, done, near_done = refs[5:]
    count = inverse.shape[0]
    face = coupling.shape[1] // 3
    first = pltpu.make_async_copy(order_far, order, order_done)
    first.start()
    pairs = ((inverse_far, inverse), (coupling_far, coupling))

    def fetch(kind, slot):
        far, near = pairs[kind]
        return pltpu.make_async_copy(far.at[slot], near.at[slot], done.at[kind, slot])

    for kind in range(2):
        for slot in range(count):
            fetch(kind, slot).start()
    first.wait()
    slots = [order[p] for p in range(count)]
    later = [
        pltpu.make_async_copy(given_far.at[slots[p]], given_near.at[p], near_done.at[0, p]) for p in range(count)
    ]
    for p in range(2, count):
        later.append(
            pltpu.make_async_copy(inverse_far.at[slots[p]], inverse_near.at[p - 2], near_done.at[1, p])
        )
        later.append(
            pltpu.make_async_copy(coupling_far.at[slots[p]], coupling_near.at[p - 2], near_done.at[2, p])
        )
    for copy in later:
        copy.start()
    for kind in range(2):
        for slot in range(count):
            fetch(kind, slot).wait()
    values = []
    for p in range(2):
        values.append(face_rows_of(inverse, slots[p], face))
        rows[p] = values[p]
    pair_maps(maps, coupling, slots[:2], values, face)
    for copy in later:
        copy.wait()


def rest_kernel(place, early_rows, inverse, coupling, given, *refs):
    count, _, width = given.shape
    maps = refs[: count // 2 - 1]
    gains = refs[count // 2 - 1 : -1]
    gathered = refs[-1]
    face = coupling.shape[1] // 3
    groups = len(gains)
    share = width // groups
    rows = [face_rows_of(inverse, p, face) for p in range(count - 2)]
    for j, target in enumerate(maps):
        pair_maps(target, coupling, (2 * j, 2 * j + 1), rows[2 * j : 2 * j + 2], face)
    rows = [early_rows[0], early_rows[1]] + rows
    every = [dot(rows[p], given[p]).T for p in range(count)]
    tiles = [gain[:, : 2 * face] for gain in every]
    for p in range(0, count, 2):
        tiles.append(by_half(every[p][:, 2 * face :], every[p + 1][:, 2 * face :]))
    for m, tile in enumerate(tiles):
        gathered[m] = tile
    for rel in range(groups):
        at = pl.multiple_of((place[0] ^ rel) * share, share)
        for m in range(len(tiles)):
            gains[rel][m] = gathered[m, pl.ds(at, share), :].astype(BF16)


def unpack_maps(map_refs, weights, face):
    for j, refs in enumerate(map_refs):
        for pos, ref in enumerate(refs):
            outs = ref[2 * 3 * face :, :]
            other = turned(outs)
            for i in range(2):
                sides = ref[i * 3 * face : (i + 1) * 3 * face, :]
                full = jnp.concatenate([sides, by_half(outs, other) if i == 0 else by_half(other, outs)], axis=1)
                weights[pos, 2 * j + i, : 3 * face, :] = full
                weights[pos, 2 * j + i, 3 * face :, :] = full[2 * face :]


def unpack_gains(gain_refs, gains, count):
    for rel, ref in enumerate(gain_refs):
        for p in range(count):
            outs = ref[count + p // 2]
            other = turned(outs)
            outs = by_half(outs, other) if p % 2 == 0 else by_half(other, outs)
            gains[reversed_static(rel, len(gain_refs)), p] = jnp.concatenate([ref[p], outs], axis=1)


def neighbours(me, pos, groups):
    own = me ^ reversed_bits(pos, groups)
    below = jnp.where(own > 0, reversed_bits(((own - 1) & (groups - 1)) ^ me, groups), groups)
    above = jnp.where(own < groups - 1, reversed_bits(((own + 1) & (groups - 1)) ^ me, groups), groups)
    return below, above


def read_lags(me, states, lags, groups, count):
    def read(pos):
        below, above = neighbours(me, pos, groups)
        for p in range(count):
            lags[pos, p] = by_half(states[above, p], states[below, p])

    over(groups, read)


def over(count, body, limit=4):
    if count <= limit:
        for i in range(count):
            body(i)
    else:

        def step(i, carry):
            body(i)
            return carry

        lax.fori_loop(0, count, step, 0)


def split_trace(out):
    high = out.astype(BF16)
    return by_half(high, (out - high.astype(F32)).astype(BF16)), high


def run_chains(chosen, entries, lags, weights, gains, states, count, face):
    share = gains.shape[2]
    outs = [[] for _ in chosen]
    for p in range(count):
        for i, pos in enumerate(chosen):
            rows = entries[i].shape[0]
            result = dot(jnp.concatenate([lags[pos, p, :rows], entries[i]], axis=1), weights[pos, p])
            first = result[:share] + gains[pos, p].astype(F32)
            result = first if rows == share else jnp.concatenate([first, result[share:]], axis=0)
            states[pos, p, :rows] = result[:, : 2 * face].astype(BF16)
            outs[i].append(result[:, 2 * face :])
        if p < count - 1:
            entries = [split_trace(o[p])[0] for o in outs]
    return outs


def respond_kernel(place, *refs, groups, count, face):
    pairs = count // 2
    map_refs = [refs[j * groups : (j + 1) * groups] for j in range(pairs)]
    gain_refs = refs[pairs * groups : (pairs + 1) * groups]
    response, offset, weights, gains, states, lags, unit = refs[(pairs + 1) * groups :]
    me = place[0]
    half = groups // 2
    share = gains.shape[2]
    unpack_maps(map_refs, weights, face)
    unpack_gains(gain_refs, gains, count)
    states[...] = jnp.zeros_like(states)
    unit[...] = jnp.zeros_like(unit)
    row = lax.broadcasted_iota(jnp.int32, unit.shape[2:], 0) - share
    lane = lax.broadcasted_iota(jnp.int32, unit.shape[2:], 1)
    for pos in range(half):
        hit = jnp.logical_and(lane < face, row == lane + pos * face)
        unit[0, pos] = jnp.where(hit, 1.0, 0.0).astype(BF16)

    def sweep(k, parity):
        read_lags(me, states, lags, groups, count)

        def block(t):
            live = [2 * t + half * parity, 2 * t + 1 + half * parity]
            bare = [2 * t + half * (1 - parity), 2 * t + 1 + half * (1 - parity)]
            entries = [unit[jnp.minimum(k, 1), pos] for pos in live]
            entries += [jnp.zeros((share, 2 * face), BF16)] * 2
            chains = run_chains(live + bare, entries, lags, weights, gains, states, count, face)
            ends = [outs[-1] for outs in chains]
            at = pl.ds(pl.multiple_of(t * 2 * face, 2 * face), 2 * face)
            full = by_half(ends[0], ends[1])
            response[k, :, at] = full[share:].astype(BF16)
            for target, tile in ((parity, full[:share]), (1 - parity, by_half(ends[2], ends[3]))):
                offset[k, target * share : (target + 1) * share, at] = tile.astype(BF16)

        over(groups // 4, block, 1)

    def both(i, carry):
        sweep(2 * i, 0)
        sweep(2 * i + 1, 1)
        return carry

    lax.fori_loop(0, SWEEPS // 2, both, 0)


def pick(flag, first, second):
    return jnp.where(flag != 0, first, second)


def pair_offset_kernel(line, own, other, got, got_other, own_offset, got_offset, offset, *, mask):
    down = (line[0] // mask) % 2
    share = own_offset.shape[1] // 2
    maps = [
        (pick(down, own[k], got[k]), pick(down, other[k], got_other[k])) for k in range(SWEEPS)
    ]
    values = []
    for k in range(SWEEPS):
        both = zip(halves_of(got_offset, k), halves_of(own_offset, k))
        values.append([pick(down, a, b) for a, b in both])
    for k in range(SWEEPS):
        both = zip(halves_of(own_offset, k), halves_of(got_offset, k))
        added = [pick(down, a, b).astype(F32) for a, b in both]
        for target, total in enumerate(moved_by(values, maps, k)):
            offset[k, target * share : (target + 1) * share] = (total + added[target]).astype(BF16)


def pair_map_kernel(line, own, other, got, got_other, response, *, mask):
    down = (line[0] // mask) % 2
    after = [
        (pick(down, own[k], got[k]), pick(down, other[k], got_other[k])) for k in range(SWEEPS)
    ]
    before = [pick(down, got[k], own[k]) for k in range(SWEEPS)]
    for m in range(SWEEPS):
        stack = jnp.concatenate([after[d][(m + d) % 2] for d in range(m + 1)], axis=0)
        left = jnp.concatenate([before[m - d] for d in range(m + 1)], axis=1)
        response[m] = dot(left, stack).astype(BF16)


def halves_of(ref, k):
    share = ref.shape[1] // 2
    return ref[k, :share], ref[k, share:]


def moved_by(values, maps, k):
    pair = []
    for target in (0, 1):
        stack = jnp.concatenate([maps[d][(target + d) % 2] for d in range(k + 1)], axis=0)
        left = jnp.concatenate([values[k - d][(target + d) % 2] for d in range(k + 1)], axis=1)
        pair.append(dot(left, stack))
    return pair


def add_own(values, maps, own):
    moved = []
    for k in range(SWEEPS):
        pair = zip(moved_by(values, maps, k), own[k])
        moved.append([(total + added.astype(F32)).astype(BF16) for total, added in pair])
    return moved


def put_halves(ref, values):
    share = ref.shape[1] // 2
    for k in range(SWEEPS):
        for target in (0, 1):
            ref[k, target * share : (target + 1) * share] = values[k][target]


def opening_kernel(even, odd, entry, own, opened):
    maps = [(even[k], odd[k]) for k in range(SWEEPS)]
    values = [halves_of(entry, k) for k in range(SWEEPS)]
    put_halves(opened, add_own(values, maps, [halves_of(own, k) for k in range(SWEEPS)]))


def join_kernel(line, own, other, got, got_other, own_offset, got_offset, near, across, joined, *, mask):
    down = (line[0] // mask) % 2
    values = [
        [pick(down, a, b) for a, b in zip(halves_of(near, k), halves_of(across, k))] for k in range(SWEEPS)
    ]
    for turn in (down, 1 - down):
        maps = [(pick(turn, got[k], own[k]), pick(turn, got_other[k], other[k])) for k in range(SWEEPS)]
        added = [
            [pick(turn, a, b) for a, b in zip(halves_of(got_offset, k), halves_of(own_offset, k))]
            for k in range(SWEEPS)
        ]
        values = add_own(values, maps, added)
    put_halves(joined, values)


def resolve_kernel(place, line, *refs, groups, count, face, masks):
    weights, gains, near, across, second, third, ahead_even, ahead_odd = refs[:8]
    levels = len(masks) - 2
    lower = refs[8 : 8 + 3 * levels]
    wanted = refs[8 + 3 * levels : 8 + 3 * levels + groups]
    states, lags, inflows = refs[8 + 3 * levels + groups :]
    me = place[0]
    half = groups // 2
    states[...] = jnp.zeros_like(states)
    flags = [(line[0] // mask) % 2 for mask in masks]
    maps = [(ahead_even[k], ahead_odd[k]) for k in range(SWEEPS)]
    given = [halves_of(third, k) for k in range(SWEEPS)]
    values = []
    for k in range(SWEEPS):
        pair = []
        for target, total in enumerate(moved_by(given, maps, k)):
            own = pick(flags[-3], halves_of(near, k)[target], halves_of(across, k)[target])
            last = (total + own.astype(F32)).astype(BF16)
            upper = pick(flags[-2], last, halves_of(second, k)[target])
            pair.append(pick(flags[-1], upper, pick(flags[-2], own, jnp.zeros_like(own))))
        values.append(pair)
    for level in range(levels - 1, -1, -1):
        even, odd, offset = lower[3 * level : 3 * level + 3]
        maps = [(even[k], odd[k]) for k in range(SWEEPS)]
        moved = []
        for k in range(SWEEPS):
            pair = []
            for target, total in enumerate(moved_by(values, maps, k)):
                total = total + halves_of(offset, k)[target].astype(F32)
                pair.append(pick(flags[level], total.astype(BF16), values[k][target]))
            moved.append(pair)
        values = moved
    blank = jnp.zeros((values[0][0].shape[0], 2 * face), BF16)
    for k in range(SWEEPS):
        for pos in range(groups):
            tile = (pos % half) // 2
            both = values[k][pos // half][:, tile * 2 * face : (tile + 1) * 2 * face]
            inflows[k, pos] = by_half(both if pos % 2 == 0 else turned(both), blank)

    def sweep(k, carry):
        read_lags(me, states, lags, groups, count)

        def block(t):
            chosen = tuple(4 * t + i for i in range(4))
            run_chains(
                chosen, [inflows[k, pos] for pos in chosen], lags, weights, gains, states, count, face
            )

        over(groups // 4, block, 1)
        return carry

    lax.fori_loop(0, SWEEPS - 1, sweep, 0)
    read_lags(me, states, lags, groups, count)
    for t in range(groups // 4):
        chosen = tuple(4 * t + i for i in range(4))
        entries = [inflows[SWEEPS - 1, pos] for pos in chosen]
        outs = run_chains(chosen, entries, lags, weights, gains, states, count, face)
        for i, pos in enumerate(chosen):
            target = wanted[reversed_static(pos, groups)]
            traces = [entries[i]] + [o.astype(BF16) for o in outs[i][:-1]]
            for p in range(count):
                target[p] = lags[pos, p]
            target[count] = by_half(traces[0], traces[-1])
            for m in range(1, count // 2):
                target[count + m] = by_half(traces[2 * m - 1], traces[2 * m])


def final_kernel(place, order, inverse, coupling, given, *refs):
    wanted = refs[:-2]
    placed, gathered = refs[-2:]
    count, nodes, width = given.shape
    face = coupling.shape[1] // 3
    share = width // len(wanted)
    for rel, ref in enumerate(wanted):
        at = pl.multiple_of((place[0] ^ rel) * share, share)
        for m in range(ref.shape[0]):
            gathered[m, pl.ds(at, share), :] = ref[m].astype(F32)
    blank = jnp.zeros((face, nodes), BF16)
    for p in range(count):
        slot = order[p]
        rows = coupling[slot]
        second = p == count - 1 or (p > 0 and p % 2 == 0)
        tile = 0 if p == count - 1 else (p + 1) // 2
        pair = [blank, rows[:face]] if second else [rows[:face], blank]
        sides = jnp.concatenate([rows[2 * face :], rows[face : 2 * face]] + pair, axis=0)
        traces = jnp.concatenate([gathered[p], gathered[count + tile]], axis=1).astype(BF16)
        source = given[slot].astype(F32) + dot(traces, sides).T
        placed[slot] = dot(inverse[slot], source.astype(BF16)).astype(BF16)


def gather_list(value, axis):
    values = [value]
    for mask in bits_of(lax.axis_size(axis))[::-1]:
        values = values + [swap(v, axis, mask) for v in values]
    return values


def exchange(values, axis):
    return [v if rel == 0 else swap(v, axis, rel) for rel, v in enumerate(values)]


def call(kernel, outs, scratch, scalars, arrays, far=0, others=(), grant=0):
    def size(shape, kind):
        total = jnp.dtype(kind).itemsize
        for extent in shape:
            total *= extent
        return total

    held = sum(size(o.shape, o.dtype) for o in outs) + sum(size(a.shape, a.dtype) for a in arrays)
    held += sum(size(shape, kind) for shape, kind in scratch)
    return pl.pallas_call(
        kernel,
        out_shape=outs,
        in_specs=[SMEM] * len(scalars) + [VMEM] * (len(arrays) - far) + [HBM] * far,
        out_specs=[VMEM] * len(outs),
        scratch_shapes=[*[pltpu.VMEM(shape, kind) for shape, kind in scratch], *others],
        compiler_params=pltpu.CompilerParams(vmem_limit_bytes=grant or min(held + (3 << 20), 60 << 20)),
    )(*scalars, *arrays)


def shards(right_sides, inverse, coupling, sweep_order):
    given = right_sides[0, 0]
    inverse = inverse[0, 0]
    order = sweep_order[0, 0]
    count, nodes, width = given.shape
    face = coupling.shape[4]
    coupling = coupling[0, 0].reshape(count, 3 * face, nodes)
    groups = lax.axis_size("span")
    share = width // groups
    half = groups // 2
    place = lax.axis_index("span").astype(jnp.int32).reshape(1)
    line = lax.axis_index("stream").astype(jnp.int32).reshape(1)
    masks = bits_of(lax.axis_size("stream"))
    tiles = count + count // 2
    shape = jax.ShapeDtypeStruct
    far = [pltpu.with_memory_space_constraint(a, pltpu.HBM) for a in (order, inverse, coupling, given)]
    maps, *near = call(
        first_kernel,
        [
            shape((3 * 3 * face, 2 * face), BF16),
            shape((2, 4 * face, nodes), BF16),
            shape((count - 2,) + inverse.shape[1:], BF16),
            shape((count - 2,) + coupling.shape[1:], BF16),
            shape(given.shape, BF16),
        ],
        [(inverse.shape, BF16), (coupling.shape, BF16)],
        [],
        far,
        4,
        (
            pltpu.SMEM(order.shape, order.dtype),
            pltpu.SemaphoreType.DMA,
            pltpu.SemaphoreType.DMA((2, count)),
            pltpu.SemaphoreType.DMA((3, count)),
        ),
    )
    all_maps = gather_list(maps, "span")
    outs = call(
        rest_kernel,
        [shape(maps.shape, BF16)] * (count // 2 - 1) + [shape((tiles, share, 2 * face), BF16)] * groups,
        [((tiles, width, 2 * face), F32)],
        [place],
        near,
    )
    gains = outs[count // 2 - 1 :]
    for maps in outs[: count // 2 - 1]:
        all_maps += gather_list(maps, "span")
    gains = exchange(gains, "span")
    sizes = dict(groups=groups, count=count, face=face)
    wide = half * face
    response, offset, weights, gains = call(
        functools.partial(respond_kernel, **sizes),
        [
            shape((SWEEPS, wide, wide), BF16),
            shape((SWEEPS, 2 * share, wide), BF16),
            shape((groups, count, 4 * face, 4 * face), BF16),
            shape((groups, count, share, 4 * face), BF16),
        ],
        [
            ((groups + 1, count, share + wide, 2 * face), BF16),
            ((groups, count, share + wide, 2 * face), BF16),
            ((2, groups, share + wide, 2 * face), BF16),
        ],
        [place],
        [*all_maps, *gains],
    )
    levels = []
    for mask in masks[:-2]:
        got_offset = swap(offset, "stream", mask)
        other = swap(response, "span", 1)
        got = swap(response, "stream", mask)
        got_other = swap(got, "span", 1)
        levels += [got, got_other, got_offset]
        arrays = [response, other, got, got_other]
        same = shape(offset.shape, BF16)
        if mask == masks[-3]:
            (opened,) = call(opening_kernel, [same], [], [], [response, other, got_offset, offset])
            near = swap(opened, "stream", masks[-2])
            across = swap(opened, "stream", masks[-2] | mask)
            joining = arrays + [offset, got_offset, near, across]
        else:
            (offset,) = call(
                functools.partial(pair_offset_kernel, mask=mask), [same], [], [line], arrays + [offset, got_offset]
            )
        (response,) = call(
            functools.partial(pair_map_kernel, mask=mask), [shape(response.shape, BF16)], [], [line], arrays
        )
    ahead_even = swap(response, "stream", masks[-2])
    (joined,) = call(functools.partial(join_kernel, mask=masks[-3]), [same], [], [line], joining)
    second = lax.ppermute(joined, "stream", crossing(masks))
    third = swap(joined, "stream", masks[-1])
    ahead_odd = swap(ahead_even, "span", 1)
    wanted = call(
        functools.partial(resolve_kernel, masks=masks, **sizes),
        [shape((tiles, share, 2 * face), BF16)] * groups,
        [
            ((groups + 1, count, share, 2 * face), BF16),
            ((groups, count, share, 2 * face), BF16),
            ((SWEEPS, groups, share, 2 * face), BF16),
        ],
        [place, line],
        [weights, gains, near, across, second, third, ahead_even, ahead_odd, *levels],
    )
    wanted = exchange(wanted, "span")
    (placed,) = call(
        final_kernel,
        [shape((count, nodes, width), BF16)],
        [((tiles, width, 2 * face), F32)],
        [place, order],
        [inverse, coupling, given, *wanted],
    )
    return placed[None, None]


def solution(mesh):
    in_specs = (
        P("stream", "span", None, None, None),
        P("stream", "span", None, None, None),
        P("stream", "span", None, None, None, None),
        P("stream", "span", None),
    )
    out_specs = P("stream", "span", None, None, None)
    return jax.shard_map(shards, mesh=mesh, in_specs=in_specs, out_specs=out_specs, check_vma=False)
```

```python
import functools

import jax
import jax.numpy as jnp
from jax import lax
from jax.experimental import pallas as pl
from jax.experimental.pallas import tpu as pltpu
from jax.sharding import PartitionSpec as P

NP = 8
SWEEPS = 6
VMEM = pl.BlockSpec(memory_space=pltpu.VMEM)
SMEM = pl.BlockSpec(memory_space=pltpu.SMEM)
HBM = pl.BlockSpec(memory_space=pltpu.HBM)
F32 = jnp.float32
BF16 = jnp.bfloat16


def bits_of(count):
    return [1 << i for i in range(count.bit_length() - 1)]


def reversed_bits(value, count):
    bits = bits_of(count)
    total = 0
    for low, high in zip(bits, bits[::-1]):
        total = total + jnp.where((value & low) != 0, high, 0)
    return total


def reversed_static(value, count):
    bits = bits_of(count)
    return sum(high for low, high in zip(bits, bits[::-1]) if value & low)


def swap(value, axis, mask):
    count = lax.axis_size(axis)
    return lax.ppermute(value, axis, [(i, i ^ mask) for i in range(count)])


def crossing(masks):
    pairs = []
    for i in range(2 * masks[-1]):
        inner = bool(i & masks[-1]) != bool(i & masks[-2])
        pairs.append((i, i ^ (masks[-1] | masks[-2] if inner else 1)))
    return pairs


def dot(left, right):
    return jnp.dot(left, right, preferred_element_type=F32)


def dot_nt(left, right):
    return lax.dot_general(left, right, (((1,), (1,)), ((), ())), preferred_element_type=F32)


def by_half(low, high):
    lane = lax.broadcasted_iota(jnp.int32, low.shape, low.ndim - 1)
    return jnp.where(lane < low.shape[-1] // 2, low, high)


def turned(value):
    return pltpu.roll(value.astype(F32), value.shape[-1] // 2, 1).astype(value.dtype)


def face_rows_of(inverse, slot, face):
    nodes = inverse.shape[1]
    part = nodes // NP
    layer = part // NP
    lower = []
    upper = []
    for a in range(NP):
        head = inverse[slot, a * part : a * part + 2 * layer, :].astype(F32)
        tail = inverse[slot, (a + 1) * part - 2 * layer : (a + 1) * part, :].astype(F32)
        lower.append(head[:layer])
        upper.append(tail[layer:])
    faces = jnp.concatenate(lower + upper, axis=0).astype(BF16)
    outflow = inverse[slot, nodes - face :, :]
    return jnp.concatenate([faces, outflow, outflow], axis=0)


def pair_maps(maps, coupling, slots, rows, face):
    outs = []
    for i, slot in enumerate(slots):
        full = dot_nt(coupling[slot], rows[i])
        full = jnp.concatenate([full[2 * face :], full[face : 2 * face], full[:face]], axis=0).astype(BF16)
        maps[i * 3 * face : (i + 1) * 3 * face, :] = full[:, : 2 * face]
        outs.append(full[:, 2 * face :])
    maps[2 * 3 * face :, :] = by_half(outs[0], outs[1])


def first_kernel(order_far, inverse_far, coupling_far, given_far, *refs):
    maps, rows, inverse_near, coupling_near, given_near = refs[:5]
    inverse, coupling, order, order_done, done = refs[5:]
    count = given_near.shape[0]
    face = coupling.shape[1] // 3
    first = pltpu.make_async_copy(order_far, order, order_done)
    first.start()
    first.wait()
    early = []
    later = []
    for p in range(count):
        slot = order[p]
        near = (inverse.at[p], coupling.at[p]) if p < 2 else (inverse_near.at[p - 2], coupling_near.at[p - 2])
        copies = early if p < 2 else later
        copies.append(pltpu.make_async_copy(inverse_far.at[slot], near[0], done.at[0, p]))
        copies.append(pltpu.make_async_copy(coupling_far.at[slot], near[1], done.at[1, p]))
        later.append(pltpu.make_async_copy(given_far.at[slot], given_near.at[p], done.at[2, p]))
    for copy in early + later:
        copy.start()
    values = []
    for p in range(2):
        early[2 * p].wait()
        early[2 * p + 1].wait()
        values.append(face_rows_of(inverse, p, face))
        rows[p] = values[p]
    pair_maps(maps, coupling, (0, 1), values, face)
    for copy in later:
        copy.wait()


def rest_kernel(place, early_rows, inverse, coupling, given, *refs):
    count, _, width = given.shape
    maps = refs[: count // 2 - 1]
    gains = refs[count // 2 - 1 : -1]
    gathered = refs[-1]
    face = coupling.shape[1] // 3
    groups = len(gains)
    share = width // groups
    rows = [face_rows_of(inverse, p, face) for p in range(count - 2)]
    for j, target in enumerate(maps):
        pair_maps(target, coupling, (2 * j, 2 * j + 1), rows[2 * j : 2 * j + 2], face)
    rows = [early_rows[0], early_rows[1]] + rows
    every = [dot(rows[p], given[p]).T for p in range(count)]
    tiles = [gain[:, : 2 * face] for gain in every]
    for p in range(0, count, 2):
        tiles.append(by_half(every[p][:, 2 * face :], every[p + 1][:, 2 * face :]))
    for m, tile in enumerate(tiles):
        gathered[m] = tile
    for rel in range(groups):
        at = pl.multiple_of((place[0] ^ rel) * share, share)
        for m in range(len(tiles)):
            gains[rel][m] = gathered[m, pl.ds(at, share), :].astype(BF16)


def unpack_maps(map_refs, weights, face):
    for j, refs in enumerate(map_refs):
        for pos, ref in enumerate(refs):
            outs = ref[2 * 3 * face :, :]
            other = turned(outs)
            for i in range(2):
                sides = ref[i * 3 * face : (i + 1) * 3 * face, :]
                full = jnp.concatenate([sides, by_half(outs, other) if i == 0 else by_half(other, outs)], axis=1)
                weights[pos, 2 * j + i, : 3 * face, :] = full
                weights[pos, 2 * j + i, 3 * face :, :] = full[2 * face :]


def unpack_gains(gain_refs, gains, count):
    for rel, ref in enumerate(gain_refs):
        for p in range(count):
            outs = ref[count + p // 2]
            other = turned(outs)
            outs = by_half(outs, other) if p % 2 == 0 else by_half(other, outs)
            gains[reversed_static(rel, len(gain_refs)), p] = jnp.concatenate([ref[p], outs], axis=1)


def neighbours(me, pos, groups):
    own = me ^ reversed_bits(pos, groups)
    below = jnp.where(own > 0, reversed_bits(((own - 1) & (groups - 1)) ^ me, groups), groups)
    above = jnp.where(own < groups - 1, reversed_bits(((own + 1) & (groups - 1)) ^ me, groups), groups)
    return below, above


def read_lags(me, states, lags, groups, count):
    def read(pos):
        below, above = neighbours(me, pos, groups)
        for p in range(count):
            lags[pos, p] = by_half(states[above, p], states[below, p])

    over(groups, read)


def over(count, body, limit=4):
    if count <= limit:
        for i in range(count):
            body(i)
    else:

        def step(i, carry):
            body(i)
            return carry

        lax.fori_loop(0, count, step, 0)


def split_trace(out):
    high = out.astype(BF16)
    return by_half(high, (out - high.astype(F32)).astype(BF16)), high


def run_chains(chosen, entries, lags, weights, gains, states, count, face, first):
    share = gains.shape[2]
    outs = [[] for _ in chosen]
    for p in range(count):
        for i, pos in enumerate(chosen):
            rows = entries[i].shape[0]
            if first:
                result = dot(entries[i], weights[pos, p, 2 * face :])
            else:
                result = dot(jnp.concatenate([lags[pos, p, :rows], entries[i]], axis=1), weights[pos, p])
            head = result[:share] + gains[pos, p].astype(F32)
            result = head if rows == share else jnp.concatenate([head, result[share:]], axis=0)
            states[pos, p, :rows] = result[:, : 2 * face].astype(BF16)
            outs[i].append(result[:, 2 * face :])
        if p < count - 1:
            entries = [split_trace(o[p])[0] for o in outs]
    return outs


def respond_kernel(place, *refs, groups, count, face):
    pairs = count // 2
    map_refs = [refs[j * groups : (j + 1) * groups] for j in range(pairs)]
    gain_refs = refs[pairs * groups : (pairs + 1) * groups]
    response, offset, weights, gains, states, lags, unit = refs[(pairs + 1) * groups :]
    me = place[0]
    half = groups // 2
    share = gains.shape[2]
    unpack_maps(map_refs, weights, face)
    unpack_gains(gain_refs, gains, count)
    states[groups] = jnp.zeros_like(states[groups])
    row = lax.broadcasted_iota(jnp.int32, unit.shape[1:], 0) - share
    lane = lax.broadcasted_iota(jnp.int32, unit.shape[1:], 1)
    for pos in range(half):
        hit = jnp.logical_and(lane < face, row == lane + pos * face)
        unit[pos] = jnp.where(hit, 1.0, 0.0).astype(BF16)

    def sweep(k, parity, first=False):
        if not first:
            read_lags(me, states, lags, groups, count)

        def block(t):
            live = [2 * t + half * parity, 2 * t + 1 + half * parity]
            bare = [2 * t + half * (1 - parity), 2 * t + 1 + half * (1 - parity)]
            entries = [unit[pos] if first else jnp.zeros_like(unit[pos]) for pos in live]
            entries += [jnp.zeros((share, 2 * face), BF16)] * 2
            chains = run_chains(live + bare, entries, lags, weights, gains, states, count, face, first)
            ends = [outs[-1] for outs in chains]
            at = pl.ds(pl.multiple_of(t * 2 * face, 2 * face), 2 * face)
            full = by_half(ends[0], ends[1])
            response[k, :, at] = full[share:].astype(BF16)
            for target, tile in ((parity, full[:share]), (1 - parity, by_half(ends[2], ends[3]))):
                offset[k, target * share : (target + 1) * share, at] = tile.astype(BF16)

        over(groups // 4, block, 1)

    def both(i, carry):
        sweep(2 * i, 0)
        sweep(2 * i + 1, 1)
        return carry

    sweep(0, 0, True)
    sweep(1, 1)
    lax.fori_loop(1, SWEEPS // 2, both, 0)


def pick(flag, first, second):
    return jnp.where(flag != 0, first, second)


def pair_offset_kernel(line, own, other, got, got_other, own_offset, got_offset, offset, *, mask):
    down = (line[0] // mask) % 2
    share = own_offset.shape[1] // 2
    maps = [
        (pick(down, own[k], got[k]), pick(down, other[k], got_other[k])) for k in range(SWEEPS)
    ]
    values = []
    for k in range(SWEEPS):
        both = zip(halves_of(got_offset, k), halves_of(own_offset, k))
        values.append([pick(down, a, b) for a, b in both])
    for k in range(SWEEPS):
        both = zip(halves_of(own_offset, k), halves_of(got_offset, k))
        added = [pick(down, a, b).astype(F32) for a, b in both]
        for target, total in enumerate(moved_by(values, maps, k)):
            offset[k, target * share : (target + 1) * share] = (total + added[target]).astype(BF16)


def pair_map_kernel(line, own, other, got, got_other, response, *, mask):
    down = (line[0] // mask) % 2
    after = [
        (pick(down, own[k], got[k]), pick(down, other[k], got_other[k])) for k in range(SWEEPS)
    ]
    before = [pick(down, got[k], own[k]) for k in range(SWEEPS)]
    for m in range(SWEEPS):
        stack = jnp.concatenate([after[d][(m + d) % 2] for d in range(m + 1)], axis=0)
        left = jnp.concatenate([before[m - d] for d in range(m + 1)], axis=1)
        response[m] = dot(left, stack).astype(BF16)


def halves_of(ref, k):
    share = ref.shape[1] // 2
    return ref[k, :share], ref[k, share:]


def moved_by(values, maps, k):
    pair = []
    for target in (0, 1):
        stack = jnp.concatenate([maps[d][(target + d) % 2] for d in range(k + 1)], axis=0)
        left = jnp.concatenate([values[k - d][(target + d) % 2] for d in range(k + 1)], axis=1)
        pair.append(dot(left, stack))
    return pair


def add_own(values, maps, own):
    moved = []
    for k in range(SWEEPS):
        pair = zip(moved_by(values, maps, k), own[k])
        moved.append([(total + added.astype(F32)).astype(BF16) for total, added in pair])
    return moved


def put_halves(ref, values):
    share = ref.shape[1] // 2
    for k in range(SWEEPS):
        for target in (0, 1):
            ref[k, target * share : (target + 1) * share] = values[k][target]


def opening_kernel(even, odd, entry, own, opened):
    maps = [(even[k], odd[k]) for k in range(SWEEPS)]
    values = [halves_of(entry, k) for k in range(SWEEPS)]
    put_halves(opened, add_own(values, maps, [halves_of(own, k) for k in range(SWEEPS)]))


def join_kernel(line, own, other, got, got_other, own_offset, got_offset, near, across, joined, *, mask):
    down = (line[0] // mask) % 2
    values = [
        [pick(down, a, b) for a, b in zip(halves_of(near, k), halves_of(across, k))] for k in range(SWEEPS)
    ]
    for turn in (down, 1 - down):
        maps = [(pick(turn, got[k], own[k]), pick(turn, got_other[k], other[k])) for k in range(SWEEPS)]
        added = [
            [pick(turn, a, b) for a, b in zip(halves_of(got_offset, k), halves_of(own_offset, k))]
            for k in range(SWEEPS)
        ]
        values = add_own(values, maps, added)
    put_halves(joined, values)


def resolve_kernel(place, line, *refs, groups, count, face, masks):
    weights, gains, near, across, second, third, ahead_even, ahead_odd = refs[:8]
    levels = len(masks) - 2
    lower = refs[8 : 8 + 3 * levels]
    wanted = refs[8 + 3 * levels : 8 + 3 * levels + groups]
    states, lags, inflows = refs[8 + 3 * levels + groups :]
    me = place[0]
    half = groups // 2
    states[groups] = jnp.zeros_like(states[groups])
    flags = [(line[0] // mask) % 2 for mask in masks]
    maps = [(ahead_even[k], ahead_odd[k]) for k in range(SWEEPS)]
    given = [halves_of(third, k) for k in range(SWEEPS)]
    values = []
    for k in range(SWEEPS):
        pair = []
        for target, total in enumerate(moved_by(given, maps, k)):
            own = pick(flags[-3], halves_of(near, k)[target], halves_of(across, k)[target])
            last = (total + own.astype(F32)).astype(BF16)
            upper = pick(flags[-2], last, halves_of(second, k)[target])
            pair.append(pick(flags[-1], upper, pick(flags[-2], own, jnp.zeros_like(own))))
        values.append(pair)
    for level in range(levels - 1, -1, -1):
        even, odd, offset = lower[3 * level : 3 * level + 3]
        maps = [(even[k], odd[k]) for k in range(SWEEPS)]
        moved = []
        for k in range(SWEEPS):
            pair = []
            for target, total in enumerate(moved_by(values, maps, k)):
                total = total + halves_of(offset, k)[target].astype(F32)
                pair.append(pick(flags[level], total.astype(BF16), values[k][target]))
            moved.append(pair)
        values = moved
    blank = jnp.zeros((values[0][0].shape[0], 2 * face), BF16)
    for k in range(SWEEPS):
        for pos in range(groups):
            tile = (pos % half) // 2
            both = values[k][pos // half][:, tile * 2 * face : (tile + 1) * 2 * face]
            inflows[k, pos] = by_half(both if pos % 2 == 0 else turned(both), blank)

    def chains(k, t, stage):
        chosen = tuple(4 * t + i for i in range(4))
        entries = [inflows[k, pos] for pos in chosen]
        every = [[entry] for entry in entries]
        for p in range(count - (stage == 2)):
            for i, pos in enumerate(chosen):
                left = every[i][p][:, :face]
                right = weights[pos, p, 2 * face : 3 * face]
                added = gains[pos, p].astype(F32)
                if stage > 0:
                    left = jnp.concatenate([lags[pos, p], left], axis=1)
                    right = weights[pos, p, : 3 * face]
                if stage == 2:
                    right = right[:, 2 * face :]
                    added = added[:, 2 * face :]
                result = dot(left, right) + added
                if stage < 2:
                    states[pos, p] = result[:, : 2 * face].astype(BF16)
                    result = result[:, 2 * face :]
                every[i].append(result.astype(BF16))
        return chosen, every

    def blocks(k, stage):
        over(groups // 4, lambda t: chains(k, t, stage), 1)

    blocks(0, 0)

    def sweep(k, carry):
        read_lags(me, states, lags, groups, count)
        blocks(k, 1)
        return carry

    lax.fori_loop(1, SWEEPS - 1, sweep, 0)
    read_lags(me, states, lags, groups, count)
    for t in range(groups // 4):
        chosen, every = chains(SWEEPS - 1, t, 2)
        for i, pos in enumerate(chosen):
            target = wanted[reversed_static(pos, groups)]
            traces = every[i]
            for p in range(count):
                target[p] = lags[pos, p]
            target[count] = by_half(traces[0], traces[count - 1])
            for m in range(1, count // 2):
                target[count + m] = by_half(traces[2 * m - 1], traces[2 * m])


def final_kernel(place, order, inverse, coupling, given, *refs):
    wanted = refs[:-4]
    placed, solved, gathered, done = refs[-4:]
    count, nodes, width = given.shape
    face = coupling.shape[1] // 3
    share = width // len(wanted)
    for rel, ref in enumerate(wanted):
        at = pl.multiple_of((place[0] ^ rel) * share, share)
        for m in range(ref.shape[0]):
            gathered[m, pl.ds(at, share), :] = ref[m].astype(gathered.dtype)
    blank = jnp.zeros((face, nodes), BF16)
    copies = []
    for p in range(count):
        slot = order[p]
        rows = coupling[slot]
        second = p == count - 1 or (p > 0 and p % 2 == 0)
        tile = 0 if p == count - 1 else (p + 1) // 2
        pair = [blank, rows[:face]] if second else [rows[:face], blank]
        sides = jnp.concatenate([rows[2 * face :], rows[face : 2 * face]] + pair, axis=0)
        traces = jnp.concatenate([gathered[p], gathered[count + tile]], axis=1).astype(BF16)
        source = given[slot].astype(F32) + dot(traces, sides).T
        solved[p] = dot(inverse[slot], source.astype(BF16)).astype(BF16)
        copies.append(pltpu.make_async_copy(solved.at[p], placed.at[slot], done.at[p]))
        copies[p].start()
    for copy in copies:
        copy.wait()


def gather_list(value, axis):
    values = [value]
    for mask in bits_of(lax.axis_size(axis))[::-1]:
        values = values + [swap(v, axis, mask) for v in values]
    return values


def exchange(values, axis):
    return [v if rel == 0 else swap(v, axis, rel) for rel, v in enumerate(values)]


def call(kernel, outs, scratch, scalars, arrays, far=0, others=(), space=VMEM):
    def size(shape, kind):
        total = jnp.dtype(kind).itemsize
        for extent in shape:
            total *= extent
        return total

    held = sum(size(o.shape, o.dtype) for o in outs) + sum(size(a.shape, a.dtype) for a in arrays)
    held += sum(size(shape, kind) for shape, kind in scratch)
    return pl.pallas_call(
        kernel,
        out_shape=outs,
        in_specs=[SMEM] * len(scalars) + [VMEM] * (len(arrays) - far) + [HBM] * far,
        out_specs=[space] * len(outs),
        scratch_shapes=[*[pltpu.VMEM(shape, kind) for shape, kind in scratch], *others],
        compiler_params=pltpu.CompilerParams(vmem_limit_bytes=min(held + (3 << 20), 60 << 20)),
    )(*scalars, *arrays)


def shards(right_sides, inverse, coupling, sweep_order):
    given = right_sides[0, 0]
    inverse = inverse[0, 0]
    order = sweep_order[0, 0]
    count, nodes, width = given.shape
    face = coupling.shape[4]
    coupling = coupling[0, 0].reshape(count, 3 * face, nodes)
    groups = lax.axis_size("span")
    share = width // groups
    half = groups // 2
    place = lax.axis_index("span").astype(jnp.int32).reshape(1)
    line = lax.axis_index("stream").astype(jnp.int32).reshape(1)
    masks = bits_of(lax.axis_size("stream"))
    tiles = count + count // 2
    shape = jax.ShapeDtypeStruct
    far = [pltpu.with_memory_space_constraint(a, pltpu.HBM) for a in (order, inverse, coupling, given)]
    maps, *near = call(
        first_kernel,
        [
            shape((3 * 3 * face, 2 * face), BF16),
            shape((2, 4 * face, nodes), BF16),
            shape((count - 2,) + inverse.shape[1:], BF16),
            shape((count - 2,) + coupling.shape[1:], BF16),
            shape(given.shape, BF16),
        ],
        [((2,) + inverse.shape[1:], BF16), ((2,) + coupling.shape[1:], BF16)],
        [],
        far,
        4,
        (
            pltpu.SMEM(order.shape, order.dtype),
            pltpu.SemaphoreType.DMA,
            pltpu.SemaphoreType.DMA((3, count)),
        ),
    )
    all_maps = gather_list(maps, "span")
    outs = call(
        rest_kernel,
        [shape(maps.shape, BF16)] * (count // 2 - 1) + [shape((tiles, share, 2 * face), BF16)] * groups,
        [((tiles, width, 2 * face), F32)],
        [place],
        near,
    )
    gains = outs[count // 2 - 1 :]
    for maps in outs[: count // 2 - 1]:
        all_maps += gather_list(maps, "span")
    gains = exchange(gains, "span")
    sizes = dict(groups=groups, count=count, face=face)
    wide = half * face
    response, offset, weights, gains = call(
        functools.partial(respond_kernel, **sizes),
        [
            shape((SWEEPS, wide, wide), BF16),
            shape((SWEEPS, 2 * share, wide), BF16),
            shape((groups, count, 4 * face, 4 * face), BF16),
            shape((groups, count, share, 4 * face), BF16),
        ],
        [
            ((groups + 1, count, share + wide, 2 * face), BF16),
            ((groups, count, share + wide, 2 * face), BF16),
            ((half, share + wide, 2 * face), BF16),
        ],
        [place],
        [*all_maps, *gains],
    )
    levels = []
    for mask in masks[:-2]:
        got_offset = swap(offset, "stream", mask)
        other = swap(response, "span", 1)
        got = swap(response, "stream", mask)
        got_other = swap(got, "span", 1)
        levels += [got, got_other, got_offset]
        arrays = [response, other, got, got_other]
        same = shape(offset.shape, BF16)
        if mask == masks[-3]:
            (opened,) = call(opening_kernel, [same], [], [], [response, other, got_offset, offset])
            near = swap(opened, "stream", masks[-2])
            across = swap(opened, "stream", masks[-2] | mask)
            joining = arrays + [offset, got_offset, near, across]
        else:
            (offset,) = call(
                functools.partial(pair_offset_kernel, mask=mask), [same], [], [line], arrays + [offset, got_offset]
            )
        (response,) = call(
            functools.partial(pair_map_kernel, mask=mask), [shape(response.shape, BF16)], [], [line], arrays
        )
    ahead_even = swap(response, "stream", masks[-2])
    (joined,) = call(functools.partial(join_kernel, mask=masks[-3]), [same], [], [line], joining)
    second = lax.ppermute(joined, "stream", crossing(masks))
    third = swap(joined, "stream", masks[-1])
    ahead_odd = swap(ahead_even, "span", 1)
    wanted = call(
        functools.partial(resolve_kernel, masks=masks, **sizes),
        [shape((tiles, share, 2 * face), BF16)] * groups,
        [
            ((groups + 1, count, share, 2 * face), BF16),
            ((groups, count, share, 2 * face), BF16),
            ((SWEEPS, groups, share, 2 * face), BF16),
        ],
        [place, line],
        [weights, gains, near, across, second, third, ahead_even, ahead_odd, *levels],
    )
    wanted = exchange(wanted, "span")
    (placed,) = call(
        final_kernel,
        [shape((count, nodes, width), BF16)],
        [((count, nodes, width), BF16), ((tiles, width, 2 * face), BF16 if share % 16 == 0 else F32)],
        [place, order],
        [inverse, coupling, given, *wanted],
        0,
        (pltpu.SemaphoreType.DMA((count,)),),
        HBM,
    )
    return placed[None, None]


def solution(mesh):
    in_specs = (
        P("stream", "span", None, None, None),
        P("stream", "span", None, None, None),
        P("stream", "span", None, None, None, None),
        P("stream", "span", None),
    )
    out_specs = P("stream", "span", None, None, None)
    return jax.shard_map(shards, mesh=mesh, in_specs=in_specs, out_specs=out_specs, check_vma=False)
```

```python
import functools

import jax
import jax.numpy as jnp
from jax import lax
from jax.experimental import pallas as pl
from jax.experimental.pallas import tpu as pltpu
from jax.sharding import PartitionSpec as P

NP = 8
SWEEPS = 6
VMEM = pl.BlockSpec(memory_space=pltpu.VMEM)
SMEM = pl.BlockSpec(memory_space=pltpu.SMEM)
HBM = pl.BlockSpec(memory_space=pltpu.HBM)
F32 = jnp.float32
BF16 = jnp.bfloat16


def bits_of(count):
    return [1 << i for i in range(count.bit_length() - 1)]


def reversed_bits(value, count):
    bits = bits_of(count)
    total = 0
    for low, high in zip(bits, bits[::-1]):
        total = total + jnp.where((value & low) != 0, high, 0)
    return total


def reversed_static(value, count):
    bits = bits_of(count)
    return sum(high for low, high in zip(bits, bits[::-1]) if value & low)


def swap(value, axis, mask):
    count = lax.axis_size(axis)
    return lax.ppermute(value, axis, [(i, i ^ mask) for i in range(count)])


def crossing(masks, first, second):
    pairs = []
    for i in range(2 * masks[-1]):
        quarter = i // masks[-2]
        inner = quarter in (first, second)
        pairs.append((i, i ^ ((first ^ second) * masks[-2] if inner else 1)))
    return pairs


def dot(left, right):
    return jnp.dot(left, right, preferred_element_type=F32)


def dot_nt(left, right):
    return lax.dot_general(left, right, (((1,), (1,)), ((), ())), preferred_element_type=F32)


def by_half(low, high):
    lane = lax.broadcasted_iota(jnp.int32, low.shape, low.ndim - 1)
    return jnp.where(lane < low.shape[-1] // 2, low, high)


def turned(value):
    return pltpu.roll(value.astype(F32), value.shape[-1] // 2, 1).astype(value.dtype)


def face_rows_of(inverse, slot, face):
    nodes = inverse.shape[1]
    part = nodes // NP
    layer = part // NP
    lower = []
    upper = []
    for a in range(NP):
        head = inverse[slot, a * part : a * part + 2 * layer, :].astype(F32)
        tail = inverse[slot, (a + 1) * part - 2 * layer : (a + 1) * part, :].astype(F32)
        lower.append(head[:layer])
        upper.append(tail[layer:])
    faces = jnp.concatenate(lower + upper, axis=0).astype(BF16)
    outflow = inverse[slot, nodes - face :, :]
    return jnp.concatenate([faces, outflow, outflow], axis=0)


def pair_maps(maps, coupling, slots, rows, face):
    outs = []
    for i, slot in enumerate(slots):
        full = dot_nt(coupling[slot], rows[i])
        full = jnp.concatenate([full[2 * face :], full[face : 2 * face], full[:face]], axis=0).astype(BF16)
        maps[i * 3 * face : (i + 1) * 3 * face, :] = full[:, : 2 * face]
        outs.append(full[:, 2 * face :])
    maps[2 * 3 * face :, :] = by_half(outs[0], outs[1])


def first_kernel(order_far, inverse_far, coupling_far, given_far, *refs):
    maps, rows, inverse_near, coupling_near, given_near = refs[:5]
    inverse, coupling, order, order_done, done = refs[5:]
    count = given_near.shape[0]
    face = coupling.shape[1] // 3
    first = pltpu.make_async_copy(order_far, order, order_done)
    first.start()
    first.wait()
    early = []
    later = []
    for p in range(count):
        slot = order[p]
        near = (inverse.at[p], coupling.at[p]) if p < 2 else (inverse_near.at[p - 2], coupling_near.at[p - 2])
        copies = early if p < 2 else later
        copies.append(pltpu.make_async_copy(inverse_far.at[slot], near[0], done.at[0, p]))
        copies.append(pltpu.make_async_copy(coupling_far.at[slot], near[1], done.at[1, p]))
        later.append(pltpu.make_async_copy(given_far.at[slot], given_near.at[p], done.at[2, p]))
    for copy in early + later:
        copy.start()
    values = []
    for p in range(2):
        early[2 * p].wait()
        early[2 * p + 1].wait()
        values.append(face_rows_of(inverse, p, face))
        rows[p] = values[p]
    pair_maps(maps, coupling, (0, 1), values, face)
    for copy in later:
        copy.wait()


def rest_kernel(place, early_rows, inverse, coupling, given, *refs):
    count, _, width = given.shape
    maps = refs[: count // 2 - 1]
    gains = refs[count // 2 - 1 : -1]
    gathered = refs[-1]
    face = coupling.shape[1] // 3
    groups = len(gains)
    share = width // groups
    rows = [face_rows_of(inverse, p, face) for p in range(count - 2)]
    for j, target in enumerate(maps):
        pair_maps(target, coupling, (2 * j, 2 * j + 1), rows[2 * j : 2 * j + 2], face)
    rows = [early_rows[0], early_rows[1]] + rows
    every = [dot(rows[p], given[p]).T for p in range(count)]
    tiles = [gain[:, : 2 * face] for gain in every]
    for p in range(0, count, 2):
        tiles.append(by_half(every[p][:, 2 * face :], every[p + 1][:, 2 * face :]))
    for m, tile in enumerate(tiles):
        gathered[m] = tile
    for rel in range(groups):
        at = pl.multiple_of((place[0] ^ rel) * share, share)
        for m in range(len(tiles)):
            gains[rel][m] = gathered[m, pl.ds(at, share), :].astype(BF16)


def unpack_maps(map_refs, weights, face):
    for j, refs in enumerate(map_refs):
        for pos, ref in enumerate(refs):
            outs = ref[2 * 3 * face :, :]
            other = turned(outs)
            for i in range(2):
                sides = ref[i * 3 * face : (i + 1) * 3 * face, :]
                full = jnp.concatenate([sides, by_half(outs, other) if i == 0 else by_half(other, outs)], axis=1)
                weights[pos, 2 * j + i, : 3 * face, :] = full
                weights[pos, 2 * j + i, 3 * face :, :] = full[2 * face :]


def unpack_gains(gain_refs, gains, count):
    for rel, ref in enumerate(gain_refs):
        for p in range(count):
            outs = ref[count + p // 2]
            other = turned(outs)
            outs = by_half(outs, other) if p % 2 == 0 else by_half(other, outs)
            gains[reversed_static(rel, len(gain_refs)), p] = jnp.concatenate([ref[p], outs], axis=1)


def neighbours(me, pos, groups):
    own = me ^ reversed_bits(pos, groups)
    below = jnp.where(own > 0, reversed_bits(((own - 1) & (groups - 1)) ^ me, groups), groups)
    above = jnp.where(own < groups - 1, reversed_bits(((own + 1) & (groups - 1)) ^ me, groups), groups)
    return below, above


def read_lags(me, states, lags, groups, count):
    def read(pos):
        below, above = neighbours(me, pos, groups)
        for p in range(count):
            lags[pos, p] = by_half(states[above, p], states[below, p])

    over(groups, read)


def over(count, body, limit=4):
    if count <= limit:
        for i in range(count):
            body(i)
    else:

        def step(i, carry):
            body(i)
            return carry

        lax.fori_loop(0, count, step, 0)


def split_trace(out):
    high = out.astype(BF16)
    return by_half(high, (out - high.astype(F32)).astype(BF16)), high


def run_chains(chosen, entries, lags, weights, gains, states, count, face, first):
    share = gains.shape[2]
    outs = [[] for _ in chosen]
    for p in range(count):
        for i, pos in enumerate(chosen):
            rows = entries[i].shape[0]
            if first:
                result = dot(entries[i], weights[pos, p, 2 * face :])
            else:
                result = dot(jnp.concatenate([lags[pos, p, :rows], entries[i]], axis=1), weights[pos, p])
            head = result[:share] + gains[pos, p].astype(F32)
            result = head if rows == share else jnp.concatenate([head, result[share:]], axis=0)
            states[pos, p, :rows] = result[:, : 2 * face].astype(BF16)
            outs[i].append(result[:, 2 * face :])
        if p < count - 1:
            entries = [split_trace(o[p])[0] for o in outs]
    return outs


def respond_kernel(place, *refs, groups, count, face):
    pairs = count // 2
    map_refs = [refs[j * groups : (j + 1) * groups] for j in range(pairs)]
    gain_refs = refs[pairs * groups : (pairs + 1) * groups]
    response, offset, weights, gains, states, lags, unit = refs[(pairs + 1) * groups :]
    me = place[0]
    half = groups // 2
    share = gains.shape[2]
    unpack_maps(map_refs, weights, face)
    unpack_gains(gain_refs, gains, count)
    states[groups] = jnp.zeros_like(states[groups])
    row = lax.broadcasted_iota(jnp.int32, unit.shape[1:], 0) - share
    lane = lax.broadcasted_iota(jnp.int32, unit.shape[1:], 1)
    for pos in range(half):
        hit = jnp.logical_and(lane < face, row == lane + pos * face)
        unit[pos] = jnp.where(hit, 1.0, 0.0).astype(BF16)

    def sweep(k, parity, first=False):
        if not first:
            read_lags(me, states, lags, groups, count)

        def block(t):
            live = [2 * t + half * parity, 2 * t + 1 + half * parity]
            bare = [2 * t + half * (1 - parity), 2 * t + 1 + half * (1 - parity)]
            entries = [unit[pos] if first else jnp.zeros_like(unit[pos]) for pos in live]
            entries += [jnp.zeros((share, 2 * face), BF16)] * 2
            chains = run_chains(live + bare, entries, lags, weights, gains, states, count, face, first)
            ends = [outs[-1] for outs in chains]
            at = pl.ds(pl.multiple_of(t * 2 * face, 2 * face), 2 * face)
            full = by_half(ends[0], ends[1])
            response[k, :, at] = full[share:].astype(BF16)
            for target, tile in ((parity, full[:share]), (1 - parity, by_half(ends[2], ends[3]))):
                offset[k, target * share : (target + 1) * share, at] = tile.astype(BF16)

        over(groups // 4, block, 1)

    def both(i, carry):
        sweep(2 * i, 0)
        sweep(2 * i + 1, 1)
        return carry

    sweep(0, 0, True)
    sweep(1, 1)
    lax.fori_loop(1, SWEEPS // 2, both, 0)


def pick(flag, first, second):
    return jnp.where(flag != 0, first, second)


def pair_offset_kernel(line, own, other, got, got_other, own_offset, got_offset, offset, *, mask):
    down = (line[0] // mask) % 2
    share = own_offset.shape[1] // 2
    maps = [
        (pick(down, own[k], got[k]), pick(down, other[k], got_other[k])) for k in range(SWEEPS)
    ]
    values = []
    for k in range(SWEEPS):
        both = zip(halves_of(got_offset, k), halves_of(own_offset, k))
        values.append([pick(down, a, b) for a, b in both])
    for k in range(SWEEPS):
        both = zip(halves_of(own_offset, k), halves_of(got_offset, k))
        added = [pick(down, a, b).astype(F32) for a, b in both]
        for target, total in enumerate(moved_by(values, maps, k)):
            offset[k, target * share : (target + 1) * share] = (total + added[target]).astype(BF16)


def pair_map_kernel(line, own, other, got, got_other, response, *, mask):
    down = (line[0] // mask) % 2
    after = [
        (pick(down, own[k], got[k]), pick(down, other[k], got_other[k])) for k in range(SWEEPS)
    ]
    before = [pick(down, got[k], own[k]) for k in range(SWEEPS)]
    for m in range(SWEEPS):
        stack = jnp.concatenate([after[d][(m + d) % 2] for d in range(m + 1)], axis=0)
        left = jnp.concatenate([before[m - d] for d in range(m + 1)], axis=1)
        response[m] = dot(left, stack).astype(BF16)


def halves_of(ref, k):
    share = ref.shape[1] // 2
    return ref[k, :share], ref[k, share:]


def moved_by(values, maps, k):
    pair = []
    for target in (0, 1):
        stack = jnp.concatenate([maps[d][(target + d) % 2] for d in range(k + 1)], axis=0)
        left = jnp.concatenate([values[k - d][(target + d) % 2] for d in range(k + 1)], axis=1)
        pair.append(dot(left, stack))
    return pair


def add_own(values, maps, own):
    moved = []
    for k in range(SWEEPS):
        pair = zip(moved_by(values, maps, k), own[k])
        moved.append([(total + added.astype(F32)).astype(BF16) for total, added in pair])
    return moved


def put_halves(ref, values):
    share = ref.shape[1] // 2
    for k in range(SWEEPS):
        for target in (0, 1):
            ref[k, target * share : (target + 1) * share] = values[k][target]


def opening_kernel(even, odd, entry, own, opened):
    maps = [(even[k], odd[k]) for k in range(SWEEPS)]
    values = [halves_of(entry, k) for k in range(SWEEPS)]
    put_halves(opened, add_own(values, maps, [halves_of(own, k) for k in range(SWEEPS)]))


def join_kernel(line, own, other, got, got_other, own_offset, got_offset, near, across, joined, *, mask):
    down = (line[0] // mask) % 2
    values = [
        [pick(down, a, b) for a, b in zip(halves_of(near, k), halves_of(across, k))] for k in range(SWEEPS)
    ]
    for turn in (down, 1 - down):
        maps = [(pick(turn, got[k], own[k]), pick(turn, got_other[k], other[k])) for k in range(SWEEPS)]
        added = [
            [pick(turn, a, b) for a, b in zip(halves_of(got_offset, k), halves_of(own_offset, k))]
            for k in range(SWEEPS)
        ]
        values = add_own(values, maps, added)
    put_halves(joined, values)


def resolve_kernel(place, line, *refs, groups, count, face, masks):
    weights, gains, near, across, second, third, ahead_even, ahead_odd = refs[:8]
    levels = len(masks) - 2
    lower = refs[8 : 8 + 3 * levels]
    wanted = refs[8 + 3 * levels : 8 + 3 * levels + groups]
    states, lags, inflows = refs[8 + 3 * levels + groups :]
    me = place[0]
    half = groups // 2
    states[groups] = jnp.zeros_like(states[groups])
    flags = [(line[0] // mask) % 2 for mask in masks]
    maps = [(ahead_even[k], ahead_odd[k]) for k in range(SWEEPS)]
    given = [halves_of(third, k) for k in range(SWEEPS)]
    values = []
    for k in range(SWEEPS):
        pair = []
        for target, total in enumerate(moved_by(given, maps, k)):
            own = pick(flags[-3], halves_of(near, k)[target], halves_of(across, k)[target])
            last = (total + own.astype(F32)).astype(BF16)
            upper = pick(flags[-2], last, halves_of(second, k)[target])
            pair.append(pick(flags[-1], upper, pick(flags[-2], own, jnp.zeros_like(own))))
        values.append(pair)
    for level in range(levels - 1, -1, -1):
        even, odd, offset = lower[3 * level : 3 * level + 3]
        maps = [(even[k], odd[k]) for k in range(SWEEPS)]
        moved = []
        for k in range(SWEEPS):
            pair = []
            for target, total in enumerate(moved_by(values, maps, k)):
                total = total + halves_of(offset, k)[target].astype(F32)
                pair.append(pick(flags[level], total.astype(BF16), values[k][target]))
            moved.append(pair)
        values = moved
    blank = jnp.zeros((values[0][0].shape[0], 2 * face), BF16)
    for k in range(SWEEPS):
        for pos in range(groups):
            tile = (pos % half) // 2
            both = values[k][pos // half][:, tile * 2 * face : (tile + 1) * 2 * face]
            inflows[k, pos] = by_half(both if pos % 2 == 0 else turned(both), blank)

    def chains(k, t, stage):
        chosen = tuple(4 * t + i for i in range(4))
        entries = [inflows[k, pos] for pos in chosen]
        every = [[entry] for entry in entries]
        for p in range(count - (stage == 2)):
            for i, pos in enumerate(chosen):
                left = every[i][p][:, :face]
                right = weights[pos, p, 2 * face : 3 * face]
                added = gains[pos, p].astype(F32)
                if stage > 0:
                    left = jnp.concatenate([lags[pos, p], left], axis=1)
                    right = weights[pos, p, : 3 * face]
                if stage == 2:
                    right = right[:, 2 * face :]
                    added = added[:, 2 * face :]
                result = dot(left, right) + added
                if stage < 2:
                    states[pos, p] = result[:, : 2 * face].astype(BF16)
                    result = result[:, 2 * face :]
                every[i].append(result.astype(BF16))
        return chosen, every

    def blocks(k, stage):
        over(groups // 4, lambda t: chains(k, t, stage), 1)

    blocks(0, 0)

    def sweep(k, carry):
        read_lags(me, states, lags, groups, count)
        blocks(k, 1)
        return carry

    lax.fori_loop(1, SWEEPS - 1, sweep, 0)
    read_lags(me, states, lags, groups, count)
    for t in range(groups // 4):
        chosen, every = chains(SWEEPS - 1, t, 2)
        for i, pos in enumerate(chosen):
            target = wanted[reversed_static(pos, groups)]
            traces = every[i]
            for p in range(count):
                target[p] = lags[pos, p]
            target[count] = by_half(traces[0], traces[count - 1])
            for m in range(1, count // 2):
                target[count + m] = by_half(traces[2 * m - 1], traces[2 * m])


def final_kernel(place, order, inverse, coupling, given, *refs):
    wanted = refs[:-4]
    placed, solved, gathered, done = refs[-4:]
    count, nodes, width = given.shape
    face = coupling.shape[1] // 3
    share = width // len(wanted)
    for rel, ref in enumerate(wanted):
        at = pl.multiple_of((place[0] ^ rel) * share, share)
        for m in range(ref.shape[0]):
            gathered[m, pl.ds(at, share), :] = ref[m].astype(gathered.dtype)
    blank = jnp.zeros((face, nodes), BF16)
    copies = []
    for p in range(count):
        slot = order[p]
        rows = coupling[slot]
        second = p == count - 1 or (p > 0 and p % 2 == 0)
        tile = 0 if p == count - 1 else (p + 1) // 2
        pair = [blank, rows[:face]] if second else [rows[:face], blank]
        sides = jnp.concatenate([rows[2 * face :], rows[face : 2 * face]] + pair, axis=0)
        traces = jnp.concatenate([gathered[p], gathered[count + tile]], axis=1).astype(BF16)
        source = given[slot].astype(F32) + dot(traces, sides).T
        solved[p] = dot(inverse[slot], source.astype(BF16)).astype(BF16)
        copies.append(pltpu.make_async_copy(solved.at[p], placed.at[slot], done.at[p]))
        copies[p].start()
    for copy in copies:
        copy.wait()


def gather_list(value, axis):
    values = [value]
    for mask in bits_of(lax.axis_size(axis))[::-1]:
        values = values + [swap(v, axis, mask) for v in values]
    return values


def exchange(values, axis):
    return [v if rel == 0 else swap(v, axis, rel) for rel, v in enumerate(values)]


def call(kernel, outs, scratch, scalars, arrays, far=0, others=(), space=VMEM):
    def size(shape, kind):
        total = jnp.dtype(kind).itemsize
        for extent in shape:
            total *= extent
        return total

    held = sum(size(o.shape, o.dtype) for o in outs) + sum(size(a.shape, a.dtype) for a in arrays)
    held += sum(size(shape, kind) for shape, kind in scratch)
    return pl.pallas_call(
        kernel,
        out_shape=outs,
        in_specs=[SMEM] * len(scalars) + [VMEM] * (len(arrays) - far) + [HBM] * far,
        out_specs=[space] * len(outs),
        scratch_shapes=[*[pltpu.VMEM(shape, kind) for shape, kind in scratch], *others],
        compiler_params=pltpu.CompilerParams(vmem_limit_bytes=min(held + (3 << 20), 60 << 20)),
    )(*scalars, *arrays)


def shards(right_sides, inverse, coupling, sweep_order):
    given = right_sides[0, 0]
    inverse = inverse[0, 0]
    order = sweep_order[0, 0]
    count, nodes, width = given.shape
    face = coupling.shape[4]
    coupling = coupling[0, 0].reshape(count, 3 * face, nodes)
    groups = lax.axis_size("span")
    share = width // groups
    half = groups // 2
    place = lax.axis_index("span").astype(jnp.int32).reshape(1)
    line = lax.axis_index("stream").astype(jnp.int32).reshape(1)
    masks = bits_of(lax.axis_size("stream"))
    tiles = count + count // 2
    shape = jax.ShapeDtypeStruct
    far = [pltpu.with_memory_space_constraint(a, pltpu.HBM) for a in (order, inverse, coupling, given)]
    maps, *near = call(
        first_kernel,
        [
            shape((3 * 3 * face, 2 * face), BF16),
            shape((2, 4 * face, nodes), BF16),
            shape((count - 2,) + inverse.shape[1:], BF16),
            shape((count - 2,) + coupling.shape[1:], BF16),
            shape(given.shape, BF16),
        ],
        [((2,) + inverse.shape[1:], BF16), ((2,) + coupling.shape[1:], BF16)],
        [],
        far,
        4,
        (
            pltpu.SMEM(order.shape, order.dtype),
            pltpu.SemaphoreType.DMA,
            pltpu.SemaphoreType.DMA((3, count)),
        ),
    )
    all_maps = gather_list(maps, "span")
    outs = call(
        rest_kernel,
        [shape(maps.shape, BF16)] * (count // 2 - 1) + [shape((tiles, share, 2 * face), BF16)] * groups,
        [((tiles, width, 2 * face), F32)],
        [place],
        near,
    )
    gains = outs[count // 2 - 1 :]
    for maps in outs[: count // 2 - 1]:
        all_maps += gather_list(maps, "span")
    gains = exchange(gains, "span")
    sizes = dict(groups=groups, count=count, face=face)
    wide = half * face
    response, offset, weights, gains = call(
        functools.partial(respond_kernel, **sizes),
        [
            shape((SWEEPS, wide, wide), BF16),
            shape((SWEEPS, 2 * share, wide), BF16),
            shape((groups, count, 4 * face, 4 * face), BF16),
            shape((groups, count, share, 4 * face), BF16),
        ],
        [
            ((groups + 1, count, share + wide, 2 * face), BF16),
            ((groups, count, share + wide, 2 * face), BF16),
            ((half, share + wide, 2 * face), BF16),
        ],
        [place],
        [*all_maps, *gains],
    )
    levels = []
    for mask in masks[:-2]:
        got_offset = swap(offset, "stream", mask)
        other = swap(response, "span", 1)
        got = swap(response, "stream", mask)
        got_other = swap(got, "span", 1)
        levels += [got, got_other, got_offset]
        arrays = [response, other, got, got_other]
        same = shape(offset.shape, BF16)
        if mask == masks[-3]:
            (opened,) = call(opening_kernel, [same], [], [], [response, other, got_offset, offset])
            near = swap(opened, "stream", masks[-2])
            across = swap(opened, "stream", masks[-2] | mask)
            joining = arrays + [offset, got_offset, near, across]
        else:
            (offset,) = call(
                functools.partial(pair_offset_kernel, mask=mask), [same], [], [line], arrays + [offset, got_offset]
            )
        (response,) = call(
            functools.partial(pair_map_kernel, mask=mask), [shape(response.shape, BF16)], [], [line], arrays
        )
    ahead_even = swap(response, "stream", masks[-2])
    (joined,) = call(functools.partial(join_kernel, mask=masks[-3]), [same], [], [line], joining)
    second = lax.ppermute(joined, "stream", crossing(masks, 1, 2))
    third = lax.ppermute(joined, "stream", crossing(masks, 1, 3))
    ahead_odd = swap(ahead_even, "span", 1)
    wanted = call(
        functools.partial(resolve_kernel, masks=masks, **sizes),
        [shape((tiles, share, 2 * face), BF16)] * groups,
        [
            ((groups + 1, count, share, 2 * face), BF16),
            ((groups, count, share, 2 * face), BF16),
            ((SWEEPS, groups, share, 2 * face), BF16),
        ],
        [place, line],
        [weights, gains, near, across, second, third, ahead_even, ahead_odd, *levels],
    )
    wanted = exchange(wanted, "span")
    (placed,) = call(
        final_kernel,
        [shape((count, nodes, width), BF16)],
        [((count, nodes, width), BF16), ((tiles, width, 2 * face), BF16 if share % 16 == 0 else F32)],
        [place, order],
        [inverse, coupling, given, *wanted],
        0,
        (pltpu.SemaphoreType.DMA((count,)),),
        HBM,
    )
    return placed[None, None]


def solution(mesh):
    in_specs = (
        P("stream", "span", None, None, None),
        P("stream", "span", None, None, None),
        P("stream", "span", None, None, None, None),
        P("stream", "span", None),
    )
    out_specs = P("stream", "span", None, None, None)
    return jax.shard_map(shards, mesh=mesh, in_specs=in_specs, out_specs=out_specs, check_vma=False)
```

```python
import functools

import jax
import jax.numpy as jnp
from jax import lax
from jax.experimental import pallas as pl
from jax.experimental.pallas import tpu as pltpu
from jax.sharding import PartitionSpec as P

NP = 8
SWEEPS = 6
VMEM = pl.BlockSpec(memory_space=pltpu.VMEM)
SMEM = pl.BlockSpec(memory_space=pltpu.SMEM)
HBM = pl.BlockSpec(memory_space=pltpu.HBM)
F32 = jnp.float32
BF16 = jnp.bfloat16


def bits_of(count):
    return [1 << i for i in range(count.bit_length() - 1)]


def reversed_bits(value, count):
    bits = bits_of(count)
    total = 0
    for low, high in zip(bits, bits[::-1]):
        total = total + jnp.where((value & low) != 0, high, 0)
    return total


def reversed_static(value, count):
    bits = bits_of(count)
    return sum(high for low, high in zip(bits, bits[::-1]) if value & low)


def swap(value, axis, mask):
    count = lax.axis_size(axis)
    return lax.ppermute(value, axis, [(i, i ^ mask) for i in range(count)])


def crossing(masks, first, second):
    pairs = []
    for i in range(2 * masks[-1]):
        quarter = i // masks[-2]
        inner = quarter in (first, second)
        pairs.append((i, i ^ ((first ^ second) * masks[-2] if inner else 1)))
    return pairs


def dot(left, right):
    return jnp.dot(left, right, preferred_element_type=F32)


def dot_nt(left, right):
    return lax.dot_general(left, right, (((1,), (1,)), ((), ())), preferred_element_type=F32)


def by_half(low, high):
    lane = lax.broadcasted_iota(jnp.int32, low.shape, low.ndim - 1)
    return jnp.where(lane < low.shape[-1] // 2, low, high)


def turned(value):
    return pltpu.roll(value.astype(F32), value.shape[-1] // 2, 1).astype(value.dtype)


def face_rows_of(inverse, slot, face):
    nodes = inverse.shape[1]
    part = nodes // NP
    layer = part // NP
    lower = []
    upper = []
    for a in range(NP):
        head = inverse[slot, a * part : a * part + 2 * layer, :].astype(F32)
        tail = inverse[slot, (a + 1) * part - 2 * layer : (a + 1) * part, :].astype(F32)
        lower.append(head[:layer])
        upper.append(tail[layer:])
    faces = jnp.concatenate(lower + upper, axis=0).astype(BF16)
    outflow = inverse[slot, nodes - face :, :]
    return jnp.concatenate([faces, outflow, outflow], axis=0)


def pair_maps(maps, coupling, slots, rows, face):
    outs = []
    for i, slot in enumerate(slots):
        full = dot_nt(coupling[slot], rows[i])
        full = jnp.concatenate([full[2 * face :], full[face : 2 * face], full[:face]], axis=0).astype(BF16)
        maps[i * 3 * face : (i + 1) * 3 * face, :] = full[:, : 2 * face]
        outs.append(full[:, 2 * face :])
    maps[2 * 3 * face :, :] = by_half(outs[0], outs[1])


def first_kernel(order_far, inverse_far, coupling_far, given_far, *refs):
    maps, rows, inverse_near, coupling_near, given_near = refs[:5]
    inverse, coupling, order, order_done, done, near_done = refs[5:]
    count = given_near.shape[0]
    face = coupling.shape[1] // 3
    first = pltpu.make_async_copy(order_far, order, order_done)
    first.start()
    copies = []
    for kind, (far, near) in enumerate(((inverse_far, inverse), (coupling_far, coupling))):
        for slot in range(count):
            copies.append(pltpu.make_async_copy(far.at[slot], near.at[slot], done.at[kind, slot]))
    for copy in copies:
        copy.start()
    first.wait()
    slots = [order[p] for p in range(count)]
    later = [
        pltpu.make_async_copy(given_far.at[slots[p]], given_near.at[p], near_done.at[0, p]) for p in range(count)
    ]
    for copy in later:
        copy.start()
    for copy in copies:
        copy.wait()
    for p in range(2, count):
        for kind, (held, near) in enumerate(((inverse, inverse_near), (coupling, coupling_near))):
            later.append(pltpu.make_async_copy(held.at[slots[p]], near.at[p - 2], near_done.at[kind + 1, p]))
            later[-1].start()
    values = []
    for p in range(2):
        values.append(face_rows_of(inverse, slots[p], face))
        rows[p] = values[p]
    pair_maps(maps, coupling, slots[:2], values, face)
    for copy in later:
        copy.wait()


def rest_kernel(place, early_rows, inverse, coupling, given, *refs):
    count, _, width = given.shape
    maps = refs[: count // 2 - 1]
    gains = refs[count // 2 - 1 : -1]
    gathered = refs[-1]
    face = coupling.shape[1] // 3
    groups = len(gains)
    share = width // groups
    rows = [face_rows_of(inverse, p, face) for p in range(count - 2)]
    for j, target in enumerate(maps):
        pair_maps(target, coupling, (2 * j, 2 * j + 1), rows[2 * j : 2 * j + 2], face)
    rows = [early_rows[0], early_rows[1]] + rows
    every = [dot(rows[p], given[p]).T for p in range(count)]
    tiles = [gain[:, : 2 * face] for gain in every]
    for p in range(0, count, 2):
        tiles.append(by_half(every[p][:, 2 * face :], every[p + 1][:, 2 * face :]))
    for m, tile in enumerate(tiles):
        gathered[m] = tile
    for rel in range(groups):
        at = pl.multiple_of((place[0] ^ rel) * share, share)
        for m in range(len(tiles)):
            gains[rel][m] = gathered[m, pl.ds(at, share), :].astype(BF16)


def unpack_maps(map_refs, weights, face):
    for j, refs in enumerate(map_refs):
        for pos, ref in enumerate(refs):
            outs = ref[2 * 3 * face :, :]
            other = turned(outs)
            for i in range(2):
                sides = ref[i * 3 * face : (i + 1) * 3 * face, :]
                full = jnp.concatenate([sides, by_half(outs, other) if i == 0 else by_half(other, outs)], axis=1)
                weights[pos, 2 * j + i] = full


def unpack_gains(gain_refs, gains, count):
    for rel, ref in enumerate(gain_refs):
        for p in range(count):
            outs = ref[count + p // 2]
            other = turned(outs)
            outs = by_half(outs, other) if p % 2 == 0 else by_half(other, outs)
            gains[reversed_static(rel, len(gain_refs)), p] = jnp.concatenate([ref[p], outs], axis=1)


def neighbours(me, pos, groups):
    own = me ^ reversed_bits(pos, groups)
    below = jnp.where(own > 0, reversed_bits(((own - 1) & (groups - 1)) ^ me, groups), groups)
    above = jnp.where(own < groups - 1, reversed_bits(((own + 1) & (groups - 1)) ^ me, groups), groups)
    return below, above


def read_lags(me, states, lags, groups, count):
    def read(pos):
        below, above = neighbours(me, pos, groups)
        for p in range(count):
            lags[pos, p] = by_half(states[above, p], states[below, p])

    over(groups, read)


def over(count, body, limit=4):
    if count <= limit:
        for i in range(count):
            body(i)
    else:

        def step(i, carry):
            body(i)
            return carry

        lax.fori_loop(0, count, step, 0)


def split_trace(out):
    high = out.astype(BF16)
    return by_half(high, (out - high.astype(F32)).astype(BF16)), high


def run_chains(chosen, entries, lags, weights, gains, states, count, face, first):
    share = gains.shape[2]
    outs = [[] for _ in chosen]
    for p in range(count):
        for i, pos in enumerate(chosen):
            rows = entries[i].shape[0]
            left = entries[i]
            own = weights[pos, p, 2 * face :]
            right = jnp.concatenate([own, own], axis=0)
            if not first:
                left = jnp.concatenate([lags[pos, p, :rows], left], axis=1)
                right = jnp.concatenate([weights[pos, p, : 2 * face], right], axis=0)
            result = dot(left, right)
            head = result[:share] + gains[pos, p].astype(F32)
            result = head if rows == share else jnp.concatenate([head, result[share:]], axis=0)
            states[pos, p, :rows] = result[:, : 2 * face].astype(BF16)
            outs[i].append(result[:, 2 * face :])
        if p < count - 1:
            entries = [split_trace(o[p])[0] for o in outs]
    return outs


def respond_kernel(place, *refs, groups, count, face):
    pairs = count // 2
    map_refs = [refs[j * groups : (j + 1) * groups] for j in range(pairs)]
    gain_refs = refs[pairs * groups : (pairs + 1) * groups]
    response, offset, weights, gains, states, lags, unit = refs[(pairs + 1) * groups :]
    me = place[0]
    half = groups // 2
    share = gains.shape[2]
    unpack_maps(map_refs, weights, face)
    unpack_gains(gain_refs, gains, count)
    states[groups] = jnp.zeros_like(states[groups])
    row = lax.broadcasted_iota(jnp.int32, unit.shape[1:], 0) - share
    lane = lax.broadcasted_iota(jnp.int32, unit.shape[1:], 1)
    for pos in range(half):
        hit = jnp.logical_and(lane < face, row == lane + pos * face)
        unit[pos] = jnp.where(hit, 1.0, 0.0).astype(BF16)

    def sweep(k, parity, first=False):
        if not first:
            read_lags(me, states, lags, groups, count)

        def block(t):
            live = [2 * t + half * parity, 2 * t + 1 + half * parity]
            bare = [2 * t + half * (1 - parity), 2 * t + 1 + half * (1 - parity)]
            entries = [unit[pos] if first else jnp.zeros_like(unit[pos]) for pos in live]
            entries += [jnp.zeros((share, 2 * face), BF16)] * 2
            chains = run_chains(live + bare, entries, lags, weights, gains, states, count, face, first)
            ends = [outs[-1] for outs in chains]
            at = pl.ds(pl.multiple_of(t * 2 * face, 2 * face), 2 * face)
            full = by_half(ends[0], ends[1])
            response[k, :, at] = full[share:].astype(BF16)
            for target, tile in ((parity, full[:share]), (1 - parity, by_half(ends[2], ends[3]))):
                offset[k, target * share : (target + 1) * share, at] = tile.astype(BF16)

        over(groups // 4, block, 1)

    def both(i, carry):
        sweep(2 * i, 0)
        sweep(2 * i + 1, 1)
        return carry

    sweep(0, 0, True)
    sweep(1, 1)
    lax.fori_loop(1, SWEEPS // 2, both, 0)


def pick(flag, first, second):
    return jnp.where(flag != 0, first, second)


def pair_offset_kernel(line, own, other, got, got_other, own_offset, got_offset, offset, *, mask):
    down = (line[0] // mask) % 2
    share = own_offset.shape[1] // 2
    maps = [
        (pick(down, own[k], got[k]), pick(down, other[k], got_other[k])) for k in range(SWEEPS)
    ]
    values = []
    for k in range(SWEEPS):
        both = zip(halves_of(got_offset, k), halves_of(own_offset, k))
        values.append([pick(down, a, b) for a, b in both])
    for k in range(SWEEPS):
        both = zip(halves_of(own_offset, k), halves_of(got_offset, k))
        added = [pick(down, a, b).astype(F32) for a, b in both]
        for target, total in enumerate(moved_by(values, maps, k)):
            offset[k, target * share : (target + 1) * share] = (total + added[target]).astype(BF16)


def pair_map_kernel(line, own, other, got, got_other, response, *, mask):
    down = (line[0] // mask) % 2
    after = [
        (pick(down, own[k], got[k]), pick(down, other[k], got_other[k])) for k in range(SWEEPS)
    ]
    before = [pick(down, got[k], own[k]) for k in range(SWEEPS)]
    for m in range(SWEEPS):
        stack = jnp.concatenate([after[d][(m + d) % 2] for d in range(m + 1)], axis=0)
        left = jnp.concatenate([before[m - d] for d in range(m + 1)], axis=1)
        response[m] = dot(left, stack).astype(BF16)


def halves_of(ref, k):
    share = ref.shape[1] // 2
    return ref[k, :share], ref[k, share:]


def moved_by(values, maps, k):
    pair = []
    for target in (0, 1):
        stack = jnp.concatenate([maps[d][(target + d) % 2] for d in range(k + 1)], axis=0)
        left = jnp.concatenate([values[k - d][(target + d) % 2] for d in range(k + 1)], axis=1)
        pair.append(dot(left, stack))
    return pair


def add_own(values, maps, own):
    moved = []
    for k in range(SWEEPS):
        pair = zip(moved_by(values, maps, k), own[k])
        moved.append([(total + added.astype(F32)).astype(BF16) for total, added in pair])
    return moved


def put_halves(ref, values):
    share = ref.shape[1] // 2
    for k in range(SWEEPS):
        for target in (0, 1):
            ref[k, target * share : (target + 1) * share] = values[k][target]


def opening_kernel(even, odd, entry, own, opened):
    maps = [(even[k], odd[k]) for k in range(SWEEPS)]
    values = [halves_of(entry, k) for k in range(SWEEPS)]
    put_halves(opened, add_own(values, maps, [halves_of(own, k) for k in range(SWEEPS)]))


def join_kernel(line, own, other, got, got_other, own_offset, got_offset, near, across, joined, *, mask):
    down = (line[0] // mask) % 2
    values = [
        [pick(down, a, b) for a, b in zip(halves_of(near, k), halves_of(across, k))] for k in range(SWEEPS)
    ]
    for turn in (down, 1 - down):
        maps = [(pick(turn, got[k], own[k]), pick(turn, got_other[k], other[k])) for k in range(SWEEPS)]
        added = [
            [pick(turn, a, b) for a, b in zip(halves_of(got_offset, k), halves_of(own_offset, k))]
            for k in range(SWEEPS)
        ]
        values = add_own(values, maps, added)
    put_halves(joined, values)


def resolve_kernel(place, line, *refs, groups, count, face, masks):
    weights, gains, near, across, second, third, ahead_even, ahead_odd = refs[:8]
    levels = len(masks) - 2
    lower = refs[8 : 8 + 3 * levels]
    wanted = refs[8 + 3 * levels : 8 + 3 * levels + groups]
    states, lags, inflows = refs[8 + 3 * levels + groups :]
    me = place[0]
    half = groups // 2
    states[groups] = jnp.zeros_like(states[groups])
    flags = [(line[0] // mask) % 2 for mask in masks]
    maps = [(ahead_even[k], ahead_odd[k]) for k in range(SWEEPS)]
    given = [halves_of(third, k) for k in range(SWEEPS)]
    values = []
    for k in range(SWEEPS):
        pair = []
        for target, total in enumerate(moved_by(given, maps, k)):
            own = pick(flags[-3], halves_of(near, k)[target], halves_of(across, k)[target])
            last = (total + own.astype(F32)).astype(BF16)
            upper = pick(flags[-2], last, halves_of(second, k)[target])
            pair.append(pick(flags[-1], upper, pick(flags[-2], own, jnp.zeros_like(own))))
        values.append(pair)
    for level in range(levels - 1, -1, -1):
        even, odd, offset = lower[3 * level : 3 * level + 3]
        maps = [(even[k], odd[k]) for k in range(SWEEPS)]
        moved = []
        for k in range(SWEEPS):
            pair = []
            for target, total in enumerate(moved_by(values, maps, k)):
                total = total + halves_of(offset, k)[target].astype(F32)
                pair.append(pick(flags[level], total.astype(BF16), values[k][target]))
            moved.append(pair)
        values = moved
    blank = jnp.zeros((values[0][0].shape[0], 2 * face), BF16)
    for k in range(SWEEPS):
        for pos in range(groups):
            tile = (pos % half) // 2
            both = values[k][pos // half][:, tile * 2 * face : (tile + 1) * 2 * face]
            inflows[k, pos] = by_half(both if pos % 2 == 0 else turned(both), blank)

    def chains(k, t, stage):
        chosen = tuple(4 * t + i for i in range(4))
        entries = [inflows[k, pos] for pos in chosen]
        every = [[entry] for entry in entries]
        for p in range(count - (stage == 2)):
            for i, pos in enumerate(chosen):
                left = every[i][p][:, :face]
                right = weights[pos, p, 2 * face :]
                added = gains[pos, p].astype(F32)
                if stage > 0:
                    left = jnp.concatenate([lags[pos, p], left], axis=1)
                    right = weights[pos, p]
                if stage == 2:
                    right = right[:, 2 * face :]
                    added = added[:, 2 * face :]
                result = dot(left, right) + added
                if stage < 2:
                    states[pos, p] = result[:, : 2 * face].astype(BF16)
                    result = result[:, 2 * face :]
                every[i].append(result.astype(BF16))
        return chosen, every

    def blocks(k, stage):
        over(groups // 4, lambda t: chains(k, t, stage), 1)

    blocks(0, 0)

    def sweep(k, carry):
        read_lags(me, states, lags, groups, count)
        blocks(k, 1)
        return carry

    lax.fori_loop(1, SWEEPS - 1, sweep, 0)
    read_lags(me, states, lags, groups, count)
    for t in range(groups // 4):
        chosen, every = chains(SWEEPS - 1, t, 2)
        for i, pos in enumerate(chosen):
            target = wanted[reversed_static(pos, groups)]
            traces = every[i]
            for p in range(count):
                target[p] = lags[pos, p]
            target[count] = by_half(traces[0], traces[count - 1])
            for m in range(1, count // 2):
                target[count + m] = by_half(traces[2 * m - 1], traces[2 * m])


def final_kernel(place, order, inverse, coupling, given, *refs):
    wanted = refs[:-4]
    placed, solved, gathered, done = refs[-4:]
    count, nodes, width = given.shape
    face = coupling.shape[1] // 3
    share = width // len(wanted)
    for rel, ref in enumerate(wanted):
        at = pl.multiple_of((place[0] ^ rel) * share, share)
        for m in range(ref.shape[0]):
            gathered[m, pl.ds(at, share), :] = ref[m].astype(gathered.dtype)
    blank = jnp.zeros((face, nodes), BF16)
    copies = []
    for p in range(count):
        slot = order[p]
        rows = coupling[slot]
        second = p == count - 1 or (p > 0 and p % 2 == 0)
        tile = 0 if p == count - 1 else (p + 1) // 2
        pair = [blank, rows[:face]] if second else [rows[:face], blank]
        sides = jnp.concatenate([rows[2 * face :], rows[face : 2 * face]] + pair, axis=0)
        traces = jnp.concatenate([gathered[p], gathered[count + tile]], axis=1).astype(BF16)
        source = given[slot].astype(F32) + dot(traces, sides).T
        solved[p] = dot(inverse[slot], source.astype(BF16)).astype(BF16)
        copies.append(pltpu.make_async_copy(solved.at[p], placed.at[slot], done.at[p]))
        copies[p].start()
    for copy in copies:
        copy.wait()


def gather_list(value, axis):
    values = [value]
    for mask in bits_of(lax.axis_size(axis))[::-1]:
        values = values + [swap(v, axis, mask) for v in values]
    return values


def exchange(values, axis):
    return [v if rel == 0 else swap(v, axis, rel) for rel, v in enumerate(values)]


def call(kernel, outs, scratch, scalars, arrays, far=0, others=(), space=VMEM):
    def size(shape, kind):
        total = jnp.dtype(kind).itemsize
        for extent in shape:
            total *= extent
        return total

    held = sum(size(o.shape, o.dtype) for o in outs) + sum(size(a.shape, a.dtype) for a in arrays)
    held += sum(size(shape, kind) for shape, kind in scratch)
    return pl.pallas_call(
        kernel,
        out_shape=outs,
        in_specs=[SMEM] * len(scalars) + [VMEM] * (len(arrays) - far) + [HBM] * far,
        out_specs=[space] * len(outs),
        scratch_shapes=[*[pltpu.VMEM(shape, kind) for shape, kind in scratch], *others],
        compiler_params=pltpu.CompilerParams(vmem_limit_bytes=min(held + (3 << 20), 60 << 20)),
    )(*scalars, *arrays)


def shards(right_sides, inverse, coupling, sweep_order):
    given = right_sides[0, 0]
    inverse = inverse[0, 0]
    order = sweep_order[0, 0]
    count, nodes, width = given.shape
    face = coupling.shape[4]
    coupling = coupling[0, 0].reshape(count, 3 * face, nodes)
    groups = lax.axis_size("span")
    share = width // groups
    half = groups // 2
    place = lax.axis_index("span").astype(jnp.int32).reshape(1)
    line = lax.axis_index("stream").astype(jnp.int32).reshape(1)
    masks = bits_of(lax.axis_size("stream"))
    tiles = count + count // 2
    shape = jax.ShapeDtypeStruct
    far = [pltpu.with_memory_space_constraint(a, pltpu.HBM) for a in (order, inverse, coupling, given)]
    maps, *near = call(
        first_kernel,
        [
            shape((3 * 3 * face, 2 * face), BF16),
            shape((2, 4 * face, nodes), BF16),
            shape((count - 2,) + inverse.shape[1:], BF16),
            shape((count - 2,) + coupling.shape[1:], BF16),
            shape(given.shape, BF16),
        ],
        [(inverse.shape, BF16), (coupling.shape, BF16)],
        [],
        far,
        4,
        (
            pltpu.SMEM(order.shape, order.dtype),
            pltpu.SemaphoreType.DMA,
            pltpu.SemaphoreType.DMA((2, count)),
            pltpu.SemaphoreType.DMA((3, count)),
        ),
    )
    all_maps = gather_list(maps, "span")
    outs = call(
        rest_kernel,
        [shape(maps.shape, BF16)] * (count // 2 - 1) + [shape((tiles, share, 2 * face), BF16)] * groups,
        [((tiles, width, 2 * face), F32)],
        [place],
        near,
    )
    gains = outs[count // 2 - 1 :]
    for maps in outs[: count // 2 - 1]:
        all_maps += gather_list(maps, "span")
    gains = exchange(gains, "span")
    sizes = dict(groups=groups, count=count, face=face)
    wide = half * face
    response, offset, weights, gains = call(
        functools.partial(respond_kernel, **sizes),
        [
            shape((SWEEPS, wide, wide), BF16),
            shape((SWEEPS, 2 * share, wide), BF16),
            shape((groups, count, 3 * face, 4 * face), BF16),
            shape((groups, count, share, 4 * face), BF16),
        ],
        [
            ((groups + 1, count, share + wide, 2 * face), BF16),
            ((groups, count, share + wide, 2 * face), BF16),
            ((half, share + wide, 2 * face), BF16),
        ],
        [place],
        [*all_maps, *gains],
    )
    levels = []
    for mask in masks[:-2]:
        got_offset = swap(offset, "stream", mask)
        other = swap(response, "span", 1)
        got = swap(response, "stream", mask)
        got_other = swap(got, "span", 1)
        levels += [got, got_other, got_offset]
        arrays = [response, other, got, got_other]
        same = shape(offset.shape, BF16)
        if mask == masks[-3]:
            (opened,) = call(opening_kernel, [same], [], [], [response, other, got_offset, offset])
            near = swap(opened, "stream", masks[-2])
            across = swap(opened, "stream", masks[-2] | mask)
            joining = arrays + [offset, got_offset, near, across]
        else:
            (offset,) = call(
                functools.partial(pair_offset_kernel, mask=mask), [same], [], [line], arrays + [offset, got_offset]
            )
        (response,) = call(
            functools.partial(pair_map_kernel, mask=mask), [shape(response.shape, BF16)], [], [line], arrays
        )
    ahead_even = swap(response, "stream", masks[-2])
    (joined,) = call(functools.partial(join_kernel, mask=masks[-3]), [same], [], [line], joining)
    second = lax.ppermute(joined, "stream", crossing(masks, 1, 2))
    third = lax.ppermute(joined, "stream", crossing(masks, 1, 3))
    ahead_odd = swap(ahead_even, "span", 1)
    wanted = call(
        functools.partial(resolve_kernel, masks=masks, **sizes),
        [shape((tiles, share, 2 * face), BF16)] * groups,
        [
            ((groups + 1, count, share, 2 * face), BF16),
            ((groups, count, share, 2 * face), BF16),
            ((SWEEPS, groups, share, 2 * face), BF16),
        ],
        [place, line],
        [weights, gains, near, across, second, third, ahead_even, ahead_odd, *levels],
    )
    wanted = exchange(wanted, "span")
    (placed,) = call(
        final_kernel,
        [shape((count, nodes, width), BF16)],
        [((count, nodes, width), BF16), ((tiles, width, 2 * face), BF16 if share % 16 == 0 else F32)],
        [place, order],
        [inverse, coupling, given, *wanted],
        0,
        (pltpu.SemaphoreType.DMA((count,)),),
        HBM,
    )
    return placed[None, None]


def solution(mesh):
    in_specs = (
        P("stream", "span", None, None, None),
        P("stream", "span", None, None, None),
        P("stream", "span", None, None, None, None),
        P("stream", "span", None),
    )
    out_specs = P("stream", "span", None, None, None)
    return jax.shard_map(shards, mesh=mesh, in_specs=in_specs, out_specs=out_specs, check_vma=False)
```

```python
import functools

import jax
import jax.numpy as jnp
from jax import lax
from jax.experimental import pallas as pl
from jax.experimental.pallas import tpu as pltpu
from jax.sharding import PartitionSpec as P

NP = 8
SWEEPS = 6
VMEM = pl.BlockSpec(memory_space=pltpu.VMEM)
SMEM = pl.BlockSpec(memory_space=pltpu.SMEM)
HBM = pl.BlockSpec(memory_space=pltpu.HBM)
F32 = jnp.float32
BF16 = jnp.bfloat16


def bits_of(count):
    return [1 << i for i in range(count.bit_length() - 1)]


def reversed_bits(value, count):
    bits = bits_of(count)
    total = 0
    for low, high in zip(bits, bits[::-1]):
        total = total + jnp.where((value & low) != 0, high, 0)
    return total


def reversed_static(value, count):
    bits = bits_of(count)
    return sum(high for low, high in zip(bits, bits[::-1]) if value & low)


def swap(value, axis, mask):
    count = lax.axis_size(axis)
    return lax.ppermute(value, axis, [(i, i ^ mask) for i in range(count)])


def crossing(masks, first, second):
    pairs = []
    for i in range(2 * masks[-1]):
        quarter = i // masks[-2]
        inner = quarter in (first, second)
        pairs.append((i, i ^ ((first ^ second) * masks[-2] if inner else 1)))
    return pairs


def dot(left, right):
    return jnp.dot(left, right, preferred_element_type=F32)


def dot_nt(left, right):
    return lax.dot_general(left, right, (((1,), (1,)), ((), ())), preferred_element_type=F32)


def by_half(low, high):
    lane = lax.broadcasted_iota(jnp.int32, low.shape, low.ndim - 1)
    return jnp.where(lane < low.shape[-1] // 2, low, high)


def turned(value):
    return pltpu.roll(value.astype(F32), value.shape[-1] // 2, 1).astype(value.dtype)


def face_rows_of(inverse, slot, face):
    nodes = inverse.shape[1]
    part = nodes // NP
    layer = part // NP
    lower = []
    upper = []
    for a in range(NP):
        head = inverse[slot, a * part : a * part + 2 * layer, :].astype(F32)
        tail = inverse[slot, (a + 1) * part - 2 * layer : (a + 1) * part, :].astype(F32)
        lower.append(head[:layer])
        upper.append(tail[layer:])
    faces = jnp.concatenate(lower + upper, axis=0).astype(BF16)
    outflow = inverse[slot, nodes - face :, :]
    return jnp.concatenate([faces, outflow, outflow], axis=0)


def pair_maps(maps, coupling, slots, rows, face):
    outs = []
    for i, slot in enumerate(slots):
        full = dot_nt(coupling[slot], rows[i])
        full = jnp.concatenate([full[2 * face :], full[face : 2 * face], full[:face]], axis=0).astype(BF16)
        maps[i * 3 * face : (i + 1) * 3 * face, :] = full[:, : 2 * face]
        outs.append(full[:, 2 * face :])
    maps[2 * 3 * face :, :] = by_half(outs[0], outs[1])


def first_kernel(order_far, inverse_far, coupling_far, given_far, *refs):
    maps, rows, coupling_near, given_near = refs[:4]
    inverse, coupling, order, order_done, done, near_done = refs[4:]
    count = given_near.shape[0]
    face = coupling.shape[1] // 3
    first = pltpu.make_async_copy(order_far, order, order_done)
    first.start()
    copies = []
    for kind, (far, near) in enumerate(((inverse_far, inverse), (coupling_far, coupling))):
        for slot in range(count):
            copies.append(pltpu.make_async_copy(far.at[slot], near.at[slot], done.at[kind, slot]))
    for copy in copies:
        copy.start()
    first.wait()
    slots = [order[p] for p in range(count)]
    later = [
        pltpu.make_async_copy(given_far.at[slots[p]], given_near.at[p], near_done.at[p]) for p in range(count)
    ]
    for copy in later:
        copy.start()
    for copy in copies:
        copy.wait()
    values = [face_rows_of(inverse, slots[p], face) for p in range(2)]
    pair_maps(maps, coupling, slots[:2], values, face)
    for p in range(2, count):
        values.append(face_rows_of(inverse, slots[p], face))
        coupling_near[p - 2] = coupling[slots[p]]
    for p in range(count):
        rows[p] = values[p]
    for copy in later:
        copy.wait()


def rest_kernel(place, rows, coupling, given, *refs):
    count, _, width = given.shape
    maps = refs[: count // 2 - 1]
    gains = refs[count // 2 - 1 : -1]
    gathered = refs[-1]
    face = coupling.shape[1] // 3
    groups = len(gains)
    share = width // groups
    rows = [rows[p] for p in range(count)]
    for j, target in enumerate(maps):
        pair_maps(target, coupling, (2 * j, 2 * j + 1), rows[2 * j + 2 : 2 * j + 4], face)
    every = [dot(rows[p], given[p]).T for p in range(count)]
    tiles = [gain[:, : 2 * face] for gain in every]
    for p in range(0, count, 2):
        tiles.append(by_half(every[p][:, 2 * face :], every[p + 1][:, 2 * face :]))
    for m, tile in enumerate(tiles):
        gathered[m] = tile
    for rel in range(groups):
        at = pl.multiple_of((place[0] ^ rel) * share, share)
        for m in range(len(tiles)):
            gains[rel][m] = gathered[m, pl.ds(at, share), :].astype(BF16)


def unpack_maps(map_refs, weights, face):
    for j, refs in enumerate(map_refs):
        for pos, ref in enumerate(refs):
            outs = ref[2 * 3 * face :, :]
            other = turned(outs)
            for i in range(2):
                sides = ref[i * 3 * face : (i + 1) * 3 * face, :]
                full = jnp.concatenate([sides, by_half(outs, other) if i == 0 else by_half(other, outs)], axis=1)
                weights[pos, 2 * j + i] = full


def unpack_gains(gain_refs, gains, count):
    for rel, ref in enumerate(gain_refs):
        for p in range(count):
            outs = ref[count + p // 2]
            other = turned(outs)
            outs = by_half(outs, other) if p % 2 == 0 else by_half(other, outs)
            gains[reversed_static(rel, len(gain_refs)), p] = jnp.concatenate([ref[p], outs], axis=1)


def neighbours(me, pos, groups):
    own = me ^ reversed_bits(pos, groups)
    below = jnp.where(own > 0, reversed_bits(((own - 1) & (groups - 1)) ^ me, groups), groups)
    above = jnp.where(own < groups - 1, reversed_bits(((own + 1) & (groups - 1)) ^ me, groups), groups)
    return below, above


def read_lags(me, states, lags, groups, count):
    def read(pos):
        below, above = neighbours(me, pos, groups)
        for p in range(count):
            lags[pos, p] = by_half(states[above, p], states[below, p])

    over(groups, read)


def over(count, body, limit=4):
    if count <= limit:
        for i in range(count):
            body(i)
    else:

        def step(i, carry):
            body(i)
            return carry

        lax.fori_loop(0, count, step, 0)


def split_trace(out):
    high = out.astype(BF16)
    return by_half(high, (out - high.astype(F32)).astype(BF16)), high


def run_chains(chosen, entries, lags, weights, gains, states, count, face, first):
    share = gains.shape[2]
    outs = [[] for _ in chosen]
    for p in range(count):
        for i, pos in enumerate(chosen):
            rows = entries[i].shape[0]
            if p == 0 and not first:
                result = dot(lags[pos, p, :rows], weights[pos, p, : 2 * face])
            else:
                left = entries[i]
                own = weights[pos, p, 2 * face :]
                right = jnp.concatenate([own, own], axis=0)
                if not first:
                    left = jnp.concatenate([lags[pos, p, :rows], left], axis=1)
                    right = jnp.concatenate([weights[pos, p, : 2 * face], right], axis=0)
                result = dot(left, right)
            head = result[:share] + gains[pos, p].astype(F32)
            result = head if rows == share else jnp.concatenate([head, result[share:]], axis=0)
            states[pos, p, :rows] = result[:, : 2 * face].astype(BF16)
            outs[i].append(result[:, 2 * face :])
        if p < count - 1:
            entries = [split_trace(o[p])[0] for o in outs]
    return outs


def respond_kernel(place, *refs, groups, count, face):
    pairs = count // 2
    map_refs = [refs[j * groups : (j + 1) * groups] for j in range(pairs)]
    gain_refs = refs[pairs * groups : (pairs + 1) * groups]
    response, offset, weights, gains, states, lags, unit = refs[(pairs + 1) * groups :]
    me = place[0]
    half = groups // 2
    share = gains.shape[2]
    unpack_maps(map_refs, weights, face)
    unpack_gains(gain_refs, gains, count)
    states[groups] = jnp.zeros_like(states[groups])
    row = lax.broadcasted_iota(jnp.int32, unit.shape[1:], 0) - share
    lane = lax.broadcasted_iota(jnp.int32, unit.shape[1:], 1)
    for pos in range(half):
        hit = jnp.logical_and(lane < face, row == lane + pos * face)
        unit[pos] = jnp.where(hit, 1.0, 0.0).astype(BF16)

    def sweep(k, parity, first=False):
        if not first:
            read_lags(me, states, lags, groups, count)

        def block(t):
            live = [2 * t + half * parity, 2 * t + 1 + half * parity]
            bare = [2 * t + half * (1 - parity), 2 * t + 1 + half * (1 - parity)]
            entries = [unit[pos] if first else jnp.zeros_like(unit[pos]) for pos in live]
            entries += [jnp.zeros((share, 2 * face), BF16)] * 2
            chains = run_chains(live + bare, entries, lags, weights, gains, states, count, face, first)
            ends = [outs[-1] for outs in chains]
            at = pl.ds(pl.multiple_of(t * 2 * face, 2 * face), 2 * face)
            full = by_half(ends[0], ends[1])
            response[k, :, at] = full[share:].astype(BF16)
            for target, tile in ((parity, full[:share]), (1 - parity, by_half(ends[2], ends[3]))):
                offset[k, target * share : (target + 1) * share, at] = tile.astype(BF16)

        over(groups // 4, block, 1)

    def both(i, carry):
        sweep(2 * i, 0)
        sweep(2 * i + 1, 1)
        return carry

    sweep(0, 0, True)
    sweep(1, 1)
    lax.fori_loop(1, SWEEPS // 2, both, 0)


def pick(flag, first, second):
    return jnp.where(flag != 0, first, second)


def pair_offset_kernel(line, own, other, got, got_other, own_offset, got_offset, offset, *, mask):
    down = (line[0] // mask) % 2
    share = own_offset.shape[1] // 2
    maps = [
        (pick(down, own[k], got[k]), pick(down, other[k], got_other[k])) for k in range(SWEEPS)
    ]
    values = []
    for k in range(SWEEPS):
        both = zip(halves_of(got_offset, k), halves_of(own_offset, k))
        values.append([pick(down, a, b) for a, b in both])
    for k in range(SWEEPS):
        both = zip(halves_of(own_offset, k), halves_of(got_offset, k))
        added = [pick(down, a, b).astype(F32) for a, b in both]
        for target, total in enumerate(moved_by(values, maps, k)):
            offset[k, target * share : (target + 1) * share] = (total + added[target]).astype(BF16)


def pair_map_kernel(line, own, other, got, got_other, response, *, mask):
    down = (line[0] // mask) % 2
    after = [
        (pick(down, own[k], got[k]), pick(down, other[k], got_other[k])) for k in range(SWEEPS)
    ]
    before = [pick(down, got[k], own[k]) for k in range(SWEEPS)]
    for m in range(SWEEPS):
        stack = jnp.concatenate([after[d][(m + d) % 2] for d in range(m + 1)], axis=0)
        left = jnp.concatenate([before[m - d] for d in range(m + 1)], axis=1)
        response[m] = dot(left, stack).astype(BF16)


def halves_of(ref, k):
    share = ref.shape[1] // 2
    return ref[k, :share], ref[k, share:]


def moved_by(values, maps, k):
    pair = []
    for target in (0, 1):
        stack = jnp.concatenate([maps[d][(target + d) % 2] for d in range(k + 1)], axis=0)
        left = jnp.concatenate([values[k - d][(target + d) % 2] for d in range(k + 1)], axis=1)
        pair.append(dot(left, stack))
    return pair


def add_own(values, maps, own):
    moved = []
    for k in range(SWEEPS):
        pair = zip(moved_by(values, maps, k), own[k])
        moved.append([(total + added.astype(F32)).astype(BF16) for total, added in pair])
    return moved


def put_halves(ref, values):
    share = ref.shape[1] // 2
    for k in range(SWEEPS):
        for target in (0, 1):
            ref[k, target * share : (target + 1) * share] = values[k][target]


def opening_kernel(even, odd, entry, own, opened):
    maps = [(even[k], odd[k]) for k in range(SWEEPS)]
    values = [halves_of(entry, k) for k in range(SWEEPS)]
    put_halves(opened, add_own(values, maps, [halves_of(own, k) for k in range(SWEEPS)]))


def join_kernel(line, own, other, got, got_other, own_offset, got_offset, near, across, joined, *, mask):
    down = (line[0] // mask) % 2
    values = [
        [pick(down, a, b) for a, b in zip(halves_of(near, k), halves_of(across, k))] for k in range(SWEEPS)
    ]
    for turn in (down, 1 - down):
        maps = [(pick(turn, got[k], own[k]), pick(turn, got_other[k], other[k])) for k in range(SWEEPS)]
        added = [
            [pick(turn, a, b) for a, b in zip(halves_of(got_offset, k), halves_of(own_offset, k))]
            for k in range(SWEEPS)
        ]
        values = add_own(values, maps, added)
    put_halves(joined, values)


def resolve_kernel(place, line, *refs, groups, count, face, masks):
    weights, gains, near, across, second, third, ahead_even, ahead_odd = refs[:8]
    levels = len(masks) - 2
    lower = refs[8 : 8 + 3 * levels]
    wanted = refs[8 + 3 * levels : 8 + 3 * levels + groups]
    states, lags, inflows = refs[8 + 3 * levels + groups :]
    me = place[0]
    half = groups // 2
    states[groups] = jnp.zeros_like(states[groups])
    flags = [(line[0] // mask) % 2 for mask in masks]
    maps = [(ahead_even[k], ahead_odd[k]) for k in range(SWEEPS)]
    given = [halves_of(third, k) for k in range(SWEEPS)]
    values = []
    for k in range(SWEEPS):
        pair = []
        for target, total in enumerate(moved_by(given, maps, k)):
            own = pick(flags[-3], halves_of(near, k)[target], halves_of(across, k)[target])
            last = (total + own.astype(F32)).astype(BF16)
            upper = pick(flags[-2], last, halves_of(second, k)[target])
            pair.append(pick(flags[-1], upper, pick(flags[-2], own, jnp.zeros_like(own))))
        values.append(pair)
    for level in range(levels - 1, -1, -1):
        even, odd, offset = lower[3 * level : 3 * level + 3]
        maps = [(even[k], odd[k]) for k in range(SWEEPS)]
        moved = []
        for k in range(SWEEPS):
            pair = []
            for target, total in enumerate(moved_by(values, maps, k)):
                total = total + halves_of(offset, k)[target].astype(F32)
                pair.append(pick(flags[level], total.astype(BF16), values[k][target]))
            moved.append(pair)
        values = moved
    blank = jnp.zeros((values[0][0].shape[0], 2 * face), BF16)
    for k in range(SWEEPS):
        for pos in range(groups):
            tile = (pos % half) // 2
            both = values[k][pos // half][:, tile * 2 * face : (tile + 1) * 2 * face]
            inflows[k, pos] = by_half(both if pos % 2 == 0 else turned(both), blank)

    def chains(k, t, stage):
        chosen = tuple(4 * t + i for i in range(4))
        entries = [inflows[k, pos] for pos in chosen]
        every = [[entry] for entry in entries]
        for p in range(count - (stage == 2)):
            for i, pos in enumerate(chosen):
                left = every[i][p][:, :face]
                right = weights[pos, p, 2 * face :]
                added = gains[pos, p].astype(F32)
                if stage > 0:
                    left = jnp.concatenate([lags[pos, p], left], axis=1)
                    right = weights[pos, p]
                if stage == 2:
                    right = right[:, 2 * face :]
                    added = added[:, 2 * face :]
                result = dot(left, right) + added
                if stage < 2:
                    states[pos, p] = result[:, : 2 * face].astype(BF16)
                    result = result[:, 2 * face :]
                every[i].append(result.astype(BF16))
        return chosen, every

    def blocks(k, stage):
        over(groups // 4, lambda t: chains(k, t, stage), 1)

    blocks(0, 0)

    def sweep(k, carry):
        read_lags(me, states, lags, groups, count)
        blocks(k, 1)
        return carry

    lax.fori_loop(1, SWEEPS - 1, sweep, 0)
    read_lags(me, states, lags, groups, count)
    for t in range(groups // 4):
        chosen, every = chains(SWEEPS - 1, t, 2)
        for i, pos in enumerate(chosen):
            target = wanted[reversed_static(pos, groups)]
            traces = every[i]
            for p in range(count):
                target[p] = lags[pos, p]
            target[count] = by_half(traces[0], traces[count - 1])
            for m in range(1, count // 2):
                target[count + m] = by_half(traces[2 * m - 1], traces[2 * m])


def final_kernel(place, order, inverse, coupling, given, *refs):
    wanted = refs[:-4]
    placed, solved, gathered, done = refs[-4:]
    count, nodes, width = given.shape
    face = coupling.shape[1] // 3
    share = width // len(wanted)
    for rel, ref in enumerate(wanted):
        at = pl.multiple_of((place[0] ^ rel) * share, share)
        for m in range(ref.shape[0]):
            gathered[m, pl.ds(at, share), :] = ref[m].astype(gathered.dtype)
    blank = jnp.zeros((face, nodes), BF16)
    copies = []
    for p in range(count):
        slot = order[p]
        rows = coupling[slot]
        second = p == count - 1 or (p > 0 and p % 2 == 0)
        tile = 0 if p == count - 1 else (p + 1) // 2
        pair = [blank, rows[:face]] if second else [rows[:face], blank]
        sides = jnp.concatenate([rows[2 * face :], rows[face : 2 * face]] + pair, axis=0)
        traces = jnp.concatenate([gathered[p], gathered[count + tile]], axis=1).astype(BF16)
        source = given[slot].astype(F32) + dot(traces, sides).T
        solved[p] = dot(inverse[slot], source.astype(BF16)).astype(BF16)
        copies.append(pltpu.make_async_copy(solved.at[p], placed.at[slot], done.at[p]))
        copies[p].start()
    for copy in copies:
        copy.wait()


def gather_list(value, axis):
    values = [value]
    for mask in bits_of(lax.axis_size(axis))[::-1]:
        values = values + [swap(v, axis, mask) for v in values]
    return values


def exchange(values, axis):
    return [v if rel == 0 else swap(v, axis, rel) for rel, v in enumerate(values)]


def call(kernel, outs, scratch, scalars, arrays, far=0, others=(), space=VMEM):
    def size(shape, kind):
        total = jnp.dtype(kind).itemsize
        for extent in shape:
            total *= extent
        return total

    held = sum(size(o.shape, o.dtype) for o in outs) + sum(size(a.shape, a.dtype) for a in arrays)
    held += sum(size(shape, kind) for shape, kind in scratch)
    return pl.pallas_call(
        kernel,
        out_shape=outs,
        in_specs=[SMEM] * len(scalars) + [VMEM] * (len(arrays) - far) + [HBM] * far,
        out_specs=[space] * len(outs),
        scratch_shapes=[*[pltpu.VMEM(shape, kind) for shape, kind in scratch], *others],
        compiler_params=pltpu.CompilerParams(vmem_limit_bytes=min(held + (3 << 20), 60 << 20)),
    )(*scalars, *arrays)


def shards(right_sides, inverse, coupling, sweep_order):
    given = right_sides[0, 0]
    inverse = inverse[0, 0]
    order = sweep_order[0, 0]
    count, nodes, width = given.shape
    face = coupling.shape[4]
    coupling = coupling[0, 0].reshape(count, 3 * face, nodes)
    groups = lax.axis_size("span")
    share = width // groups
    half = groups // 2
    place = lax.axis_index("span").astype(jnp.int32).reshape(1)
    line = lax.axis_index("stream").astype(jnp.int32).reshape(1)
    masks = bits_of(lax.axis_size("stream"))
    tiles = count + count // 2
    shape = jax.ShapeDtypeStruct
    far = [pltpu.with_memory_space_constraint(a, pltpu.HBM) for a in (order, inverse, coupling, given)]
    maps, *near = call(
        first_kernel,
        [
            shape((3 * 3 * face, 2 * face), BF16),
            shape((count, 4 * face, nodes), BF16),
            shape((count - 2,) + coupling.shape[1:], BF16),
            shape(given.shape, BF16),
        ],
        [(inverse.shape, BF16), (coupling.shape, BF16)],
        [],
        far,
        4,
        (
            pltpu.SMEM(order.shape, order.dtype),
            pltpu.SemaphoreType.DMA,
            pltpu.SemaphoreType.DMA((2, count)),
            pltpu.SemaphoreType.DMA((count,)),
        ),
    )
    all_maps = gather_list(maps, "span")
    outs = call(
        rest_kernel,
        [shape(maps.shape, BF16)] * (count // 2 - 1) + [shape((tiles, share, 2 * face), BF16)] * groups,
        [((tiles, width, 2 * face), F32)],
        [place],
        near,
    )
    gains = outs[count // 2 - 1 :]
    for maps in outs[: count // 2 - 1]:
        all_maps += gather_list(maps, "span")
    gains = exchange(gains, "span")
    sizes = dict(groups=groups, count=count, face=face)
    wide = half * face
    response, offset, weights, gains = call(
        functools.partial(respond_kernel, **sizes),
        [
            shape((SWEEPS, wide, wide), BF16),
            shape((SWEEPS, 2 * share, wide), BF16),
            shape((groups, count, 3 * face, 4 * face), BF16),
            shape((groups, count, share, 4 * face), BF16),
        ],
        [
            ((groups + 1, count, share + wide, 2 * face), BF16),
            ((groups, count, share + wide, 2 * face), BF16),
            ((half, share + wide, 2 * face), BF16),
        ],
        [place],
        [*all_maps, *gains],
    )
    levels = []
    for mask in masks[:-2]:
        got_offset = swap(offset, "stream", mask)
        other = swap(response, "span", 1)
        got = swap(response, "stream", mask)
        got_other = swap(got, "span", 1)
        levels += [got, got_other, got_offset]
        arrays = [response, other, got, got_other]
        same = shape(offset.shape, BF16)
        if mask == masks[-3]:
            (opened,) = call(opening_kernel, [same], [], [], [response, other, got_offset, offset])
            near = swap(opened, "stream", masks[-2])
            across = swap(opened, "stream", masks[-2] | mask)
            joining = arrays + [offset, got_offset, near, across]
        else:
            (offset,) = call(
                functools.partial(pair_offset_kernel, mask=mask), [same], [], [line], arrays + [offset, got_offset]
            )
        (response,) = call(
            functools.partial(pair_map_kernel, mask=mask), [shape(response.shape, BF16)], [], [line], arrays
        )
    ahead_even = swap(response, "stream", masks[-2])
    (joined,) = call(functools.partial(join_kernel, mask=masks[-3]), [same], [], [line], joining)
    second = lax.ppermute(joined, "stream", crossing(masks, 1, 2))
    third = lax.ppermute(joined, "stream", crossing(masks, 1, 3))
    ahead_odd = swap(ahead_even, "span", 1)
    wanted = call(
        functools.partial(resolve_kernel, masks=masks, **sizes),
        [shape((tiles, share, 2 * face), BF16)] * groups,
        [
            ((groups + 1, count, share, 2 * face), BF16),
            ((groups, count, share, 2 * face), BF16),
            ((SWEEPS, groups, share, 2 * face), BF16),
        ],
        [place, line],
        [weights, gains, near, across, second, third, ahead_even, ahead_odd, *levels],
    )
    wanted = exchange(wanted, "span")
    (placed,) = call(
        final_kernel,
        [shape((count, nodes, width), BF16)],
        [((count, nodes, width), BF16), ((tiles, width, 2 * face), BF16 if share % 16 == 0 else F32)],
        [place, order],
        [inverse, coupling, given, *wanted],
        0,
        (pltpu.SemaphoreType.DMA((count,)),),
        HBM,
    )
    return placed[None, None]


def solution(mesh):
    in_specs = (
        P("stream", "span", None, None, None),
        P("stream", "span", None, None, None),
        P("stream", "span", None, None, None, None),
        P("stream", "span", None),
    )
    out_specs = P("stream", "span", None, None, None)
    return jax.shard_map(shards, mesh=mesh, in_specs=in_specs, out_specs=out_specs, check_vma=False)
```

```python
import functools

import jax
import jax.numpy as jnp
from jax import lax
from jax.experimental import pallas as pl
from jax.experimental.pallas import tpu as pltpu
from jax.sharding import PartitionSpec as P

NP = 8
SWEEPS = 6
VMEM = pl.BlockSpec(memory_space=pltpu.VMEM)
SMEM = pl.BlockSpec(memory_space=pltpu.SMEM)
HBM = pl.BlockSpec(memory_space=pltpu.HBM)
F32 = jnp.float32
BF16 = jnp.bfloat16


def bits_of(count):
    return [1 << i for i in range(count.bit_length() - 1)]


def reversed_bits(value, count):
    bits = bits_of(count)
    total = 0
    for low, high in zip(bits, bits[::-1]):
        total = total + jnp.where((value & low) != 0, high, 0)
    return total


def reversed_static(value, count):
    bits = bits_of(count)
    return sum(high for low, high in zip(bits, bits[::-1]) if value & low)


def swap(value, axis, mask):
    count = lax.axis_size(axis)
    return lax.ppermute(value, axis, [(i, i ^ mask) for i in range(count)])


def crossing(masks, first, second):
    pairs = []
    for i in range(2 * masks[-1]):
        quarter = i // masks[-2]
        inner = quarter in (first, second)
        pairs.append((i, i ^ ((first ^ second) * masks[-2] if inner else 1)))
    return pairs


def dot(left, right):
    return jnp.dot(left, right, preferred_element_type=F32)


def dot_nt(left, right):
    return lax.dot_general(left, right, (((1,), (1,)), ((), ())), preferred_element_type=F32)


def by_half(low, high):
    lane = lax.broadcasted_iota(jnp.int32, low.shape, low.ndim - 1)
    return jnp.where(lane < low.shape[-1] // 2, low, high)


def turned(value):
    return pltpu.roll(value.astype(F32), value.shape[-1] // 2, 1).astype(value.dtype)


def face_rows_of(inverse, slot, face):
    nodes = inverse.shape[1]
    part = nodes // NP
    layer = part // NP
    lower = []
    upper = []
    for a in range(NP):
        head = inverse[slot, a * part : a * part + 2 * layer, :].astype(F32)
        tail = inverse[slot, (a + 1) * part - 2 * layer : (a + 1) * part, :].astype(F32)
        lower.append(head[:layer])
        upper.append(tail[layer:])
    faces = jnp.concatenate(lower + upper, axis=0).astype(BF16)
    outflow = inverse[slot, nodes - face :, :]
    return jnp.concatenate([faces, outflow, outflow], axis=0)


def pair_maps(maps, coupling, slots, rows, face):
    outs = []
    for i, slot in enumerate(slots):
        full = dot_nt(coupling[slot], rows[i])
        full = jnp.concatenate([full[2 * face :], full[face : 2 * face], full[:face]], axis=0).astype(BF16)
        maps[i * 3 * face : (i + 1) * 3 * face, :] = full[:, : 2 * face]
        outs.append(full[:, 2 * face :])
    maps[2 * 3 * face :, :] = by_half(outs[0], outs[1])


def first_kernel(order_far, inverse_far, coupling_far, given_far, *refs):
    maps, rows, coupling_near, given_near = refs[:4]
    inverse, coupling, order, order_done, done, near_done = refs[4:]
    count = given_near.shape[0]
    face = coupling.shape[1] // 3
    first = pltpu.make_async_copy(order_far, order, order_done)
    first.start()
    copies = []
    for kind, (far, near) in enumerate(((inverse_far, inverse), (coupling_far, coupling))):
        for slot in range(count):
            copies.append(pltpu.make_async_copy(far.at[slot], near.at[slot], done.at[kind, slot]))
    for copy in copies:
        copy.start()
    first.wait()
    slots = [order[p] for p in range(count)]
    later = [
        pltpu.make_async_copy(given_far.at[slots[p]], given_near.at[p], near_done.at[p]) for p in range(count)
    ]
    for copy in later:
        copy.start()

    def arrived(p):
        for kind, (far, near) in enumerate(((inverse_far, inverse), (coupling_far, coupling))):
            pltpu.make_async_copy(far.at[slots[p]], near.at[slots[p]], done.at[kind, slots[p]]).wait()

    values = []
    for p in range(2):
        arrived(p)
        values.append(face_rows_of(inverse, slots[p], face))
    pair_maps(maps, coupling, slots[:2], values, face)
    for p in range(2, count):
        arrived(p)
        values.append(face_rows_of(inverse, slots[p], face))
        coupling_near[p - 2] = coupling[slots[p]]
    for p in range(count):
        rows[p] = values[p]
    for copy in later:
        copy.wait()


def rest_kernel(place, rows, coupling, given, *refs):
    count, _, width = given.shape
    maps = refs[: count // 2 - 1]
    gains = refs[count // 2 - 1 : -1]
    gathered = refs[-1]
    face = coupling.shape[1] // 3
    groups = len(gains)
    share = width // groups
    rows = [rows[p] for p in range(count)]
    for j, target in enumerate(maps):
        pair_maps(target, coupling, (2 * j, 2 * j + 1), rows[2 * j + 2 : 2 * j + 4], face)
    every = [dot(rows[p], given[p]).T for p in range(count)]
    tiles = [gain[:, : 2 * face] for gain in every]
    for p in range(0, count, 2):
        tiles.append(by_half(every[p][:, 2 * face :], every[p + 1][:, 2 * face :]))
    for m, tile in enumerate(tiles):
        gathered[m] = tile
    for rel in range(groups):
        at = pl.multiple_of((place[0] ^ rel) * share, share)
        for m in range(len(tiles)):
            gains[rel][m] = gathered[m, pl.ds(at, share), :].astype(BF16)


def unpack_maps(map_refs, weights, face):
    for j, refs in enumerate(map_refs):
        for pos, ref in enumerate(refs):
            outs = ref[2 * 3 * face :, :]
            other = turned(outs)
            for i in range(2):
                sides = ref[i * 3 * face : (i + 1) * 3 * face, :]
                full = jnp.concatenate([sides, by_half(outs, other) if i == 0 else by_half(other, outs)], axis=1)
                weights[pos, 2 * j + i] = full


def unpack_gains(gain_refs, gains, count):
    for rel, ref in enumerate(gain_refs):
        for p in range(count):
            outs = ref[count + p // 2]
            other = turned(outs)
            outs = by_half(outs, other) if p % 2 == 0 else by_half(other, outs)
            gains[reversed_static(rel, len(gain_refs)), p] = jnp.concatenate([ref[p], outs], axis=1)


def neighbours(me, pos, groups):
    own = me ^ reversed_bits(pos, groups)
    below = jnp.where(own > 0, reversed_bits(((own - 1) & (groups - 1)) ^ me, groups), groups)
    above = jnp.where(own < groups - 1, reversed_bits(((own + 1) & (groups - 1)) ^ me, groups), groups)
    return below, above


def read_lags(me, states, lags, groups, count):
    def read(pos):
        below, above = neighbours(me, pos, groups)
        for p in range(count):
            lags[pos, p] = by_half(states[above, p], states[below, p])

    over(groups, read)


def over(count, body, limit=4):
    if count <= limit:
        for i in range(count):
            body(i)
    else:

        def step(i, carry):
            body(i)
            return carry

        lax.fori_loop(0, count, step, 0)


def split_trace(out):
    high = out.astype(BF16)
    return by_half(high, (out - high.astype(F32)).astype(BF16)), high


def run_chains(chosen, entries, lags, weights, gains, states, count, face, first):
    share = gains.shape[2]
    outs = [[] for _ in chosen]
    for p in range(count):
        for i, pos in enumerate(chosen):
            rows = entries[i].shape[0]
            if p == 0 and not first:
                result = dot(lags[pos, p, :rows], weights[pos, p, : 2 * face])
            else:
                left = entries[i]
                own = weights[pos, p, 2 * face :]
                right = jnp.concatenate([own, own], axis=0)
                if not first:
                    left = jnp.concatenate([lags[pos, p, :rows], left], axis=1)
                    right = jnp.concatenate([weights[pos, p, : 2 * face], right], axis=0)
                result = dot(left, right)
            head = result[:share] + gains[pos, p].astype(F32)
            result = head if rows == share else jnp.concatenate([head, result[share:]], axis=0)
            states[pos, p, :rows] = result[:, : 2 * face].astype(BF16)
            outs[i].append(result[:, 2 * face :])
        if p < count - 1:
            entries = [split_trace(o[p])[0] for o in outs]
    return outs


def respond_kernel(place, *refs, groups, count, face):
    pairs = count // 2
    map_refs = [refs[j * groups : (j + 1) * groups] for j in range(pairs)]
    gain_refs = refs[pairs * groups : (pairs + 1) * groups]
    response, offset, weights, gains, states, lags, unit = refs[(pairs + 1) * groups :]
    me = place[0]
    half = groups // 2
    share = gains.shape[2]
    unpack_maps(map_refs, weights, face)
    unpack_gains(gain_refs, gains, count)
    states[groups] = jnp.zeros_like(states[groups])
    row = lax.broadcasted_iota(jnp.int32, unit.shape[1:], 0) - share
    lane = lax.broadcasted_iota(jnp.int32, unit.shape[1:], 1)
    for pos in range(half):
        hit = jnp.logical_and(lane < face, row == lane + pos * face)
        unit[pos] = jnp.where(hit, 1.0, 0.0).astype(BF16)

    def sweep(k, parity, first=False):
        if not first:
            read_lags(me, states, lags, groups, count)

        def block(t):
            live = [2 * t + half * parity, 2 * t + 1 + half * parity]
            bare = [2 * t + half * (1 - parity), 2 * t + 1 + half * (1 - parity)]
            entries = [unit[pos] if first else jnp.zeros_like(unit[pos]) for pos in live]
            entries += [jnp.zeros((share, 2 * face), BF16)] * 2
            chains = run_chains(live + bare, entries, lags, weights, gains, states, count, face, first)
            ends = [outs[-1] for outs in chains]
            at = pl.ds(pl.multiple_of(t * 2 * face, 2 * face), 2 * face)
            full = by_half(ends[0], ends[1])
            response[k, :, at] = full[share:].astype(BF16)
            for target, tile in ((parity, full[:share]), (1 - parity, by_half(ends[2], ends[3]))):
                offset[k, target * share : (target + 1) * share, at] = tile.astype(BF16)

        over(groups // 4, block, 1)

    def both(i, carry):
        sweep(2 * i, 0)
        sweep(2 * i + 1, 1)
        return carry

    sweep(0, 0, True)
    sweep(1, 1)
    lax.fori_loop(1, SWEEPS // 2, both, 0)


def pick(flag, first, second):
    return jnp.where(flag != 0, first, second)


def pair_offset_kernel(line, own, other, got, got_other, own_offset, got_offset, offset, *, mask):
    down = (line[0] // mask) % 2
    share = own_offset.shape[1] // 2
    maps = [
        (pick(down, own[k], got[k]), pick(down, other[k], got_other[k])) for k in range(SWEEPS)
    ]
    values = []
    for k in range(SWEEPS):
        both = zip(halves_of(got_offset, k), halves_of(own_offset, k))
        values.append([pick(down, a, b) for a, b in both])
    for k in range(SWEEPS):
        both = zip(halves_of(own_offset, k), halves_of(got_offset, k))
        added = [pick(down, a, b).astype(F32) for a, b in both]
        for target, total in enumerate(moved_by(values, maps, k)):
            offset[k, target * share : (target + 1) * share] = (total + added[target]).astype(BF16)


def pair_map_kernel(line, own, other, got, got_other, response, *, mask):
    down = (line[0] // mask) % 2
    after = [
        (pick(down, own[k], got[k]), pick(down, other[k], got_other[k])) for k in range(SWEEPS)
    ]
    before = [pick(down, got[k], own[k]) for k in range(SWEEPS)]
    for m in range(SWEEPS):
        stack = jnp.concatenate([after[d][(m + d) % 2] for d in range(m + 1)], axis=0)
        left = jnp.concatenate([before[m - d] for d in range(m + 1)], axis=1)
        response[m] = dot(left, stack).astype(BF16)


def halves_of(ref, k):
    share = ref.shape[1] // 2
    return ref[k, :share], ref[k, share:]


def moved_by(values, maps, k):
    pair = []
    for target in (0, 1):
        stack = jnp.concatenate([maps[d][(target + d) % 2] for d in range(k + 1)], axis=0)
        left = jnp.concatenate([values[k - d][(target + d) % 2] for d in range(k + 1)], axis=1)
        pair.append(dot(left, stack))
    return pair


def add_own(values, maps, own):
    moved = []
    for k in range(SWEEPS):
        pair = zip(moved_by(values, maps, k), own[k])
        moved.append([(total + added.astype(F32)).astype(BF16) for total, added in pair])
    return moved


def put_halves(ref, values):
    share = ref.shape[1] // 2
    for k in range(SWEEPS):
        for target in (0, 1):
            ref[k, target * share : (target + 1) * share] = values[k][target]


def opening_kernel(even, odd, entry, own, opened):
    maps = [(even[k], odd[k]) for k in range(SWEEPS)]
    values = [halves_of(entry, k) for k in range(SWEEPS)]
    put_halves(opened, add_own(values, maps, [halves_of(own, k) for k in range(SWEEPS)]))


def join_kernel(line, own, other, got, got_other, own_offset, got_offset, near, across, joined, *, mask):
    down = (line[0] // mask) % 2
    values = [
        [pick(down, a, b) for a, b in zip(halves_of(near, k), halves_of(across, k))] for k in range(SWEEPS)
    ]
    for turn in (down, 1 - down):
        maps = [(pick(turn, got[k], own[k]), pick(turn, got_other[k], other[k])) for k in range(SWEEPS)]
        added = [
            [pick(turn, a, b) for a, b in zip(halves_of(got_offset, k), halves_of(own_offset, k))]
            for k in range(SWEEPS)
        ]
        values = add_own(values, maps, added)
    put_halves(joined, values)


def resolve_kernel(place, line, *refs, groups, count, face, masks):
    weights, gains, near, across, second, third, ahead_even, ahead_odd = refs[:8]
    levels = len(masks) - 2
    lower = refs[8 : 8 + 3 * levels]
    wanted = refs[8 + 3 * levels : 8 + 3 * levels + groups]
    states, lags, inflows = refs[8 + 3 * levels + groups :]
    me = place[0]
    half = groups // 2
    states[groups] = jnp.zeros_like(states[groups])
    flags = [(line[0] // mask) % 2 for mask in masks]
    maps = [(ahead_even[k], ahead_odd[k]) for k in range(SWEEPS)]
    given = [halves_of(third, k) for k in range(SWEEPS)]
    values = []
    for k in range(SWEEPS):
        pair = []
        for target, total in enumerate(moved_by(given, maps, k)):
            own = pick(flags[-3], halves_of(near, k)[target], halves_of(across, k)[target])
            last = (total + own.astype(F32)).astype(BF16)
            upper = pick(flags[-2], last, halves_of(second, k)[target])
            pair.append(pick(flags[-1], upper, pick(flags[-2], own, jnp.zeros_like(own))))
        values.append(pair)
    for level in range(levels - 1, -1, -1):
        even, odd, offset = lower[3 * level : 3 * level + 3]
        maps = [(even[k], odd[k]) for k in range(SWEEPS)]
        moved = []
        for k in range(SWEEPS):
            pair = []
            for target, total in enumerate(moved_by(values, maps, k)):
                total = total + halves_of(offset, k)[target].astype(F32)
                pair.append(pick(flags[level], total.astype(BF16), values[k][target]))
            moved.append(pair)
        values = moved
    blank = jnp.zeros((values[0][0].shape[0], 2 * face), BF16)
    for k in range(SWEEPS):
        for pos in range(groups):
            tile = (pos % half) // 2
            both = values[k][pos // half][:, tile * 2 * face : (tile + 1) * 2 * face]
            inflows[k, pos] = by_half(both if pos % 2 == 0 else turned(both), blank)

    def chains(k, t, stage):
        chosen = tuple(4 * t + i for i in range(4))
        entries = [inflows[k, pos] for pos in chosen]
        every = [[entry] for entry in entries]
        for p in range(count - (stage == 2)):
            for i, pos in enumerate(chosen):
                left = every[i][p][:, :face]
                right = weights[pos, p, 2 * face :]
                added = gains[pos, p].astype(F32)
                if stage > 0:
                    left = jnp.concatenate([lags[pos, p], left], axis=1)
                    right = weights[pos, p]
                if stage == 2:
                    right = right[:, 2 * face :]
                    added = added[:, 2 * face :]
                result = dot(left, right) + added
                if stage < 2:
                    states[pos, p] = result[:, : 2 * face].astype(BF16)
                    result = result[:, 2 * face :]
                every[i].append(result.astype(BF16))
        return chosen, every

    def blocks(k, stage):
        over(groups // 4, lambda t: chains(k, t, stage), 1)

    blocks(0, 0)

    def sweep(k, carry):
        read_lags(me, states, lags, groups, count)
        blocks(k, 1)
        return carry

    lax.fori_loop(1, SWEEPS - 1, sweep, 0)
    read_lags(me, states, lags, groups, count)
    for t in range(groups // 4):
        chosen, every = chains(SWEEPS - 1, t, 2)
        for i, pos in enumerate(chosen):
            target = wanted[reversed_static(pos, groups)]
            traces = every[i]
            for p in range(count):
                target[p] = lags[pos, p]
            target[count] = by_half(traces[0], traces[count - 1])
            for m in range(1, count // 2):
                target[count + m] = by_half(traces[2 * m - 1], traces[2 * m])


def final_kernel(place, order, inverse, coupling, given, *refs):
    wanted = refs[:-4]
    placed, solved, gathered, done = refs[-4:]
    count, nodes, width = given.shape
    face = coupling.shape[1] // 3
    share = width // len(wanted)
    for rel, ref in enumerate(wanted):
        at = pl.multiple_of((place[0] ^ rel) * share, share)
        for m in range(ref.shape[0]):
            gathered[m, pl.ds(at, share), :] = ref[m].astype(gathered.dtype)
    blank = jnp.zeros((face, nodes), BF16)
    copies = []
    for p in range(count):
        slot = order[p]
        rows = coupling[slot]
        second = p == count - 1 or (p > 0 and p % 2 == 0)
        tile = 0 if p == count - 1 else (p + 1) // 2
        pair = [blank, rows[:face]] if second else [rows[:face], blank]
        sides = jnp.concatenate([rows[2 * face :], rows[face : 2 * face]] + pair, axis=0)
        traces = jnp.concatenate([gathered[p], gathered[count + tile]], axis=1).astype(BF16)
        source = given[slot].astype(F32) + dot(traces, sides).T
        solved[p] = dot(inverse[slot], source.astype(BF16)).astype(BF16)
        copies.append(pltpu.make_async_copy(solved.at[p], placed.at[slot], done.at[p]))
        copies[p].start()
    for copy in copies:
        copy.wait()


def gather_list(value, axis):
    values = [value]
    for mask in bits_of(lax.axis_size(axis))[::-1]:
        values = values + [swap(v, axis, mask) for v in values]
    return values


def exchange(values, axis):
    return [v if rel == 0 else swap(v, axis, rel) for rel, v in enumerate(values)]


def call(kernel, outs, scratch, scalars, arrays, far=0, others=(), space=VMEM):
    def size(shape, kind):
        total = jnp.dtype(kind).itemsize
        for extent in shape:
            total *= extent
        return total

    held = sum(size(o.shape, o.dtype) for o in outs) + sum(size(a.shape, a.dtype) for a in arrays)
    held += sum(size(shape, kind) for shape, kind in scratch)
    return pl.pallas_call(
        kernel,
        out_shape=outs,
        in_specs=[SMEM] * len(scalars) + [VMEM] * (len(arrays) - far) + [HBM] * far,
        out_specs=[space] * len(outs),
        scratch_shapes=[*[pltpu.VMEM(shape, kind) for shape, kind in scratch], *others],
        compiler_params=pltpu.CompilerParams(vmem_limit_bytes=min(held + (3 << 20), 60 << 20)),
    )(*scalars, *arrays)


def shards(right_sides, inverse, coupling, sweep_order):
    given = right_sides[0, 0]
    inverse = inverse[0, 0]
    order = sweep_order[0, 0]
    count, nodes, width = given.shape
    face = coupling.shape[4]
    coupling = coupling[0, 0].reshape(count, 3 * face, nodes)
    groups = lax.axis_size("span")
    share = width // groups
    half = groups // 2
    place = lax.axis_index("span").astype(jnp.int32).reshape(1)
    line = lax.axis_index("stream").astype(jnp.int32).reshape(1)
    masks = bits_of(lax.axis_size("stream"))
    tiles = count + count // 2
    shape = jax.ShapeDtypeStruct
    far = [pltpu.with_memory_space_constraint(a, pltpu.HBM) for a in (order, inverse, coupling, given)]
    maps, *near = call(
        first_kernel,
        [
            shape((3 * 3 * face, 2 * face), BF16),
            shape((count, 4 * face, nodes), BF16),
            shape((count - 2,) + coupling.shape[1:], BF16),
            shape(given.shape, BF16),
        ],
        [(inverse.shape, BF16), (coupling.shape, BF16)],
        [],
        far,
        4,
        (
            pltpu.SMEM(order.shape, order.dtype),
            pltpu.SemaphoreType.DMA,
            pltpu.SemaphoreType.DMA((2, count)),
            pltpu.SemaphoreType.DMA((count,)),
        ),
    )
    all_maps = gather_list(maps, "span")
    outs = call(
        rest_kernel,
        [shape(maps.shape, BF16)] * (count // 2 - 1) + [shape((tiles, share, 2 * face), BF16)] * groups,
        [((tiles, width, 2 * face), F32)],
        [place],
        near,
    )
    gains = outs[count // 2 - 1 :]
    for maps in outs[: count // 2 - 1]:
        all_maps += gather_list(maps, "span")
    gains = exchange(gains, "span")
    sizes = dict(groups=groups, count=count, face=face)
    wide = half * face
    response, offset, weights, gains = call(
        functools.partial(respond_kernel, **sizes),
        [
            shape((SWEEPS, wide, wide), BF16),
            shape((SWEEPS, 2 * share, wide), BF16),
            shape((groups, count, 3 * face, 4 * face), BF16),
            shape((groups, count, share, 4 * face), BF16),
        ],
        [
            ((groups + 1, count, share + wide, 2 * face), BF16),
            ((groups, count, share + wide, 2 * face), BF16),
            ((half, share + wide, 2 * face), BF16),
        ],
        [place],
        [*all_maps, *gains],
    )
    levels = []
    for mask in masks[:-2]:
        got_offset = swap(offset, "stream", mask)
        other = swap(response, "span", 1)
        got = swap(response, "stream", mask)
        got_other = swap(got, "span", 1)
        levels += [got, got_other, got_offset]
        arrays = [response, other, got, got_other]
        same = shape(offset.shape, BF16)
        if mask == masks[-3]:
            (opened,) = call(opening_kernel, [same], [], [], [response, other, got_offset, offset])
            near = swap(opened, "stream", masks[-2])
            across = swap(opened, "stream", masks[-2] | mask)
            joining = arrays + [offset, got_offset, near, across]
        else:
            (offset,) = call(
                functools.partial(pair_offset_kernel, mask=mask), [same], [], [line], arrays + [offset, got_offset]
            )
        (response,) = call(
            functools.partial(pair_map_kernel, mask=mask), [shape(response.shape, BF16)], [], [line], arrays
        )
    ahead_even = swap(response, "stream", masks[-2])
    (joined,) = call(functools.partial(join_kernel, mask=masks[-3]), [same], [], [line], joining)
    second = lax.ppermute(joined, "stream", crossing(masks, 1, 2))
    third = lax.ppermute(joined, "stream", crossing(masks, 1, 3))
    ahead_odd = swap(ahead_even, "span", 1)
    wanted = call(
        functools.partial(resolve_kernel, masks=masks, **sizes),
        [shape((tiles, share, 2 * face), BF16)] * groups,
        [
            ((groups + 1, count, share, 2 * face), BF16),
            ((groups, count, share, 2 * face), BF16),
            ((SWEEPS, groups, share, 2 * face), BF16),
        ],
        [place, line],
        [weights, gains, near, across, second, third, ahead_even, ahead_odd, *levels],
    )
    wanted = exchange(wanted, "span")
    (placed,) = call(
        final_kernel,
        [shape((count, nodes, width), BF16)],
        [((count, nodes, width), BF16), ((tiles, width, 2 * face), BF16 if share % 16 == 0 else F32)],
        [place, order],
        [inverse, coupling, given, *wanted],
        0,
        (pltpu.SemaphoreType.DMA((count,)),),
        HBM,
    )
    return placed[None, None]


def solution(mesh):
    in_specs = (
        P("stream", "span", None, None, None),
        P("stream", "span", None, None, None),
        P("stream", "span", None, None, None, None),
        P("stream", "span", None),
    )
    out_specs = P("stream", "span", None, None, None)
    return jax.shard_map(shards, mesh=mesh, in_specs=in_specs, out_specs=out_specs, check_vma=False)
```
